256 devices in a mesh: img: 8 (over z_hi, core), band: 8 (over z_lo, x), pw: 4 (over y).
Axes of the slice: x: 4, y: 4, z: 8 (z_hi: 4, z_lo: 2; z = z_hi * 2 + z_lo), core: 2. Of those that a mesh axis runs over, the one named last changes fastest.
Arguments:
- coefficients: bfloat16 [8, 1024, 32, 2048], P('img', None, ('band', 'pw')), may hold values from -6 to 6
- rotation: bfloat16 [8, 1024, 256], P('img'), may hold values from -0.1875 to 0.1875
- positions: int32 [8, 3, 256], P('img'), may hold values from 0 to 63, as said below
- start_pos: int32 [3, 256], replicated, may hold values from 0 to 63, as said below
- end_pos: int32 [3, 256], replicated, may hold values from 0 to 63, as said below
- species: int32 [256], replicated, may hold values from 0 to 3
- depth: float32 [4], replicated, may hold values from 0.5 to 3
Outputs:
- correction: bfloat16 [8, 256, 32, 2048], P('img', None, ('band', 'pw'))
- ritz_values: float32 [8, 256], P('img')
- band_force: float32 [8, 3, 256], P('img')
- along_force: float32 [8], P('img')
The draws below stay inside these ranges and needn't reach their ends.
Inputs may be any that keep to these rules, and one draw needn't show every extreme that they name: `positions`: grid index of each atom's centre along each dimension. `start_pos`: grid index of each atom's centre along each dimension. `end_pos`: grid index of each atom's centre along each dimension.
All inputs are finite; a program needn't handle non-finite values.
Results may differ from the reference program's by a relative error of at most 0.012.
The reference program's roundings to bfloat16 on the way count: a program that leaves them out, or rounds other values in their place, can miss the bound.
Values may be sent and summed in bfloat16 or wider, within the bound.
No kernel may reach another device: no remote copies, remote signals or barrier semaphores. Data moves between devices by JAX's collectives and lax.ppermute only.
A program may use at most 128 MiB of HBM per device.

```python
import math
import jax
import jax.numpy as jnp
from jax import lax

G = 64
W = 32
BANDS = 1024
BLOCK = 256
ATOMS = 256
SPECIES = 4
IMAGES = 8
NPW = 32768


def common_base(key):
    return jax.random.randint(jax.random.fold_in(key, 11), (3, ATOMS), 0, G)


def displaced(key, salt_value, shape_full):
    return jax.random.randint(jax.random.fold_in(key, salt_value), shape_full, -2, 3)


def draw_positions(key, part):
    base_grid = common_base(key)
    return jnp.mod(base_grid[None] + displaced(key, 12, (IMAGES, 3, ATOMS)), G).astype(jnp.int32)


def draw_start_pos(key, part):
    base_grid = common_base(key)
    return jnp.mod(base_grid + displaced(key, 13, (3, ATOMS)), G).astype(jnp.int32)


def draw_end_pos(key, part):
    base_grid = common_base(key)
    return jnp.mod(base_grid + displaced(key, 14, (3, ATOMS)), G).astype(jnp.int32)


def with_ends(values, stream_key, least, high):
    index_at = [jax.random.randint(jax.random.fold_in(stream_key, axis), (), 0, length) for axis, length in enumerate(values.shape)]
    main_axis = values.shape.index(max(values.shape))
    next_to = index_at[:main_axis] + [(index_at[main_axis] + 1) % values.shape[main_axis]] + index_at[main_axis + 1:]
    return values.at[tuple(index_at)].set(least).at[tuple(next_to)].set(high)


def levels(own_key, shape, pieces, smallest, largest):
    level = 1.0
    for axis_at, shards_of in pieces:
        steps = jax.random.uniform(jax.random.fold_in(jax.random.fold_in(own_key, 6), axis_at), (shards_of,), jnp.float32, smallest / len(pieces), largest / len(pieces))
        level = level * jnp.repeat(jnp.exp(steps), shape[axis_at] // shards_of).reshape((-1,) + (1,) * (len(shape) - 1 - axis_at))
    return level


def normal_values(own_key, shape, scale, reach, pieces=(), held_as=jnp.bfloat16):
    drawn = jax.random.normal(own_key, shape, jnp.float32) * scale
    if len(pieces) > 0:
        drawn = levels(own_key, shape, pieces, -0.22, 0.18) * drawn
    return jnp.clip(drawn, min=-reach, max=reach).astype(held_as)


def setup_inputs(seed: int = 0) -> dict:
    splits = jax.random.split(jax.random.key(seed), 8)
    return {
        "coefficients": normal_values(splits[0], (IMAGES, BANDS, W, W * 2 * W), 1.0, 6.0, ((0, 8), (2, 32))),
        "rotation": normal_values(splits[1], (IMAGES, BANDS, BLOCK), BANDS ** -0.5, 0.1875, ((0, 8),)),
        "positions": draw_positions(jax.random.fold_in(splits[7], 71), 0),
        "start_pos": draw_start_pos(jax.random.fold_in(splits[7], 71), 0),
        "end_pos": draw_end_pos(jax.random.fold_in(splits[7], 71), 0),
        "species": with_ends(jax.random.randint(splits[5], (ATOMS,), 0, SPECIES), jax.random.fold_in(splits[5], 1), 0, SPECIES - 1).astype(jnp.int32),
        "depth": jnp.clip(jnp.exp(jax.random.uniform(splits[6], (SPECIES,), jnp.float32, math.log(0.5), math.log(3.0))), 0.5, 3.0),
    }


kinetic_scale = 0.01
sigma_cells = 3.0
spring_constant = 2.0
epsilon = 1e-06
highest = lax.Precision.HIGHEST

def product(pattern, left_op, right_op):
    return jnp.einsum(pattern, left_op.astype(jnp.float32), right_op.astype(jnp.float32), precision=highest)

def phases(box_order, box_size, grid_size):
    wavenum = box_order.astype(jnp.int32) - box_size // 2
    grid_cells = jnp.arange(grid_size, dtype=jnp.int32)
    turn_count = jnp.mod(wavenum[:, None] * grid_cells[None, :], grid_size)
    return turn_count.astype(jnp.float32) * (2.0 * math.pi / grid_size)

def forward_table(box_order, box_size, grid_size):
    angle_tab = phases(box_order, box_size, grid_size)
    cosine = jnp.cos(angle_tab) / math.sqrt(box_size)
    sine_part = jnp.sin(angle_tab) / math.sqrt(box_size)
    dft_table = jnp.stack([jnp.stack([cosine, sine_part], 1), jnp.stack([-sine_part, cosine], 1)], 0)
    return dft_table.astype(jnp.bfloat16)

def inverse_table(box_order, box_size, grid_size):
    angle_tab = phases(box_order, box_size, grid_size).T
    factor = math.sqrt(box_size) / grid_size
    cosine = jnp.cos(angle_tab) * factor
    sine_part = jnp.sin(angle_tab) * factor
    dft_table = jnp.stack([jnp.stack([cosine, -sine_part], 1), jnp.stack([sine_part, cosine], 1)], 0)
    return dft_table.astype(jnp.bfloat16)

def section_zy(coeff_block, table_z, table_y):
    leading = coeff_block.shape[0]
    planes = coeff_block.shape[1]
    split_up = coeff_block.reshape(leading, planes, W, 2, W)
    along_z = product('blyck,ckdn->blydn', split_up, table_z).astype(jnp.bfloat16)
    along_y = product('blycz,cydm->blmdz', along_z, table_y).astype(jnp.bfloat16)
    return along_y.reshape(leading, planes, G * 2 * G)

def section_x(arrived, table_x):
    leading = arrived.shape[0]
    y_rows = arrived.shape[2] // (2 * G)
    split_up = arrived.reshape(leading, W, y_rows, 2, G)
    return product('bxycz,cxdn->bnydz', split_up, table_x)

def section_x_inverse(weighted, table_x):
    leading = weighted.shape[0]
    y_rows = weighted.shape[2]
    along_x = product('bnydz,dncx->bxycz', weighted, table_x).astype(jnp.bfloat16)
    return along_x.reshape(leading, W, y_rows * 2 * G)

def section_zy_inverse(returned, table_y, table_z):
    leading = returned.shape[0]
    planes = returned.shape[1]
    split_up = returned.reshape(leading, planes, G, 2, G)
    along_y = product('blmdz,dmcy->blycz', split_up, table_y).astype(jnp.bfloat16)
    along_z = product('blydn,dnck->blyck', along_y, table_z)
    return along_z.reshape(leading, planes, W * 2 * W)

def wrap_offset(values):
    return jnp.mod(values + G // 2, G) - G // 2

def gaussians(coords, grid_cells):
    offset = wrap_offset(grid_cells[None, :] - coords[:, None]).astype(jnp.float32)
    return (jnp.exp(-offset * offset / (2.0 * sigma_cells * sigma_cells)), offset)

def atom_tables(own_pos, y_cells):
    grid_cells = jnp.arange(G, dtype=jnp.int32)
    gauss_x, offset_x = gaussians(own_pos[0], grid_cells)
    gauss_y, offset_y = gaussians(own_pos[1], y_cells)
    gauss_z, offset_z = gaussians(own_pos[2], grid_cells)
    return (gauss_x, offset_x, gauss_y, offset_y, gauss_z, offset_z)

def local_potential(tables, strength):
    gauss_x, offset_x, gauss_y, offset_y, gauss_z, offset_z = tables
    atom_count = gauss_x.shape[0]
    joined = (gauss_y[:, :, None] * gauss_z[:, None, :]).reshape(atom_count, -1)
    potential = jnp.dot((strength[:, None] * gauss_x).T, joined, precision=highest)
    return (potential, joined)

def atom_forces(density, tables, joined, strength):
    gauss_x, offset_x, gauss_y, offset_y, gauss_z, offset_z = tables
    atom_count = gauss_x.shape[0]
    with_y = ((gauss_y * offset_y)[:, :, None] * gauss_z[:, None, :]).reshape(atom_count, -1)
    with_z = (gauss_y[:, :, None] * (gauss_z * offset_z)[:, None, :]).reshape(atom_count, -1)
    stacked = jnp.concatenate([joined, with_y, with_z], 0)
    moments = jnp.dot(density, stacked.T, precision=highest)
    prefactor = -strength / (sigma_cells * sigma_cells)
    force_x = prefactor * lax.optimization_barrier(jnp.sum(gauss_x * offset_x * moments[:, :atom_count].T, 1))
    force_y = prefactor * lax.optimization_barrier(jnp.sum(gauss_x * moments[:, atom_count:2 * atom_count].T, 1))
    force_z = prefactor * lax.optimization_barrier(jnp.sum(gauss_x * moments[:, 2 * atom_count:].T, 1))
    return jnp.stack([force_x, force_y, force_z], 0)

def kinetic_table(x_cells):
    entries = jnp.arange(W * 2 * W, dtype=jnp.int32)
    wave_y = entries // (2 * W) - W // 2
    wave_z = jnp.mod(entries, W) - W // 2
    wave_x = x_cells - W // 2
    squared = wave_x[:, None] * wave_x[:, None] + (wave_y * wave_y + wave_z * wave_z)[None, :]
    return kinetic_scale * 0.5 * squared.astype(jnp.float32)

def rotate_quarter(values):
    leading = values.shape[0]
    middle = values.shape[1]
    split_up = values.reshape(leading, middle, W, 2, W)
    turned = jnp.stack([-split_up[:, :, :, 1, :], split_up[:, :, :, 0, :]], 3)
    return turned.reshape(values.shape)

def chain_forces(force, own_pos, before, after):
    ahead_step = wrap_offset(after - own_pos).astype(jnp.float32)
    behind = wrap_offset(own_pos - before).astype(jnp.float32)
    tangent_raw = ahead_step + behind
    entries = 3 * own_pos.shape[1]
    tangent = tangent_raw * lax.rsqrt(jnp.mean(tangent_raw * tangent_raw) + epsilon) / math.sqrt(entries)
    length_ahead = jnp.sqrt(entries * (jnp.mean(ahead_step * ahead_step) + epsilon))
    length_behind = jnp.sqrt(entries * (jnp.mean(behind * behind) + epsilon))
    along_path = jnp.sum(force * tangent)
    band_push = force - along_path * tangent + spring_constant * (length_ahead - length_behind) * tangent
    return (band_push, along_path)

def one_image(coeffs, rotation_one, own_pos, before, after, strength):
    flat_all = coeffs.reshape(BANDS, -1)
    orbitals = jnp.dot(rotation_one.T, flat_all, preferred_element_type=jnp.float32).astype(jnp.bfloat16)
    orbitals = orbitals.reshape(BLOCK, W, W * 2 * W)
    natural = jnp.arange(W, dtype=jnp.int32)
    table_f = forward_table(natural, W, G)
    table_i = inverse_table(natural, W, G)
    tables = atom_tables(own_pos, jnp.arange(G, dtype=jnp.int32))
    potential, joined = local_potential(tables, strength)
    grid_potential = potential.reshape(G, G, G)
    group_size = math.gcd(BLOCK, 16)
    blocks = orbitals.reshape(BLOCK // group_size, group_size, W, W * 2 * W)

    def apply_block(density, band_block):
        spread = section_zy(band_block, table_f, table_f)
        in_space = section_x(spread, table_f)
        density = density + lax.optimization_barrier(jnp.sum(in_space * in_space, axis=(0, 3)))
        weighted = (in_space * grid_potential[:, :, None, :]).astype(jnp.bfloat16)
        returned = section_x_inverse(weighted, table_i)
        return (density, section_zy_inverse(returned, table_i, table_i))
    density, applied = lax.scan(apply_block, jnp.zeros((G, G, G), jnp.float32), blocks)
    applied = applied.reshape(BLOCK, W, W * 2 * W)
    kinetic = kinetic_table(natural)
    orbitals_wide = orbitals.astype(jnp.float32)
    hamiltonian = kinetic[None] * orbitals_wide + applied
    numerator = lax.optimization_barrier(jnp.sum(orbitals_wide * hamiltonian, axis=(1, 2)))
    denominator = lax.optimization_barrier(jnp.sum(orbitals_wide * orbitals_wide, axis=(1, 2)))
    ritz_values = numerator / NPW / (denominator / NPW + epsilon)
    residual = hamiltonian - ritz_values[:, None, None] * orbitals_wide
    search = (residual / (1.0 + kinetic)[None]).astype(jnp.bfloat16)
    search_pair = jnp.concatenate([search.reshape(BLOCK, -1), (-rotate_quarter(search)).reshape(BLOCK, -1)], 0)
    intersections = jnp.dot(flat_all, search_pair.T, preferred_element_type=jnp.float32) / NPW
    intersections = intersections.astype(jnp.bfloat16)
    projected = jnp.dot(intersections.T, flat_all, preferred_element_type=jnp.float32)
    projection = projected[:BLOCK].reshape(BLOCK, W, -1) + rotate_quarter(projected[BLOCK:].reshape(BLOCK, W, -1))
    correction = (search.astype(jnp.float32) - projection).astype(jnp.bfloat16)
    atom_force = atom_forces((density / BLOCK).reshape(G, G * G), tables, joined, strength)
    band_push, along_path = chain_forces(atom_force, own_pos, before, after)
    return (correction, ritz_values, band_push, along_path)

def reference(coefficients, rotation, positions, start_pos, end_pos, species, depth):
    kind_ids = jnp.arange(SPECIES, dtype=jnp.int32)
    strength = lax.optimization_barrier(jnp.sum(jnp.where(species[:, None] == kind_ids[None, :], depth[None, :], 0.0), 1))
    results = []
    for image_idx in range(IMAGES):
        before = start_pos if image_idx == 0 else positions[image_idx - 1]
        after = end_pos if image_idx == IMAGES - 1 else positions[image_idx + 1]
        results.append(one_image(coefficients[image_idx], rotation[image_idx], positions[image_idx], before, after, strength))
    return (jnp.stack([entry_one[0] for entry_one in results], 0), jnp.stack([entry_one[1] for entry_one in results], 0), jnp.stack([entry_one[2] for entry_one in results], 0), jnp.stack([entry_one[3] for entry_one in results], 0))
```

```python
import math

import jax
import jax.numpy as jnp
import numpy as np
from jax import lax
from jax.experimental import pallas as pl
from jax.experimental.pallas import tpu as pltpu
from jax.sharding import PartitionSpec as P

G = 64
W = 32
BANDS = 1024
BLOCK = 256
SPECIES = 4
NPW = W * W * W
PEERS = 32
OWN = BLOCK // PEERS // 2
HALF = BLOCK // 2
PITCH = 2 * G
ROWS = 136

kinetic_scale = 0.01
sigma_cells = 3.0
spring_constant = 2.0
epsilon = 1e-06

f32 = jnp.float32
bf16 = jnp.bfloat16
GRID_AXES = ("band", "pw")


def host_phases():
    turns = np.mod((np.arange(W) - W // 2)[:, None] * np.arange(G)[None, :], G)
    return turns.astype(np.float32) * np.float32(2.0 * math.pi / G)


def host_tables():
    angle = host_phases()
    cosine, sine = np.cos(angle), np.sin(angle)
    s = np.float32(1.0 / math.sqrt(W))
    fwd = np.stack([np.stack([cosine, sine], 1), np.stack([-sine, cosine], 1)], 0) * s
    t = np.float32(math.sqrt(W) / G)
    c2, s2 = cosine.T * t, sine.T * t
    inv = np.stack([np.stack([c2, -s2], 1), np.stack([s2, c2], 1)], 0)
    left = fwd.transpose(2, 3, 0, 1).reshape(2 * G, 2 * W)
    left_inv = inv.transpose(2, 3, 0, 1).reshape(2 * W, 2 * G)
    eye = np.eye(2, dtype=np.float32)
    z_fwd = np.einsum("cjdn,pq->pcjdqn", fwd, eye).reshape(4 * W, 4 * G)
    z_inv = np.einsum("dncj,pq->dpnqcj", inv, eye).reshape(4 * G, 4 * W)
    return [np.asarray(a, dtype=bf16) for a in (z_fwd, left, left_inv, z_inv)]


def host_pack():
    move = np.zeros((2, 2, 64, 2, 2, 64), np.float32)
    for h in range(2):
        for y in range(2):
            move[h, y, np.arange(64), y, h, np.arange(64)] = 1.0
    return move.reshape(256, 256)


def host_unpack():
    plain = host_pack().T
    e = np.arange(64)
    turn = np.zeros((64, 64), np.float32)
    turn[(e + 32) % 64, e] = np.where(e < 32, 1.0, -1.0)
    whole = np.kron(np.eye(4, dtype=np.float32), turn)
    return np.concatenate([plain, plain @ whole], 1)


def split_two(value):
    high = value.astype(bf16)
    return high, (value - high.astype(f32)).astype(bf16)


def split_three(value):
    high = value.astype(bf16)
    rest = value - high.astype(f32)
    middle = rest.astype(bf16)
    return high, middle, (rest - middle.astype(f32)).astype(bf16)


def dot(a, b):
    return jnp.dot(a, b, preferred_element_type=f32)


def dot_nt(a, b):
    return lax.dot_general(a, b, (((1,), (1,)), ((), ())), preferred_element_type=f32)


def iota(shape, dim):
    return lax.broadcasted_iota(jnp.int32, shape, dim)


def orbitals_kernel(rot_ref, coeff_ref, pack_ref, out_ref, wide_ref):
    step = pl.program_id(0)
    both = lax.dot_general(
        rot_ref[...], coeff_ref[...], (((0,), (0,)), ((), ())), preferred_element_type=f32
    ).astype(bf16)
    lanes = both.shape[1]
    for j in range(lanes // 128):
        at = slice(128 * j, 128 * j + 128)
        pair = jnp.concatenate([both[:HALF, at], both[HALF:, at]], 1)
        moved = dot(pair, pack_ref[...])
        y = step * (lanes // 64) + 2 * j
        wide_ref[pl.ds(y, HALF, stride=W), :] = moved[:, :128]
        wide_ref[pl.ds(y + 1, HALF, stride=W), :] = moved[:, 128:]

    @pl.when(step == pl.num_programs(0) - 1)
    def _():
        out_ref[...] = wide_ref[...].astype(bf16)


def own_orbitals(rotation, coeff):
    lanes = 512
    full = lambda k: (0, 0)
    return pl.pallas_call(
        orbitals_kernel,
        grid=(2048 // lanes,),
        in_specs=[
            pl.BlockSpec((BANDS, BLOCK), full),
            pl.BlockSpec((BANDS, lanes), lambda k: (0, k)),
            pl.BlockSpec((256, 256), full),
        ],
        out_specs=pl.BlockSpec((HALF * W, 128), full),
        out_shape=jax.ShapeDtypeStruct((HALF * W, 128), bf16),
        scratch_shapes=[pltpu.VMEM((HALF * W, 128), f32)],
        compiler_params=pltpu.CompilerParams(vmem_limit_bytes=40 << 20),
        name="orbitals",
    )(rotation, coeff, jnp.asarray(host_pack(), bf16))


def gaussian(position, rows):
    cells = iota((rows, position.shape[1]), 0) & (G - 1)
    offset = (((cells - position + G // 2) & (G - 1)) - G // 2).astype(f32)
    return jnp.exp(-offset * offset / (2.0 * sigma_cells * sigma_cells)), offset


def strengths(species, depth_ref):
    strength = jnp.zeros(species.shape, f32)
    for kind in range(SPECIES):
        strength = jnp.where(species == kind, depth_ref[kind], strength)
    return strength


def potential_kernel(depth_ref, pos_ref, species_ref, out_ref, gy_ref):
    strength = strengths(species_ref[...], depth_ref)
    gauss_x, _ = gaussian(pos_ref[0:1, :], G)
    gauss_x = gauss_x * strength
    gy_ref[...], _ = gaussian(pos_ref[1:2, :], G)
    gauss_z, _ = gaussian(pos_ref[2:3, :], 2 * G)
    z_high, z_low = split_two(gauss_z)
    per = 8

    def some(i, carry):
        for k in range(per):
            m = i * per + k
            value = gauss_x * gy_ref[pl.ds(m, 1), :]
            high, low = split_two(value)
            out_ref[pl.ds(pl.multiple_of(m * G, G), G), :] = (
                dot_nt(high, z_high) + dot_nt(high, z_low) + dot_nt(low, z_high)
            )
        return carry

    lax.fori_loop(0, G // per, some, 0)


def vmem(count):
    return [pl.BlockSpec(memory_space=pltpu.VMEM)] * count


def grid_potential(depth, pos, species):
    return pl.pallas_call(
        potential_kernel,
        in_specs=[pl.BlockSpec(memory_space=pltpu.SMEM)] + vmem(2),
        out_specs=vmem(1)[0],
        out_shape=jax.ShapeDtypeStruct((G * G, 128), f32),
        scratch_shapes=[pltpu.VMEM((G, 256), f32)],
        compiler_params=pltpu.CompilerParams(vmem_limit_bytes=40 << 20),
        name="potential",
    )(depth, pos, species)


def transform_kernel(
    orb_ref, pot_ref, zf_ref, left_ref, left_inv_ref, zi_ref,
    out_ref, ritz_ref, dens_ref,
    mid_ref, ham_ref, num_ref, den_ref,
):
    group = 2
    rows = group * OWN * W

    def forward(i, carry):
        x = i * group
        zin = orb_ref[pl.ds(pl.multiple_of(x * OWN * W, rows), rows), :]
        along_z = dot(zin, zf_ref[...]).astype(bf16)
        parts = []
        for g in range(group * OWN):
            piece = along_z[W * g : W * g + W]
            parts.append(jnp.concatenate([piece[:, :128], piece[:, 128:]], 0))
        along_y = dot(left_ref[...], jnp.concatenate(parts, 1))
        for g in range(group * OWN):
            xx, tt = x + g // OWN, g % OWN
            at = pl.multiple_of((tt * W + xx) * PITCH, 8)
            mid_ref[pl.ds(at, 2 * G), :] = along_y[:, 128 * g : 128 * g + 128]
        return carry

    lax.fori_loop(0, W // group, forward, 0)

    def space(m, carry):
        parts = []
        for tt in range(OWN):
            base = tt * W * PITCH + m
            parts.append(
                jnp.concatenate(
                    [mid_ref[pl.ds(base + c * G, W, stride=PITCH), :] for c in range(2)], 0
                ).astype(bf16)
            )
        in_space = dot(left_ref[...], jnp.concatenate(parts, 1))
        at = pl.multiple_of(m * G, G)
        potential = pot_ref[pl.ds(at, G), :]
        potential = jnp.concatenate([potential, potential], 0)
        density = jnp.zeros((2 * G, 128), f32)
        weighted = []
        for tt in range(OWN):
            one = in_space[:, 128 * tt : 128 * tt + 128]
            density = density + one * one
            weighted.append((one * potential).astype(bf16))
        dens_ref[pl.ds(at, G), :] = (density[:G] + density[G:]) * (1.0 / BLOCK)
        back = dot(left_inv_ref[...], jnp.concatenate(weighted, 1))
        for tt in range(OWN):
            base = tt * W * PITCH + m
            for c in range(2):
                mid_ref[pl.ds(base + c * G, W, stride=PITCH), :] = back[
                    W * c : W * c + W, 128 * tt : 128 * tt + 128
                ]
        return carry

    lax.fori_loop(0, G, space, 0)

    lane = iota((W, 128), 1)
    wave_y = iota((W, 128), 0) - W // 2
    wave_z = (lane & (W - 1)) - W // 2
    plane = wave_y * wave_y + wave_z * wave_z

    def kinetic(x):
        wave_x = x - W // 2
        return (kinetic_scale * 0.5) * (plane + wave_x * wave_x).astype(f32)

    num_ref[...] = jnp.zeros_like(num_ref)
    den_ref[...] = jnp.zeros_like(den_ref)

    def backward(i, carry):
        x = i * group
        parts = []
        for g in range(group * OWN):
            xx, tt = x + g // OWN, g % OWN
            at = pl.multiple_of((tt * W + xx) * PITCH, 8)
            parts.append(mid_ref[pl.ds(at, 2 * G), :].astype(bf16))
        back_y = dot(left_inv_ref[...], jnp.concatenate(parts, 1)).astype(bf16)
        parts = []
        for g in range(group * OWN):
            piece = back_y[:, 128 * g : 128 * g + 128]
            parts.append(jnp.concatenate([piece[:W], piece[W:]], 1))
        local = dot(jnp.concatenate(parts, 0), zi_ref[...])
        for g in range(group * OWN):
            xx, tt = x + g // OWN, g % OWN
            at = pl.multiple_of((xx * OWN + tt) * W, W)
            orbital = orb_ref[pl.ds(at, W), :].astype(f32)
            ham = kinetic(xx) * orbital + local[W * g : W * g + W]
            ham_ref[pl.ds(at, W), :] = ham
            num_ref[pl.ds(tt * W, W), :] += orbital * ham
            den_ref[pl.ds(tt * W, W), :] += orbital * orbital
        return carry

    lax.fori_loop(0, W // group, backward, 0)

    lane_row = iota((1, 128), 1)
    low = lane_row < 64
    ritz_row = jnp.zeros((1, 128), f32)
    ritz = []
    for tt in range(OWN):
        halves = []
        num = jnp.sum(num_ref[pl.ds(tt * W, W), :], 0, keepdims=True)
        den = jnp.sum(den_ref[pl.ds(tt * W, W), :], 0, keepdims=True)
        for p in range(2):
            mine = low if p == 0 else jnp.logical_not(low)
            top = jnp.sum(jnp.where(mine, num, 0.0), 1, keepdims=True)
            bottom = jnp.sum(jnp.where(mine, den, 0.0), 1, keepdims=True)
            value = (top / NPW) / (bottom / NPW + epsilon)
            halves.append(value)
            ritz_row = jnp.where(lane_row == 32 + p * OWN + tt, value, ritz_row)
        ritz.append(jnp.where(low, halves[0], halves[1]))
    ritz_ref[...] = jnp.broadcast_to(ritz_row, (8, 128))

    def finish(x, carry):
        kin = kinetic(x)
        scale = 1.0 / (1.0 + kin)
        for tt in range(OWN):
            at = pl.multiple_of((x * OWN + tt) * W, W)
            orbital = orb_ref[pl.ds(at, W), :].astype(f32)
            residual = ham_ref[pl.ds(at, W), :] - ritz[tt] * orbital
            out_ref[pl.ds(at, W), :] = (residual * scale).astype(bf16)
        return carry

    lax.fori_loop(0, W, finish, 0, unroll=2)


def searched(orbitals, potential):
    z_fwd, left, left_inv, z_inv = host_tables()
    return pl.pallas_call(
        transform_kernel,
        in_specs=vmem(6),
        out_specs=vmem(3),
        out_shape=[
            jax.ShapeDtypeStruct((W * OWN * W, 128), bf16),
            jax.ShapeDtypeStruct((8, 128), f32),
            jax.ShapeDtypeStruct((G * G, 128), f32),
        ],
        scratch_shapes=[
            pltpu.VMEM((OWN * W * PITCH, 128), f32),
            pltpu.VMEM((W * OWN * W, 128), f32),
            pltpu.VMEM((OWN * W, 128), f32),
            pltpu.VMEM((OWN * W, 128), f32),
        ],
        compiler_params=pltpu.CompilerParams(vmem_limit_bytes=48 << 20),
        name="transform",
    )(orbitals, potential, z_fwd, left, left_inv, z_inv)


def force_kernel(
    depth_ref, dens_ref, pos_ref, species_ref, ritz_ref, out_ref, gy_ref, gyo_ref, wide_ref
):
    strength = strengths(species_ref[...], depth_ref)
    gauss_x, offset_x = gaussian(pos_ref[0:1, :], G)
    gauss_y, offset_y = gaussian(pos_ref[1:2, :], G)
    gauss_z, offset_z = gaussian(pos_ref[2:3, :], 2 * G)
    gy_ref[...] = gauss_y
    gyo_ref[...] = gauss_y * offset_y
    high, low = split_two(jnp.concatenate([gauss_z, gauss_z * offset_z], 1))
    both = jnp.concatenate([high, low], 0)
    per = 4

    def some(i, carry):
        sum_x, sum_y, sum_z = carry
        at = pl.multiple_of(i * per * G, per * G)
        d_high, d_low = split_two(dens_ref[pl.ds(at, per * G), :])
        moments = dot(jnp.concatenate([d_high, d_high], 1), both) + dot(d_low, high)
        for k in range(per):
            gy = gy_ref[pl.ds(i * per + k, 1), :]
            gyo = gyo_ref[pl.ds(i * per + k, 1), :]
            plain = moments[G * k : G * k + G, :256]
            sum_x = sum_x + plain * gy
            sum_y = sum_y + plain * gyo
            sum_z = sum_z + moments[G * k : G * k + G, 256:] * gy
        return sum_x, sum_y, sum_z

    zero = jnp.zeros((G, 256), f32)
    sum_x, sum_y, sum_z = lax.fori_loop(0, G // per, some, (zero, zero, zero))
    factor = -strength / (sigma_cells * sigma_cells)
    force = [
        factor * jnp.sum(gauss_x * offset_x * sum_x, 0, keepdims=True),
        factor * jnp.sum(gauss_x * sum_y, 0, keepdims=True),
        factor * jnp.sum(gauss_x * sum_z, 0, keepdims=True),
    ]
    peer, atom = iota((PEERS, 256), 0), iota((PEERS, 256), 1)
    from_atom, lane = iota((256, 128), 0), iota((256, 128), 1)
    parts = [part.astype(f32) for part in split_three(ritz_ref[0:1, :])]
    totals = [jnp.broadcast_to(part, (PEERS, 128)) for part in parts]
    for alpha in range(3):
        own = jnp.where(atom // 8 == peer, force[alpha], 0.0)
        choose = jnp.where((from_atom & 7) + 8 * alpha == lane, 1.0, 0.0).astype(bf16)
        for k, part in enumerate(split_three(own)):
            totals[k] = totals[k] + dot(part, choose)
    wide_ref[...] = jnp.zeros_like(wide_ref)
    for k in range(3):
        wide_ref[pl.ds(k, PEERS, stride=8), :] = totals[k]
    out_ref[...] = wide_ref[...].reshape(PEERS, 8, 128).astype(bf16)


def force_parts(depth, density, pos, species, ritz):
    return pl.pallas_call(
        force_kernel,
        in_specs=[pl.BlockSpec(memory_space=pltpu.SMEM)] + vmem(4),
        out_specs=vmem(1)[0],
        out_shape=jax.ShapeDtypeStruct((PEERS, 8, 128), bf16),
        scratch_shapes=[
            pltpu.VMEM((G, 256), f32),
            pltpu.VMEM((G, 256), f32),
            pltpu.VMEM((PEERS * 8, 128), f32),
        ],
        compiler_params=pltpu.CompilerParams(vmem_limit_bytes=40 << 20),
        name="force",
    )(depth, density, pos, species, ritz)


def intersect_kernel(
    search_ref, unpack_ref, coeff_ref, extra_ref, out_ref, flat_ref, wide_ref, pair_ref
):
    step = pl.program_id(0)

    @pl.when(step == 0)
    def _():
        wide_ref[...] = search_ref[...].astype(f32)
        for j in range(W // 2):
            even = wide_ref[pl.ds(2 * j, HALF, stride=W), :]
            odd = wide_ref[pl.ds(2 * j + 1, HALF, stride=W), :]
            moved = dot(jnp.concatenate([even, odd], 1).astype(bf16), unpack_ref[...]).astype(bf16)
            at = slice(128 * j, 128 * j + 128)
            for q in range(4):
                pair_ref[HALF * q : HALF * q + HALF, at] = moved[:, 128 * q : 128 * q + 128]
        flat_ref[...] = pair_ref[: 2 * HALF, :]
        out_ref[:, 128:, :] = extra_ref[...]

    part = (dot_nt(pair_ref[...], coeff_ref[...]) * (1.0 / NPW)).astype(bf16)
    tiles = coeff_ref.shape[0] // 128
    for j in range(tiles):
        out_ref[:, pl.ds(pl.multiple_of((step * tiles + j) * 16, 16), 16), :] = part[
            :, 128 * j : 128 * j + 128
        ].reshape(PEERS, 16, 128)


def own_intersections(search, coeff, extra):
    some = 256
    full2 = lambda k: (0, 0)
    full3 = lambda k: (0, 0, 0)
    return pl.pallas_call(
        intersect_kernel,
        grid=(BANDS // some,),
        in_specs=[
            pl.BlockSpec((HALF * W, 128), full2),
            pl.BlockSpec((256, 512), full2),
            pl.BlockSpec((some, 2048), lambda k: (k, 0)),
            pl.BlockSpec((PEERS, 8, 128), full3),
        ],
        out_specs=[
            pl.BlockSpec((PEERS, ROWS, 128), full3),
            pl.BlockSpec((BLOCK, 2048), full2),
        ],
        out_shape=[
            jax.ShapeDtypeStruct((PEERS, ROWS, 128), bf16),
            jax.ShapeDtypeStruct((BLOCK, 2048), bf16),
        ],
        scratch_shapes=[
            pltpu.VMEM((HALF * W, 128), f32),
            pltpu.VMEM((2 * BLOCK, 2048), bf16),
        ],
        compiler_params=pltpu.CompilerParams(vmem_limit_bytes=48 << 20),
        name="intersect",
    )(search, jnp.asarray(host_unpack(), bf16), coeff, extra)


def total_kernel(in_ref, out_ref):
    for r in range(8):
        at = slice(16 * r, 16 * r + 16)
        total = in_ref[0, at, :].astype(f32)
        for peer in range(1, PEERS):
            total = total + in_ref[peer, at, :].astype(f32)
        total = total.astype(bf16)
        for peer in range(PEERS):
            out_ref[peer, at, :] = total
    extra = in_ref[0, 128:, :].astype(f32)
    for peer in range(1, PEERS):
        extra = extra + in_ref[peer, 128:, :].astype(f32)
    high, middle, low = split_three(extra[0:1] + extra[1:2] + extra[2:3])
    row = iota((8, 128), 0)
    parts = jnp.where(row == 0, high.astype(f32), 0.0)
    parts = jnp.where(row == 1, middle.astype(f32), parts)
    parts = jnp.where(row == 2, low.astype(f32), parts).astype(bf16)
    for peer in range(PEERS):
        out_ref[peer, 128:, :] = parts


def totals_for_all(arrived):
    return pl.pallas_call(
        total_kernel,
        in_specs=vmem(1),
        out_specs=vmem(1)[0],
        out_shape=jax.ShapeDtypeStruct((PEERS, ROWS, 128), bf16),
        compiler_params=pltpu.CompilerParams(vmem_limit_bytes=40 << 20),
        name="total",
    )(arrived)


def wrap_offset(values):
    return ((values + G // 2) & (G - 1)) - G // 2


def project_kernel(
    image_ref, whole_ref, first_ref, coeff_ref, flat_ref, pos_ref, before_ref, after_ref,
    start_ref, end_ref, out_ref, ritz_ref, push_ref, along_ref, inter_ref,
):
    step = pl.program_id(0)

    @pl.when(step == 0)
    def _():
        for j in range(8):
            inter_ref[:, 128 * j : 128 * j + 128] = whole_ref[:, 16 * j : 16 * j + 16, :].reshape(
                2 * BLOCK, 128
            )

    projected = dot(inter_ref[...], coeff_ref[...])
    lanes = projected.shape[1]
    first = (iota((BLOCK, 128), 1) & 63) < 32
    for j in range(lanes // 128):
        at = slice(128 * j, 128 * j + 128)
        turned = projected[BLOCK:, at]
        turned = jnp.where(first, -pltpu.roll(turned, 96, 1), pltpu.roll(turned, 32, 1))
        out_ref[:, at] = (flat_ref[:, at].astype(f32) - (projected[:BLOCK, at] + turned)).astype(bf16)

    @pl.when(step == pl.num_programs(0) - 1)
    def _():
        lane, column = iota((128, 256), 0), iota((128, 256), 1)
        peer, at = iota((PEERS, 256), 0), iota((PEERS, 256), 1)

        def row_of(ref, base, lane_wanted, peer_wanted):
            choose = jnp.where(lane == lane_wanted, 1.0, 0.0).astype(bf16)
            total = jnp.zeros((1, 256), f32)
            parts = ref[:, base : base + 8, :].astype(f32)
            for k in range(3):
                here = dot(parts[:, k, :].astype(bf16), choose)
                here = jnp.where(peer == peer_wanted, here, 0.0)
                total = total + jnp.sum(here, 0, keepdims=True)
            return total

        ritz_ref[...] = row_of(
            first_ref, 0, 32 + OWN * (column // HALF) + column % OWN, at % HALF // OWN
        )
        pos = pos_ref[...]
        image = image_ref[0]
        before = jnp.where(image == 0, start_ref[...], before_ref[...])
        after = jnp.where(image == image_ref[1] - 1, end_ref[...], after_ref[...])
        ahead = wrap_offset(after - pos).astype(f32)
        behind = wrap_offset(pos - before).astype(f32)
        raw = ahead + behind
        entries = pos.shape[0] * pos.shape[1]

        def mean_square(value):
            return jnp.sum(jnp.sum(value * value, 1, keepdims=True), 0, keepdims=True) / entries

        tangent = raw * lax.rsqrt(mean_square(raw) + epsilon) * (1.0 / math.sqrt(entries))
        length_ahead = jnp.sqrt(entries * (mean_square(ahead) + epsilon))
        length_behind = jnp.sqrt(entries * (mean_square(behind) + epsilon))
        force = jnp.concatenate(
            [row_of(whole_ref, 128, 8 * alpha + (column & 7), at // 8) for alpha in range(3)], 0
        )
        along = jnp.sum(jnp.sum(force * tangent, 1, keepdims=True), 0, keepdims=True)
        push_ref[...] = (
            force - along * tangent + spring_constant * (length_ahead - length_behind) * tangent
        )
        along_ref[...] = along


def corrected(image, whole, arrived, coeff, flat, pos, before, after, start_pos, end_pos):
    lanes = 256
    full2 = lambda k: (0, 0)
    full3 = lambda k: (0, 0, 0)
    small = pl.BlockSpec((3, 256), full2)
    return pl.pallas_call(
        project_kernel,
        grid=(2048 // lanes,),
        in_specs=[
            pl.BlockSpec(memory_space=pltpu.SMEM),
            pl.BlockSpec((PEERS, ROWS, 128), full3),
            pl.BlockSpec((PEERS, 8, 128), lambda k: (0, 16, 0)),
            pl.BlockSpec((BANDS, lanes), lambda k: (0, k)),
            pl.BlockSpec((BLOCK, lanes), lambda k: (0, k)),
            small, small, small, small, small,
        ],
        out_specs=[
            pl.BlockSpec((BLOCK, lanes), lambda k: (0, k)),
            pl.BlockSpec((1, 256), full2),
            pl.BlockSpec((3, 256), full2),
            pl.BlockSpec((1, 1), full2),
        ],
        out_shape=[
            jax.ShapeDtypeStruct((BLOCK, 2048), bf16),
            jax.ShapeDtypeStruct((1, 256), f32),
            jax.ShapeDtypeStruct((3, 256), f32),
            jax.ShapeDtypeStruct((1, 1), f32),
        ],
        scratch_shapes=[pltpu.VMEM((2 * BLOCK, BANDS), bf16)],
        compiler_params=pltpu.CompilerParams(vmem_limit_bytes=48 << 20),
        name="project",
    )(image, whole, arrived, coeff, flat, pos, before, after, start_pos, end_pos)


def exchanged(array):
    return lax.all_to_all(array, GRID_AXES, split_axis=0, concat_axis=0, tiled=True)


def passed_along(block, axis, distance):
    devices = range(lax.axis_size(axis))
    route = [(i - distance, i) for i in devices if i - distance in devices]
    return lax.ppermute(block, axis, route)


def body(coefficients, rotation, positions, start_pos, end_pos, species, depth):
    coeff = coefficients.reshape(BANDS, 2048)
    pos = positions[0]
    kinds = species.reshape(1, -1)
    orbitals = own_orbitals(rotation[0], coeff)
    vectors = exchanged(orbitals.reshape(PEERS, OWN * W, 128))
    before = passed_along(pos, "img", 1)
    after = passed_along(pos, "img", -1)
    potential = grid_potential(depth, pos, kinds)
    search, ritz, density = searched(vectors.reshape(W * OWN * W, 128), potential)
    own_search = exchanged(search.reshape(PEERS, OWN * W, 128))
    extra = force_parts(depth, density, pos, kinds, ritz)
    parts, flat = own_intersections(own_search.reshape(HALF * W, 128), coeff, extra)
    arrived = exchanged(parts)
    whole = exchanged(totals_for_all(arrived))
    image = jnp.stack([lax.axis_index("img"), lax.axis_size("img")]).astype(jnp.int32)
    correction, ritz_values, push, along = corrected(
        image, whole, arrived, coeff, flat, pos, before, after, start_pos, end_pos
    )
    return (correction.reshape(1, BLOCK, 1, 2048), ritz_values, push[None], along.reshape(1))


def solution(mesh):
    in_specs = (
        P("img", None, GRID_AXES, None),
        P("img", None, None),
        P("img", None, None),
        P(),
        P(),
        P(),
        P(),
    )
    out_specs = (
        P("img", None, GRID_AXES, None),
        P("img", None),
        P("img", None, None),
        P("img"),
    )
    return jax.shard_map(body, mesh=mesh, in_specs=in_specs, out_specs=out_specs, check_vma=False)
```

```python
import math

import jax
import jax.numpy as jnp
import numpy as np
from jax import lax
from jax.experimental import pallas as pl
from jax.experimental.pallas import tpu as pltpu
from jax.sharding import PartitionSpec as P

G = 64
W = 32
BANDS = 1024
BLOCK = 256
SPECIES = 4
NPW = W * W * W
PEERS = 32
OWN = BLOCK // PEERS // 2
HALF = BLOCK // 2
PITCH = 2 * G + 1
GROUP = 32
MB = 16
SU = 1
ROWS = 136

kinetic_scale = 0.01
sigma_cells = 3.0
spring_constant = 2.0
epsilon = 1e-06

f32 = jnp.float32
bf16 = jnp.bfloat16
GRID_AXES = ("band", "pw")


def host_phases():
    turns = np.mod((np.arange(W) - W // 2)[:, None] * np.arange(G)[None, :], G)
    return turns.astype(np.float32) * np.float32(2.0 * math.pi / G)


def host_tables():
    angle = host_phases()
    cosine, sine = np.cos(angle), np.sin(angle)
    s = np.float32(1.0 / math.sqrt(W))
    fwd = np.stack([np.stack([cosine, sine], 1), np.stack([-sine, cosine], 1)], 0) * s
    t = np.float32(math.sqrt(W) / G)
    c2, s2 = cosine.T * t, sine.T * t
    inv = np.stack([np.stack([c2, -s2], 1), np.stack([s2, c2], 1)], 0)
    left = fwd.transpose(2, 3, 0, 1).reshape(2 * G, 2 * W)
    left_inv = inv.transpose(2, 3, 0, 1).reshape(2 * W, 2 * G)
    eye = np.eye(2, dtype=np.float32)
    z_fwd = np.einsum("cjdn,pq->pcjdqn", fwd, eye).reshape(4 * W, 4 * G)
    z_inv = np.einsum("dncj,pq->dpnqcj", inv, eye).reshape(4 * G, 4 * W)
    return [np.asarray(a, dtype=bf16) for a in (z_fwd, left, left_inv, z_inv)]


def host_pack():
    move = np.zeros((2, 2, 64, 2, 2, 64), np.float32)
    for h in range(2):
        for y in range(2):
            move[h, y, np.arange(64), y, h, np.arange(64)] = 1.0
    return move.reshape(256, 256)


def host_unpack():
    plain = host_pack().T
    e = np.arange(64)
    turn = np.zeros((64, 64), np.float32)
    turn[(e + 32) % 64, e] = np.where(e < 32, 1.0, -1.0)
    whole = np.kron(np.eye(4, dtype=np.float32), turn)
    return np.concatenate([plain, plain @ whole], 1)


def split_two(value):
    high = value.astype(bf16)
    return high, (value - high.astype(f32)).astype(bf16)


def split_three(value):
    high = value.astype(bf16)
    rest = value - high.astype(f32)
    middle = rest.astype(bf16)
    return high, middle, (rest - middle.astype(f32)).astype(bf16)


def dot(a, b):
    return jnp.dot(a, b, preferred_element_type=f32)


def dot_nt(a, b):
    return lax.dot_general(a, b, (((1,), (1,)), ((), ())), preferred_element_type=f32)


def iota(shape, dim):
    return lax.broadcasted_iota(jnp.int32, shape, dim)


def orbitals_kernel(rot_ref, coeff_ref, pack_ref, out_ref, wide_ref):
    step = pl.program_id(0)
    both = lax.dot_general(
        rot_ref[...], coeff_ref[...], (((0,), (0,)), ((), ())), preferred_element_type=f32
    ).astype(bf16)
    lanes = both.shape[1]
    for j in range(lanes // 128):
        at = slice(128 * j, 128 * j + 128)
        pair = jnp.concatenate([both[:HALF, at], both[HALF:, at]], 1)
        moved = dot(pair, pack_ref[...])
        y = step * (lanes // 64) + 2 * j
        wide_ref[pl.ds(y, HALF, stride=W), :] = moved[:, :128]
        wide_ref[pl.ds(y + 1, HALF, stride=W), :] = moved[:, 128:]

    @pl.when(step == pl.num_programs(0) - 1)
    def _():
        out_ref[...] = wide_ref[...].astype(bf16)


def own_orbitals(rotation, coeff):
    lanes = 512
    full = lambda k: (0, 0)
    return pl.pallas_call(
        orbitals_kernel,
        grid=(2048 // lanes,),
        in_specs=[
            pl.BlockSpec((BANDS, BLOCK), full),
            pl.BlockSpec((BANDS, lanes), lambda k: (0, k)),
            pl.BlockSpec((256, 256), full),
        ],
        out_specs=pl.BlockSpec((HALF * W, 128), full),
        out_shape=jax.ShapeDtypeStruct((HALF * W, 128), bf16),
        scratch_shapes=[pltpu.VMEM((HALF * W, 128), f32)],
        compiler_params=pltpu.CompilerParams(vmem_limit_bytes=40 << 20),
        name="orbitals",
    )(rotation, coeff, jnp.asarray(host_pack(), bf16))


def gaussian(position, rows):
    cells = iota((rows, position.shape[1]), 0) & (G - 1)
    offset = (((cells - position + G // 2) & (G - 1)) - G // 2).astype(f32)
    return jnp.exp(-offset * offset / (2.0 * sigma_cells * sigma_cells)), offset


def strengths(species, depth_ref):
    strength = jnp.zeros(species.shape, f32)
    for kind in range(SPECIES):
        strength = jnp.where(species == kind, depth_ref[kind], strength)
    return strength


def potential_kernel(depth_ref, pos_ref, species_ref, out_ref, gy_ref):
    strength = strengths(species_ref[...], depth_ref)
    gauss_x, _ = gaussian(pos_ref[0:1, :], G)
    gauss_x = gauss_x * strength
    gy_ref[...], _ = gaussian(pos_ref[1:2, :], G)
    gauss_z, _ = gaussian(pos_ref[2:3, :], 2 * G)
    z_high, z_low = split_two(gauss_z)
    per = 8

    def some(i, carry):
        for k in range(per):
            m = i * per + k
            value = gauss_x * gy_ref[pl.ds(m, 1), :]
            high, low = split_two(value)
            out_ref[pl.ds(pl.multiple_of(m * G, G), G), :] = (
                dot_nt(high, z_high) + dot_nt(high, z_low) + dot_nt(low, z_high)
            )
        return carry

    lax.fori_loop(0, G // per, some, 0)


def vmem(count):
    return [pl.BlockSpec(memory_space=pltpu.VMEM)] * count


def grid_potential(depth, pos, species):
    return pl.pallas_call(
        potential_kernel,
        in_specs=[pl.BlockSpec(memory_space=pltpu.SMEM)] + vmem(2),
        out_specs=vmem(1)[0],
        out_shape=jax.ShapeDtypeStruct((G * G, 128), f32),
        scratch_shapes=[pltpu.VMEM((G, 256), f32)],
        compiler_params=pltpu.CompilerParams(vmem_limit_bytes=40 << 20),
        name="potential",
    )(depth, pos, species)


def transform_kernel(
    orb_ref, pot_ref, zf_ref, left_ref, left_inv_ref, zi_ref,
    out_ref, ritz_ref, dens_ref,
    mid_ref, ret_ref, ham_ref, num_ref, den_ref,
):
    group = GROUP
    rows = group * OWN * W

    def forward(i, carry):
        x = i * group
        zin = orb_ref[pl.ds(pl.multiple_of(x * OWN * W, rows), rows), :]
        along_z = dot(zin, zf_ref[...]).astype(bf16)
        parts = []
        for g in range(group * OWN):
            piece = along_z[W * g : W * g + W]
            parts.append(jnp.concatenate([piece[:, :128], piece[:, 128:]], 0))
        along_y = dot(left_ref[...], jnp.concatenate(parts, 1))
        for g in range(group * OWN):
            xx, tt = x + g // OWN, g % OWN
            at = (tt * W + xx) * PITCH
            mid_ref[pl.ds(at, 2 * G), :] = along_y[:, 128 * g : 128 * g + 128]
        return carry

    lax.fori_loop(0, W // group, forward, 0)

    def space(i, carry):
        parts = []
        for k in range(MB * OWN):
            base = (k % OWN) * W * PITCH + i * MB + k // OWN
            parts.append(
                jnp.concatenate(
                    [mid_ref[pl.ds(base + c * G, W, stride=PITCH), :] for c in range(2)], 0
                ).astype(bf16)
            )
        in_space = dot(left_ref[...], jnp.concatenate(parts, 1))
        weighted = []
        for mm in range(MB):
            at = pl.multiple_of((i * MB + mm) * G, G)
            potential = pot_ref[pl.ds(at, G), :]
            potential = jnp.concatenate([potential, potential], 0)
            density = jnp.zeros((2 * G, 128), f32)
            for tt in range(OWN):
                k = mm * OWN + tt
                one = in_space[:, 128 * k : 128 * k + 128]
                density = density + one * one
                weighted.append((one * potential).astype(bf16))
            dens_ref[pl.ds(at, G), :] = (density[:G] + density[G:]) * (1.0 / BLOCK)
        back = dot(left_inv_ref[...], jnp.concatenate(weighted, 1))
        for k in range(MB * OWN):
            base = (k % OWN) * W * PITCH + i * MB + k // OWN
            for c in range(2):
                ret_ref[pl.ds(base + c * G, W, stride=PITCH), :] = back[
                    W * c : W * c + W, 128 * k : 128 * k + 128
                ]
        return carry

    lax.fori_loop(0, G // MB, space, 0, unroll=SU)

    lane = iota((W, 128), 1)
    wave_y = iota((W, 128), 0) - W // 2
    wave_z = (lane & (W - 1)) - W // 2
    plane = wave_y * wave_y + wave_z * wave_z

    def kinetic(x):
        wave_x = x - W // 2
        return (kinetic_scale * 0.5) * (plane + wave_x * wave_x).astype(f32)

    num_ref[...] = jnp.zeros_like(num_ref)
    den_ref[...] = jnp.zeros_like(den_ref)

    def backward(i, carry):
        x = i * group
        parts = []
        for g in range(group * OWN):
            xx, tt = x + g // OWN, g % OWN
            at = (tt * W + xx) * PITCH
            parts.append(ret_ref[pl.ds(at, 2 * G), :].astype(bf16))
        back_y = dot(left_inv_ref[...], jnp.concatenate(parts, 1)).astype(bf16)
        parts = []
        for g in range(group * OWN):
            piece = back_y[:, 128 * g : 128 * g + 128]
            parts.append(jnp.concatenate([piece[:W], piece[W:]], 1))
        local = dot(jnp.concatenate(parts, 0), zi_ref[...])
        for g in range(group * OWN):
            xx, tt = x + g // OWN, g % OWN
            at = pl.multiple_of((xx * OWN + tt) * W, W)
            orbital = orb_ref[pl.ds(at, W), :].astype(f32)
            ham = kinetic(xx) * orbital + local[W * g : W * g + W]
            ham_ref[pl.ds(at, W), :] = ham
            num_ref[pl.ds(tt * W, W), :] += orbital * ham
            den_ref[pl.ds(tt * W, W), :] += orbital * orbital
        return carry

    lax.fori_loop(0, W // group, backward, 0)

    lane_row = iota((1, 128), 1)
    low = lane_row < 64
    ritz_row = jnp.zeros((1, 128), f32)
    ritz = []
    for tt in range(OWN):
        halves = []
        num = jnp.sum(num_ref[pl.ds(tt * W, W), :], 0, keepdims=True)
        den = jnp.sum(den_ref[pl.ds(tt * W, W), :], 0, keepdims=True)
        for p in range(2):
            mine = low if p == 0 else jnp.logical_not(low)
            top = jnp.sum(jnp.where(mine, num, 0.0), 1, keepdims=True)
            bottom = jnp.sum(jnp.where(mine, den, 0.0), 1, keepdims=True)
            value = (top / NPW) / (bottom / NPW + epsilon)
            halves.append(value)
            ritz_row = jnp.where(lane_row == 32 + p * OWN + tt, value, ritz_row)
        ritz.append(jnp.where(low, halves[0], halves[1]))
    ritz_ref[...] = jnp.broadcast_to(ritz_row, (8, 128))

    def finish(x, carry):
        kin = kinetic(x)
        scale = 1.0 / (1.0 + kin)
        for tt in range(OWN):
            at = pl.multiple_of((x * OWN + tt) * W, W)
            orbital = orb_ref[pl.ds(at, W), :].astype(f32)
            residual = ham_ref[pl.ds(at, W), :] - ritz[tt] * orbital
            out_ref[pl.ds(at, W), :] = (residual * scale).astype(bf16)
        return carry

    lax.fori_loop(0, W, finish, 0, unroll=2)


def searched(orbitals, potential):
    z_fwd, left, left_inv, z_inv = host_tables()
    return pl.pallas_call(
        transform_kernel,
        in_specs=vmem(6),
        out_specs=vmem(3),
        out_shape=[
            jax.ShapeDtypeStruct((W * OWN * W, 128), bf16),
            jax.ShapeDtypeStruct((8, 128), f32),
            jax.ShapeDtypeStruct((G * G, 128), f32),
        ],
        scratch_shapes=[
            pltpu.VMEM((OWN * W * PITCH, 128), f32),
            pltpu.VMEM((OWN * W * PITCH, 128), f32),
            pltpu.VMEM((W * OWN * W, 128), f32),
            pltpu.VMEM((OWN * W, 128), f32),
            pltpu.VMEM((OWN * W, 128), f32),
        ],
        compiler_params=pltpu.CompilerParams(vmem_limit_bytes=48 << 20),
        name="transform",
    )(orbitals, potential, z_fwd, left, left_inv, z_inv)


def force_kernel(
    depth_ref, dens_ref, pos_ref, species_ref, ritz_ref, out_ref, gy_ref, gyo_ref, wide_ref
):
    strength = strengths(species_ref[...], depth_ref)
    gauss_x, offset_x = gaussian(pos_ref[0:1, :], G)
    gauss_y, offset_y = gaussian(pos_ref[1:2, :], G)
    gauss_z, offset_z = gaussian(pos_ref[2:3, :], 2 * G)
    gy_ref[...] = gauss_y
    gyo_ref[...] = gauss_y * offset_y
    high, low = split_two(jnp.concatenate([gauss_z, gauss_z * offset_z], 1))
    both = jnp.concatenate([high, low], 0)
    per = 4

    def some(i, carry):
        sum_x, sum_y, sum_z = carry
        at = pl.multiple_of(i * per * G, per * G)
        d_high, d_low = split_two(dens_ref[pl.ds(at, per * G), :])
        moments = dot(jnp.concatenate([d_high, d_high], 1), both) + dot(d_low, high)
        for k in range(per):
            gy = gy_ref[pl.ds(i * per + k, 1), :]
            gyo = gyo_ref[pl.ds(i * per + k, 1), :]
            plain = moments[G * k : G * k + G, :256]
            sum_x = sum_x + plain * gy
            sum_y = sum_y + plain * gyo
            sum_z = sum_z + moments[G * k : G * k + G, 256:] * gy
        return sum_x, sum_y, sum_z

    zero = jnp.zeros((G, 256), f32)
    sum_x, sum_y, sum_z = lax.fori_loop(0, G // per, some, (zero, zero, zero))
    factor = -strength / (sigma_cells * sigma_cells)
    force = [
        factor * jnp.sum(gauss_x * offset_x * sum_x, 0, keepdims=True),
        factor * jnp.sum(gauss_x * sum_y, 0, keepdims=True),
        factor * jnp.sum(gauss_x * sum_z, 0, keepdims=True),
    ]
    peer, atom = iota((PEERS, 256), 0), iota((PEERS, 256), 1)
    from_atom, lane = iota((256, 128), 0), iota((256, 128), 1)
    parts = [part.astype(f32) for part in split_three(ritz_ref[0:1, :])]
    totals = [jnp.broadcast_to(part, (PEERS, 128)) for part in parts]
    for alpha in range(3):
        own = jnp.where(atom // 8 == peer, force[alpha], 0.0)
        choose = jnp.where((from_atom & 7) + 8 * alpha == lane, 1.0, 0.0).astype(bf16)
        for k, part in enumerate(split_three(own)):
            totals[k] = totals[k] + dot(part, choose)
    wide_ref[...] = jnp.zeros_like(wide_ref)
    for k in range(3):
        wide_ref[pl.ds(k, PEERS, stride=8), :] = totals[k]
    out_ref[...] = wide_ref[...].reshape(PEERS, 8, 128).astype(bf16)


def force_parts(depth, density, pos, species, ritz):
    return pl.pallas_call(
        force_kernel,
        in_specs=[pl.BlockSpec(memory_space=pltpu.SMEM)] + vmem(4),
        out_specs=vmem(1)[0],
        out_shape=jax.ShapeDtypeStruct((PEERS, 8, 128), bf16),
        scratch_shapes=[
            pltpu.VMEM((G, 256), f32),
            pltpu.VMEM((G, 256), f32),
            pltpu.VMEM((PEERS * 8, 128), f32),
        ],
        compiler_params=pltpu.CompilerParams(vmem_limit_bytes=40 << 20),
        name="force",
    )(depth, density, pos, species, ritz)


def intersect_kernel(
    search_ref, unpack_ref, coeff_ref, extra_ref, out_ref, flat_ref, wide_ref, pair_ref
):
    step = pl.program_id(0)

    @pl.when(step == 0)
    def _():
        wide_ref[...] = search_ref[...].astype(f32)
        for j in range(W // 2):
            even = wide_ref[pl.ds(2 * j, HALF, stride=W), :]
            odd = wide_ref[pl.ds(2 * j + 1, HALF, stride=W), :]
            moved = dot(jnp.concatenate([even, odd], 1).astype(bf16), unpack_ref[...]).astype(bf16)
            at = slice(128 * j, 128 * j + 128)
            for q in range(4):
                pair_ref[HALF * q : HALF * q + HALF, at] = moved[:, 128 * q : 128 * q + 128]
        flat_ref[...] = pair_ref[: 2 * HALF, :]
        out_ref[:, 128:, :] = extra_ref[...]

    part = (dot_nt(pair_ref[...], coeff_ref[...]) * (1.0 / NPW)).astype(bf16)
    tiles = coeff_ref.shape[0] // 128
    for j in range(tiles):
        out_ref[:, pl.ds(pl.multiple_of((step * tiles + j) * 16, 16), 16), :] = part[
            :, 128 * j : 128 * j + 128
        ].reshape(PEERS, 16, 128)


def own_intersections(search, coeff, extra):
    some = 256
    full2 = lambda k: (0, 0)
    full3 = lambda k: (0, 0, 0)
    return pl.pallas_call(
        intersect_kernel,
        grid=(BANDS // some,),
        in_specs=[
            pl.BlockSpec((HALF * W, 128), full2),
            pl.BlockSpec((256, 512), full2),
            pl.BlockSpec((some, 2048), lambda k: (k, 0)),
            pl.BlockSpec((PEERS, 8, 128), full3),
        ],
        out_specs=[
            pl.BlockSpec((PEERS, ROWS, 128), full3),
            pl.BlockSpec((BLOCK, 2048), full2),
        ],
        out_shape=[
            jax.ShapeDtypeStruct((PEERS, ROWS, 128), bf16),
            jax.ShapeDtypeStruct((BLOCK, 2048), bf16),
        ],
        scratch_shapes=[
            pltpu.VMEM((HALF * W, 128), f32),
            pltpu.VMEM((2 * BLOCK, 2048), bf16),
        ],
        compiler_params=pltpu.CompilerParams(vmem_limit_bytes=48 << 20),
        name="intersect",
    )(search, jnp.asarray(host_unpack(), bf16), coeff, extra)


def total_kernel(in_ref, out_ref):
    for r in range(8):
        at = slice(16 * r, 16 * r + 16)
        total = in_ref[0, at, :].astype(f32)
        for peer in range(1, PEERS):
            total = total + in_ref[peer, at, :].astype(f32)
        total = total.astype(bf16)
        for peer in range(PEERS):
            out_ref[peer, at, :] = total
    extra = in_ref[0, 128:, :].astype(f32)
    for peer in range(1, PEERS):
        extra = extra + in_ref[peer, 128:, :].astype(f32)
    high, middle, low = split_three(extra[0:1] + extra[1:2] + extra[2:3])
    row = iota((8, 128), 0)
    parts = jnp.where(row == 0, high.astype(f32), 0.0)
    parts = jnp.where(row == 1, middle.astype(f32), parts)
    parts = jnp.where(row == 2, low.astype(f32), parts).astype(bf16)
    for peer in range(PEERS):
        out_ref[peer, 128:, :] = parts


def totals_for_all(arrived):
    return pl.pallas_call(
        total_kernel,
        in_specs=vmem(1),
        out_specs=vmem(1)[0],
        out_shape=jax.ShapeDtypeStruct((PEERS, ROWS, 128), bf16),
        compiler_params=pltpu.CompilerParams(vmem_limit_bytes=40 << 20),
        name="total",
    )(arrived)


def wrap_offset(values):
    return ((values + G // 2) & (G - 1)) - G // 2


def project_kernel(
    image_ref, whole_ref, first_ref, coeff_ref, flat_ref, pos_ref, before_ref, after_ref,
    start_ref, end_ref, out_ref, ritz_ref, push_ref, along_ref, inter_ref,
):
    step = pl.program_id(0)

    @pl.when(step == 0)
    def _():
        for j in range(8):
            inter_ref[:, 128 * j : 128 * j + 128] = whole_ref[:, 16 * j : 16 * j + 16, :].reshape(
                2 * BLOCK, 128
            )

    projected = dot(inter_ref[...], coeff_ref[...])
    lanes = projected.shape[1]
    first = (iota((BLOCK, 128), 1) & 63) < 32
    for j in range(lanes // 128):
        at = slice(128 * j, 128 * j + 128)
        turned = projected[BLOCK:, at]
        turned = jnp.where(first, -pltpu.roll(turned, 96, 1), pltpu.roll(turned, 32, 1))
        out_ref[:, at] = (flat_ref[:, at].astype(f32) - (projected[:BLOCK, at] + turned)).astype(bf16)

    @pl.when(step == pl.num_programs(0) - 1)
    def _():
        lane, column = iota((128, 256), 0), iota((128, 256), 1)
        peer, at = iota((PEERS, 256), 0), iota((PEERS, 256), 1)

        def row_of(ref, base, lane_wanted, peer_wanted):
            choose = jnp.where(lane == lane_wanted, 1.0, 0.0).astype(bf16)
            total = jnp.zeros((1, 256), f32)
            parts = ref[:, base : base + 8, :].astype(f32)
            for k in range(3):
                here = dot(parts[:, k, :].astype(bf16), choose)
                here = jnp.where(peer == peer_wanted, here, 0.0)
                total = total + jnp.sum(here, 0, keepdims=True)
            return total

        ritz_ref[...] = row_of(
            first_ref, 0, 32 + OWN * (column // HALF) + column % OWN, at % HALF // OWN
        )
        pos = pos_ref[...]
        image = image_ref[0]
        before = jnp.where(image == 0, start_ref[...], before_ref[...])
        after = jnp.where(image == image_ref[1] - 1, end_ref[...], after_ref[...])
        ahead = wrap_offset(after - pos).astype(f32)
        behind = wrap_offset(pos - before).astype(f32)
        raw = ahead + behind
        entries = pos.shape[0] * pos.shape[1]

        def mean_square(value):
            return jnp.sum(jnp.sum(value * value, 1, keepdims=True), 0, keepdims=True) / entries

        tangent = raw * lax.rsqrt(mean_square(raw) + epsilon) * (1.0 / math.sqrt(entries))
        length_ahead = jnp.sqrt(entries * (mean_square(ahead) + epsilon))
        length_behind = jnp.sqrt(entries * (mean_square(behind) + epsilon))
        force = jnp.concatenate(
            [row_of(whole_ref, 128, 8 * alpha + (column & 7), at // 8) for alpha in range(3)], 0
        )
        along = jnp.sum(jnp.sum(force * tangent, 1, keepdims=True), 0, keepdims=True)
        push_ref[...] = (
            force - along * tangent + spring_constant * (length_ahead - length_behind) * tangent
        )
        along_ref[...] = along


def corrected(image, whole, arrived, coeff, flat, pos, before, after, start_pos, end_pos):
    lanes = 256
    full2 = lambda k: (0, 0)
    full3 = lambda k: (0, 0, 0)
    small = pl.BlockSpec((3, 256), full2)
    return pl.pallas_call(
        project_kernel,
        grid=(2048 // lanes,),
        in_specs=[
            pl.BlockSpec(memory_space=pltpu.SMEM),
            pl.BlockSpec((PEERS, ROWS, 128), full3),
            pl.BlockSpec((PEERS, 8, 128), lambda k: (0, 16, 0)),
            pl.BlockSpec((BANDS, lanes), lambda k: (0, k)),
            pl.BlockSpec((BLOCK, lanes), lambda k: (0, k)),
            small, small, small, small, small,
        ],
        out_specs=[
            pl.BlockSpec((BLOCK, lanes), lambda k: (0, k)),
            pl.BlockSpec((1, 256), full2),
            pl.BlockSpec((3, 256), full2),
            pl.BlockSpec((1, 1), full2),
        ],
        out_shape=[
            jax.ShapeDtypeStruct((BLOCK, 2048), bf16),
            jax.ShapeDtypeStruct((1, 256), f32),
            jax.ShapeDtypeStruct((3, 256), f32),
            jax.ShapeDtypeStruct((1, 1), f32),
        ],
        scratch_shapes=[pltpu.VMEM((2 * BLOCK, BANDS), bf16)],
        compiler_params=pltpu.CompilerParams(vmem_limit_bytes=48 << 20),
        name="project",
    )(image, whole, arrived, coeff, flat, pos, before, after, start_pos, end_pos)


def exchanged(array):
    return lax.all_to_all(array, GRID_AXES, split_axis=0, concat_axis=0, tiled=True)


def passed_along(block, axis, distance):
    devices = range(lax.axis_size(axis))
    route = [(i - distance, i) for i in devices if i - distance in devices]
    return lax.ppermute(block, axis, route)


def body(coefficients, rotation, positions, start_pos, end_pos, species, depth):
    coeff = coefficients.reshape(BANDS, 2048)
    pos = positions[0]
    kinds = species.reshape(1, -1)
    orbitals = own_orbitals(rotation[0], coeff)
    vectors = exchanged(orbitals.reshape(PEERS, OWN * W, 128))
    before = passed_along(pos, "img", 1)
    after = passed_along(pos, "img", -1)
    potential = grid_potential(depth, pos, kinds)
    search, ritz, density = searched(vectors.reshape(W * OWN * W, 128), potential)
    own_search = exchanged(search.reshape(PEERS, OWN * W, 128))
    extra = force_parts(depth, density, pos, kinds, ritz)
    parts, flat = own_intersections(own_search.reshape(HALF * W, 128), coeff, extra)
    arrived = exchanged(parts)
    whole = exchanged(totals_for_all(arrived))
    image = jnp.stack([lax.axis_index("img"), lax.axis_size("img")]).astype(jnp.int32)
    correction, ritz_values, push, along = corrected(
        image, whole, arrived, coeff, flat, pos, before, after, start_pos, end_pos
    )
    return (correction.reshape(1, BLOCK, 1, 2048), ritz_values, push[None], along.reshape(1))


def solution(mesh):
    in_specs = (
        P("img", None, GRID_AXES, None),
        P("img", None, None),
        P("img", None, None),
        P(),
        P(),
        P(),
        P(),
    )
    out_specs = (
        P("img", None, GRID_AXES, None),
        P("img", None),
        P("img", None, None),
        P("img"),
    )
    return jax.shard_map(body, mesh=mesh, in_specs=in_specs, out_specs=out_specs, check_vma=False)
```

```python
import math

import jax
import jax.numpy as jnp
import numpy as np
from jax import lax
from jax.experimental import pallas as pl
from jax.experimental.pallas import tpu as pltpu
from jax.sharding import PartitionSpec as P

G = 64
W = 32
BANDS = 1024
BLOCK = 256
SPECIES = 4
NPW = W * W * W
PEERS = 32
OWN = BLOCK // PEERS // 2
HALF = BLOCK // 2
PITCH = 2 * G + 1
GROUP = 32
MB = 16
SU = 1
ROWS = 136
CHUNKS = 2
FETCHES = 2
LINE = W + 1

kinetic_scale = 0.01
sigma_cells = 3.0
spring_constant = 2.0
epsilon = 1e-06

f32 = jnp.float32
bf16 = jnp.bfloat16
GRID_AXES = ("band", "pw")


def host_phases():
    turns = np.mod((np.arange(W) - W // 2)[:, None] * np.arange(G)[None, :], G)
    return turns.astype(np.float32) * np.float32(2.0 * math.pi / G)


def host_tables():
    angle = host_phases()
    cosine, sine = np.cos(angle), np.sin(angle)
    s = np.float32(1.0 / math.sqrt(W))
    fwd = np.stack([np.stack([cosine, sine], 1), np.stack([-sine, cosine], 1)], 0) * s
    t = np.float32(math.sqrt(W) / G)
    c2, s2 = cosine.T * t, sine.T * t
    inv = np.stack([np.stack([c2, -s2], 1), np.stack([s2, c2], 1)], 0)
    left = fwd.transpose(2, 3, 0, 1).reshape(2 * G, 2 * W)
    left_inv = inv.transpose(2, 3, 0, 1).reshape(2 * W, 2 * G)
    eye = np.eye(2, dtype=np.float32)
    z_fwd = np.einsum("cjdn,pq->pcjdqn", fwd, eye).reshape(4 * W, 4 * G)
    z_inv = np.einsum("dncj,pq->dpnqcj", inv, eye).reshape(4 * G, 4 * W)
    return [np.asarray(a, dtype=bf16) for a in (z_fwd, left, left_inv, z_inv)]


def split_two(value):
    high = value.astype(bf16)
    return high, (value - high.astype(f32)).astype(bf16)


def split_three(value):
    high = value.astype(bf16)
    rest = value - high.astype(f32)
    middle = rest.astype(bf16)
    return high, middle, (rest - middle.astype(f32)).astype(bf16)


def dot(a, b):
    return jnp.dot(a, b, preferred_element_type=f32)


def dot_nt(a, b):
    return lax.dot_general(a, b, (((1,), (1,)), ((), ())), preferred_element_type=f32)


def iota(shape, dim):
    return lax.broadcasted_iota(jnp.int32, shape, dim)


def orbitals_kernel(
    rot_hbm, coeff_hbm, out_hbm, coeff_ref, rot_ref, turned_ref, wide_ref, out_ref, sems
):
    lanes = 2048 // CHUNKS

    def fetch(k):
        at = pl.ds(k * lanes, lanes)
        return pltpu.make_async_copy(coeff_hbm.at[:, at], coeff_ref.at[:, at], sems.at[k])

    turned = pltpu.make_async_copy(rot_hbm, rot_ref, sems.at[CHUNKS])
    turned.start()
    for k in range(CHUNKS):
        fetch(k).start()
    source, target = iota((256, 256), 0), iota((256, 256), 1)
    same = (source & 63) == (target & 63)
    same &= (source >> 7) == ((target >> 6) & 1)
    same &= ((source >> 6) & 1) == (target >> 7)
    pack = jnp.where(same, 1.0, 0.0).astype(bf16)
    turned.wait()
    turned_ref[...] = rot_ref[...].T
    for k in range(CHUNKS):
        fetch(k).wait()
        both = dot(turned_ref[...], coeff_ref[:, k * lanes : (k + 1) * lanes]).astype(bf16)
        for j in range(lanes // 128):
            at = slice(128 * j, 128 * j + 128)
            pair = jnp.concatenate([both[:HALF, at], both[HALF:, at]], 1)
            moved = dot(pair, pack)
            y = k * (lanes // 64) + 2 * j
            wide_ref[pl.ds(y, HALF, stride=LINE), :] = moved[:, :128]
            wide_ref[pl.ds(y + 1, HALF, stride=LINE), :] = moved[:, 128:]
    parts = 4
    rows = HALF * W // parts

    def send(k):
        at = pl.ds(k * rows, rows)
        return pltpu.make_async_copy(out_ref.at[at], out_hbm.at[at], sems.at[CHUNKS + 1 + k])

    for k in range(parts):
        for t in range(k * HALF // parts, (k + 1) * HALF // parts):
            out_ref[t * W : t * W + W, :] = wide_ref[t * LINE : t * LINE + W, :].astype(bf16)
        send(k).start()
    for k in range(parts):
        send(k).wait()


def own_orbitals(rotation, coeff):
    return pl.pallas_call(
        orbitals_kernel,
        in_specs=hbm(2),
        out_specs=hbm(1)[0],
        out_shape=pltpu.HBM((HALF * W, 128), bf16),
        scratch_shapes=[
            pltpu.VMEM((BANDS, 2048), bf16),
            pltpu.VMEM((BANDS, BLOCK), bf16),
            pltpu.VMEM((BLOCK, BANDS), bf16),
            pltpu.VMEM((HALF * LINE, 128), f32),
            pltpu.VMEM((HALF * W, 128), bf16),
            pltpu.SemaphoreType.DMA((CHUNKS + 5,)),
        ],
        compiler_params=pltpu.CompilerParams(vmem_limit_bytes=20 << 20),
        name="orbitals",
    )(in_hbm(rotation), in_hbm(coeff))


def in_hbm(array):
    return pltpu.with_memory_space_constraint(array, pltpu.HBM)


def hbm(count):
    return [pl.BlockSpec(memory_space=pltpu.HBM)] * count


def vmem(count):
    return [pl.BlockSpec(memory_space=pltpu.VMEM)] * count


def gaussian(position, rows):
    cells = iota((rows, position.shape[1]), 0) & (G - 1)
    offset = (((cells - position + G // 2) & (G - 1)) - G // 2).astype(f32)
    return jnp.exp(-offset * offset / (2.0 * sigma_cells * sigma_cells)), offset


def strengths(species, depth_ref):
    strength = jnp.zeros(species.shape, f32)
    for kind in range(SPECIES):
        strength = jnp.where(species == kind, depth_ref[kind], strength)
    return strength


def potential_kernel(depth_ref, pos_ref, species_ref, out_ref, gy_ref):
    strength = strengths(species_ref[...], depth_ref)
    gauss_x, _ = gaussian(pos_ref[0:1, :], G)
    gauss_x = gauss_x * strength
    gy_ref[...], _ = gaussian(pos_ref[1:2, :], G)
    gauss_z, _ = gaussian(pos_ref[2:3, :], 2 * G)
    z_high, z_low = split_two(gauss_z)
    per = 8

    def some(i, carry):
        for k in range(per):
            m = i * per + k
            value = gauss_x * gy_ref[pl.ds(m, 1), :]
            high, low = split_two(value)
            out_ref[pl.ds(pl.multiple_of(m * G, G), G), :] = (
                dot_nt(high, z_high) + dot_nt(high, z_low) + dot_nt(low, z_high)
            )
        return carry

    lax.fori_loop(0, G // per, some, 0)


def grid_potential(depth, pos, species):
    return pl.pallas_call(
        potential_kernel,
        in_specs=[pl.BlockSpec(memory_space=pltpu.SMEM)] + vmem(2),
        out_specs=vmem(1)[0],
        out_shape=jax.ShapeDtypeStruct((G * G, 128), f32),
        scratch_shapes=[pltpu.VMEM((G, 256), f32)],
        compiler_params=pltpu.CompilerParams(vmem_limit_bytes=10 << 20),
        name="potential",
    )(depth, pos, species)


def transform_kernel(
    orb_ref, pot_ref, zf_ref, left_ref, left_inv_ref, zi_ref,
    out_hbm, dens_hbm, ritz_ref,
    mid_ref, ham_ref, num_ref, den_ref, dens_ref, out_ref, sems,
):
    group = GROUP
    rows = group * OWN * W

    def forward(i, carry):
        x = i * group
        zin = orb_ref[pl.ds(pl.multiple_of(x * OWN * W, rows), rows), :]
        along_z = dot(zin, zf_ref[...]).astype(bf16)
        parts = []
        for g in range(group * OWN):
            piece = along_z[W * g : W * g + W]
            parts.append(jnp.concatenate([piece[:, :128], piece[:, 128:]], 0))
        along_y = dot(left_ref[...], jnp.concatenate(parts, 1))
        for g in range(group * OWN):
            xx, tt = x + g // OWN, g % OWN
            at = (tt * W + xx) * PITCH
            mid_ref[pl.ds(at, 2 * G), :] = along_y[:, 128 * g : 128 * g + 128]
        return carry

    lax.fori_loop(0, W // group, forward, 0)

    def space(i, carry):
        parts = []
        for k in range(MB * OWN):
            base = (k % OWN) * W * PITCH + i * MB + k // OWN
            parts.append(
                jnp.concatenate(
                    [mid_ref[pl.ds(base + c * G, W, stride=PITCH), :] for c in range(2)], 0
                ).astype(bf16)
            )
        in_space = dot(left_ref[...], jnp.concatenate(parts, 1))
        weighted = []
        for mm in range(MB):
            at = pl.multiple_of((i * MB + mm) * G, G)
            potential = pot_ref[pl.ds(at, G), :]
            potential = jnp.concatenate([potential, potential], 0)
            density = jnp.zeros((2 * G, 128), f32)
            for tt in range(OWN):
                k = mm * OWN + tt
                one = in_space[:, 128 * k : 128 * k + 128]
                density = density + one * one
                weighted.append((one * potential).astype(bf16))
            dens_ref[pl.ds(at, G), :] = (density[:G] + density[G:]) * (1.0 / BLOCK)
        back = dot(left_inv_ref[...], jnp.concatenate(weighted, 1))
        for k in range(MB * OWN):
            base = (k % OWN) * W * PITCH + i * MB + k // OWN
            for c in range(2):
                mid_ref[pl.ds(base + c * G, W, stride=PITCH), :] = back[
                    W * c : W * c + W, 128 * k : 128 * k + 128
                ]
        return carry

    lax.fori_loop(0, G // MB, space, 0, unroll=SU)
    keep = pltpu.make_async_copy(dens_ref, dens_hbm, sems.at[4])
    keep.start()

    lane = iota((W, 128), 1)
    wave_y = iota((W, 128), 0) - W // 2
    wave_z = (lane & (W - 1)) - W // 2
    plane = wave_y * wave_y + wave_z * wave_z

    def kinetic(x):
        wave_x = x - W // 2
        return (kinetic_scale * 0.5) * (plane + wave_x * wave_x).astype(f32)

    num_ref[...] = jnp.zeros_like(num_ref)
    den_ref[...] = jnp.zeros_like(den_ref)

    def backward(i, carry):
        x = i * group
        parts = []
        for g in range(group * OWN):
            xx, tt = x + g // OWN, g % OWN
            at = (tt * W + xx) * PITCH
            parts.append(mid_ref[pl.ds(at, 2 * G), :].astype(bf16))
        back_y = dot(left_inv_ref[...], jnp.concatenate(parts, 1)).astype(bf16)
        parts = []
        for g in range(group * OWN):
            piece = back_y[:, 128 * g : 128 * g + 128]
            parts.append(jnp.concatenate([piece[:W], piece[W:]], 1))
        local = dot(jnp.concatenate(parts, 0), zi_ref[...])
        for g in range(group * OWN):
            xx, tt = x + g // OWN, g % OWN
            at = pl.multiple_of((xx * OWN + tt) * W, W)
            orbital = orb_ref[pl.ds(at, W), :].astype(f32)
            ham = kinetic(xx) * orbital + local[W * g : W * g + W]
            ham_ref[pl.ds(at, W), :] = ham
            num_ref[pl.ds(tt * W, W), :] += orbital * ham
            den_ref[pl.ds(tt * W, W), :] += orbital * orbital
        return carry

    lax.fori_loop(0, W // group, backward, 0)

    lane_row = iota((1, 128), 1)
    low = lane_row < 64
    ritz_row = jnp.zeros((1, 128), f32)
    ritz = []
    for tt in range(OWN):
        halves = []
        num = jnp.sum(num_ref[pl.ds(tt * W, W), :], 0, keepdims=True)
        den = jnp.sum(den_ref[pl.ds(tt * W, W), :], 0, keepdims=True)
        for p in range(2):
            mine = low if p == 0 else jnp.logical_not(low)
            top = jnp.sum(jnp.where(mine, num, 0.0), 1, keepdims=True)
            bottom = jnp.sum(jnp.where(mine, den, 0.0), 1, keepdims=True)
            value = (top / NPW) / (bottom / NPW + epsilon)
            halves.append(value)
            ritz_row = jnp.where(lane_row == 32 + p * OWN + tt, value, ritz_row)
        ritz.append(jnp.where(low, halves[0], halves[1]))
    ritz_ref[...] = jnp.broadcast_to(ritz_row, (8, 128))

    parts = 4
    rows = W * OWN * W // parts

    def send(k):
        at = pl.ds(k * rows, rows)
        return pltpu.make_async_copy(out_ref.at[at], out_hbm.at[at], sems.at[k])

    for x in range(W):
        kin = kinetic(x)
        scale = 1.0 / (1.0 + kin)
        for tt in range(OWN):
            at = pl.ds((x * OWN + tt) * W, W)
            orbital = orb_ref[at, :].astype(f32)
            residual = ham_ref[at, :] - ritz[tt] * orbital
            out_ref[at, :] = (residual * scale).astype(bf16)
        if (x + 1) % (W // parts) == 0:
            send(x // (W // parts)).start()
    for k in range(parts):
        send(k).wait()
    keep.wait()


def searched(orbitals, potential):
    z_fwd, left, left_inv, z_inv = host_tables()
    return pl.pallas_call(
        transform_kernel,
        in_specs=vmem(6),
        out_specs=hbm(2) + vmem(1),
        out_shape=[
            pltpu.HBM((W * OWN * W, 128), bf16),
            pltpu.HBM((G * G, 128), f32),
            jax.ShapeDtypeStruct((8, 128), f32),
        ],
        scratch_shapes=[
            pltpu.VMEM((OWN * W * PITCH, 128), f32),
            pltpu.VMEM((W * OWN * W, 128), f32),
            pltpu.VMEM((OWN * W, 128), f32),
            pltpu.VMEM((OWN * W, 128), f32),
            pltpu.VMEM((G * G, 128), f32),
            pltpu.VMEM((W * OWN * W, 128), bf16),
            pltpu.SemaphoreType.DMA((5,)),
        ],
        compiler_params=pltpu.CompilerParams(vmem_limit_bytes=30 << 20),
        name="transform",
    )(orbitals, potential, z_fwd, left, left_inv, z_inv)


def force_kernel(
    depth_ref, dens_ref, pos_ref, species_ref, ritz_ref, out_ref, gy_ref, gyo_ref, wide_ref
):
    strength = strengths(species_ref[...], depth_ref)
    gauss_x, offset_x = gaussian(pos_ref[0:1, :], G)
    gauss_y, offset_y = gaussian(pos_ref[1:2, :], G)
    gauss_z, offset_z = gaussian(pos_ref[2:3, :], 2 * G)
    gy_ref[...] = gauss_y
    gyo_ref[...] = gauss_y * offset_y
    high, low = split_two(jnp.concatenate([gauss_z, gauss_z * offset_z], 1))
    both = jnp.concatenate([high, low], 0)
    per = 4

    def some(i, carry):
        sum_x, sum_y, sum_z = carry
        at = pl.multiple_of(i * per * G, per * G)
        d_high, d_low = split_two(dens_ref[pl.ds(at, per * G), :])
        moments = dot(jnp.concatenate([d_high, d_high], 1), both) + dot(d_low, high)
        for k in range(per):
            gy = gy_ref[pl.ds(i * per + k, 1), :]
            gyo = gyo_ref[pl.ds(i * per + k, 1), :]
            plain = moments[G * k : G * k + G, :256]
            sum_x = sum_x + plain * gy
            sum_y = sum_y + plain * gyo
            sum_z = sum_z + moments[G * k : G * k + G, 256:] * gy
        return sum_x, sum_y, sum_z

    zero = jnp.zeros((G, 256), f32)
    sum_x, sum_y, sum_z = lax.fori_loop(0, G // per, some, (zero, zero, zero))
    factor = -strength / (sigma_cells * sigma_cells)
    force = [
        factor * jnp.sum(gauss_x * offset_x * sum_x, 0, keepdims=True),
        factor * jnp.sum(gauss_x * sum_y, 0, keepdims=True),
        factor * jnp.sum(gauss_x * sum_z, 0, keepdims=True),
    ]
    peer, atom = iota((PEERS, 256), 0), iota((PEERS, 256), 1)
    from_atom, lane = iota((256, 128), 0), iota((256, 128), 1)
    parts = [part.astype(f32) for part in split_three(ritz_ref[0:1, :])]
    totals = [jnp.broadcast_to(part, (PEERS, 128)) for part in parts]
    for alpha in range(3):
        own = jnp.where(atom // 8 == peer, force[alpha], 0.0)
        choose = jnp.where((from_atom & 7) + 8 * alpha == lane, 1.0, 0.0).astype(bf16)
        for k, part in enumerate(split_three(own)):
            totals[k] = totals[k] + dot(part, choose)
    wide_ref[...] = jnp.zeros_like(wide_ref)
    for k in range(3):
        wide_ref[pl.ds(k, PEERS, stride=8), :] = totals[k]
    out_ref[...] = wide_ref[...].reshape(PEERS, 8, 128).astype(bf16)


def force_parts(depth, density, pos, species, ritz):
    return pl.pallas_call(
        force_kernel,
        in_specs=[pl.BlockSpec(memory_space=pltpu.SMEM)] + vmem(4),
        out_specs=vmem(1)[0],
        out_shape=jax.ShapeDtypeStruct((PEERS, 8, 128), bf16),
        scratch_shapes=[
            pltpu.VMEM((G, 256), f32),
            pltpu.VMEM((G, 256), f32),
            pltpu.VMEM((PEERS * 8, 128), f32),
        ],
        compiler_params=pltpu.CompilerParams(vmem_limit_bytes=10 << 20),
        name="force",
    )(depth, density, pos, species, ritz)


def intersect_kernel(
    search_ref, extra_ref, coeff_hbm, out_ref, flat_ref,
    coeff_ref, wide_ref, pair_ref, sems,
):
    bands = BANDS // FETCHES

    def fetch(k):
        at = pl.ds(k * bands, bands)
        return pltpu.make_async_copy(coeff_hbm.at[at], coeff_ref.at[at], sems.at[k])

    for k in range(FETCHES):
        fetch(k).start()
    source, target = iota((256, 512), 0), iota((256, 512), 1)
    part, element = target >> 7, target & 63
    turned = part >> 1
    same = (source & 63) == (element ^ (turned * 32))
    same &= (source >> 7) == ((target >> 6) & 1)
    same &= ((source >> 6) & 1) == (part & 1)
    sign = jnp.where((turned == 1) & (element >= 32), -1.0, 1.0)
    unpack = jnp.where(same, sign, 0.0).astype(bf16)
    for t in range(HALF):
        wide_ref[t * LINE : t * LINE + W, :] = search_ref[t * W : t * W + W, :].astype(f32)
    out_ref[:, 128:, :] = extra_ref[...]
    for j in range(W // 2):
        even = wide_ref[pl.ds(2 * j, HALF, stride=LINE), :]
        odd = wide_ref[pl.ds(2 * j + 1, HALF, stride=LINE), :]
        moved = dot(jnp.concatenate([even, odd], 1).astype(bf16), unpack).astype(bf16)
        at = slice(128 * j, 128 * j + 128)
        for q in range(4):
            piece = moved[:, 128 * q : 128 * q + 128]
            pair_ref[HALF * q : HALF * q + HALF, at] = piece
            if q < 2:
                flat_ref[HALF * q : HALF * q + HALF, at] = piece
    for k in range(FETCHES):
        fetch(k).wait()
        part = dot_nt(pair_ref[...], coeff_ref[bands * k : bands * k + bands, :])
        part = (part * (1.0 / NPW)).astype(bf16)
        for j in range(bands // 128):
            at = 16 * (k * bands // 128 + j)
            out_ref[:, at : at + 16, :] = part[:, 128 * j : 128 * j + 128].reshape(PEERS, 16, 128)


def own_intersections(search, coeff, extra):
    return pl.pallas_call(
        intersect_kernel,
        in_specs=vmem(2) + hbm(1),
        out_specs=vmem(2),
        out_shape=[
            jax.ShapeDtypeStruct((PEERS, ROWS, 128), bf16),
            jax.ShapeDtypeStruct((BLOCK, 2048), bf16),
        ],
        scratch_shapes=[
            pltpu.VMEM((BANDS, 2048), bf16),
            pltpu.VMEM((HALF * LINE, 128), f32),
            pltpu.VMEM((2 * BLOCK, 2048), bf16),
            pltpu.SemaphoreType.DMA((FETCHES,)),
        ],
        compiler_params=pltpu.CompilerParams(vmem_limit_bytes=20 << 20),
        name="intersect",
    )(search, extra, in_hbm(coeff))


def total_kernel(in_ref, out_ref):
    for r in range(8):
        at = slice(16 * r, 16 * r + 16)
        total = in_ref[0, at, :].astype(f32)
        for peer in range(1, PEERS):
            total = total + in_ref[peer, at, :].astype(f32)
        total = total.astype(bf16)
        for peer in range(PEERS):
            out_ref[peer, at, :] = total
    extra = in_ref[0, 128:, :].astype(f32)
    for peer in range(1, PEERS):
        extra = extra + in_ref[peer, 128:, :].astype(f32)
    high, middle, low = split_three(extra[0:1] + extra[1:2] + extra[2:3])
    row = iota((8, 128), 0)
    parts = jnp.where(row == 0, high.astype(f32), 0.0)
    parts = jnp.where(row == 1, middle.astype(f32), parts)
    parts = jnp.where(row == 2, low.astype(f32), parts).astype(bf16)
    for peer in range(PEERS):
        out_ref[peer, 128:, :] = parts


def totals_for_all(arrived):
    return pl.pallas_call(
        total_kernel,
        in_specs=vmem(1),
        out_specs=vmem(1)[0],
        out_shape=jax.ShapeDtypeStruct((PEERS, ROWS, 128), bf16),
        compiler_params=pltpu.CompilerParams(vmem_limit_bytes=6 << 20),
        name="total",
    )(arrived)


def wrap_offset(values):
    return ((values + G // 2) & (G - 1)) - G // 2


def row_of(ref, base, lane_wanted, peer_wanted):
    lane = iota((128, 256), 0)
    choose = jnp.where(lane == lane_wanted, 1.0, 0.0).astype(bf16)
    parts = ref[:, base : base + 8, :].astype(f32).reshape(PEERS * 8, 128).astype(bf16)
    here = jnp.where((iota((PEERS * 8, 256), 0) >> 3) == peer_wanted, dot(parts, choose), 0.0)
    return jnp.sum(here, 0, keepdims=True)


def prepare_kernel(
    image_ref, first_ref, pos_ref, before_ref, after_ref, start_ref, end_ref,
    ritz_ref, tangent_ref, spring_ref,
):
    column, at = iota((128, 256), 1), iota((PEERS * 8, 256), 1)
    ritz_ref[...] = row_of(
        first_ref, 128, 32 + OWN * (column // HALF) + column % OWN, at % HALF // OWN
    )
    pos = pos_ref[...]
    image = image_ref[0]
    before = jnp.where(image == 0, start_ref[...], before_ref[...])
    after = jnp.where(image == image_ref[1] - 1, end_ref[...], after_ref[...])
    ahead = wrap_offset(after - pos).astype(f32)
    behind = wrap_offset(pos - before).astype(f32)
    raw = ahead + behind
    entries = pos.shape[0] * pos.shape[1]

    def mean_square(value):
        return jnp.sum(jnp.sum(value * value, 1, keepdims=True), 0, keepdims=True) / entries

    tangent = raw * lax.rsqrt(mean_square(raw) + epsilon) * (1.0 / math.sqrt(entries))
    length_ahead = jnp.sqrt(entries * (mean_square(ahead) + epsilon))
    length_behind = jnp.sqrt(entries * (mean_square(behind) + epsilon))
    tangent_ref[...] = tangent
    spring_ref[...] = spring_constant * (length_ahead - length_behind) * tangent


def prepared(image, arrived, pos, before, after, start_pos, end_pos):
    return pl.pallas_call(
        prepare_kernel,
        in_specs=[pl.BlockSpec(memory_space=pltpu.SMEM)] + vmem(6),
        out_specs=vmem(3),
        out_shape=[
            jax.ShapeDtypeStruct((1, 256), f32),
            jax.ShapeDtypeStruct((3, 256), f32),
            jax.ShapeDtypeStruct((3, 256), f32),
        ],
        compiler_params=pltpu.CompilerParams(vmem_limit_bytes=6 << 20),
        name="prepare",
    )(image, arrived, pos, before, after, start_pos, end_pos)


def project_kernel(
    whole_ref, flat_ref, tangent_ref, spring_ref, coeff_hbm,
    out_hbm, push_ref, along_ref, coeff_ref, inter_ref, done_ref, sems, fetch_sems,
):
    wide = 2048 // FETCHES

    def fetch(k):
        at = pl.ds(k * wide, wide)
        return pltpu.make_async_copy(coeff_hbm.at[:, at], coeff_ref.at[:, at], fetch_sems.at[k])

    for k in range(FETCHES):
        fetch(k).start()
    lanes = 256
    chunks = 2048 // lanes
    for j in range(8):
        inter_ref[:, 128 * j : 128 * j + 128] = whole_ref[:, 16 * j : 16 * j + 16, :].reshape(
            2 * BLOCK, 128
        )
    first = (iota((BLOCK, 128), 1) & 63) < 32

    def send(k):
        at = pl.ds(k * lanes, lanes)
        return pltpu.make_async_copy(done_ref.at[:, at], out_hbm.at[:, at], sems.at[k])

    column, at = iota((128, 256), 1), iota((PEERS * 8, 256), 1)
    tangent = tangent_ref[...]
    force = jnp.concatenate(
        [row_of(whole_ref, 128, 8 * alpha + (column & 7), at >> 3) for alpha in range(3)], 0
    )
    along = jnp.sum(jnp.sum(force * tangent, 1, keepdims=True), 0, keepdims=True)
    push = force - along * tangent + spring_ref[...]
    for alpha in range(3):
        push_ref[alpha] = push[alpha : alpha + 1]
    along_ref[...] = along
    for k in range(chunks):
        if k * lanes % wide == 0:
            fetch(k * lanes // wide).wait()
        projected = dot(inter_ref[...], coeff_ref[:, k * lanes : (k + 1) * lanes])
        for j in range(lanes // 128):
            here = slice(128 * j, 128 * j + 128)
            at = slice(k * lanes + 128 * j, k * lanes + 128 * j + 128)
            turned = projected[BLOCK:, here]
            turned = jnp.where(first, -pltpu.roll(turned, 96, 1), pltpu.roll(turned, 32, 1))
            done_ref[:, at] = (
                flat_ref[:, at].astype(f32) - (projected[:BLOCK, here] + turned)
            ).astype(bf16)
        send(k).start()

    for k in range(chunks):
        send(k).wait()


def corrected(whole, flat, tangent, spring, coeff):
    return pl.pallas_call(
        project_kernel,
        in_specs=vmem(4) + hbm(1),
        out_specs=hbm(1) + vmem(2),
        out_shape=[
            pltpu.HBM((BLOCK, 2048), bf16),
            jax.ShapeDtypeStruct((3, 1, 256), f32),
            jax.ShapeDtypeStruct((1, 1), f32),
        ],
        scratch_shapes=[
            pltpu.VMEM((BANDS, 2048), bf16),
            pltpu.VMEM((2 * BLOCK, BANDS), bf16),
            pltpu.VMEM((BLOCK, 2048), bf16),
            pltpu.SemaphoreType.DMA((8,)),
            pltpu.SemaphoreType.DMA((FETCHES,)),
        ],
        compiler_params=pltpu.CompilerParams(vmem_limit_bytes=16 << 20),
        name="project",
    )(whole, flat, tangent, spring, in_hbm(coeff))


def exchanged(array):
    return lax.all_to_all(array, GRID_AXES, split_axis=0, concat_axis=0, tiled=True)


def passed_along(block, axis, distance):
    devices = range(lax.axis_size(axis))
    route = [(i - distance, i) for i in devices if i - distance in devices]
    return lax.ppermute(block, axis, route)


def body(coefficients, rotation, positions, start_pos, end_pos, species, depth):
    coeff = coefficients.reshape(BANDS, 2048)
    pos = positions[0]
    kinds = species.reshape(1, -1)
    orbitals = own_orbitals(rotation[0], coeff)
    vectors = exchanged(orbitals.reshape(PEERS, OWN * W, 128))
    potential = grid_potential(depth, pos, kinds)
    search, density, ritz = searched(vectors.reshape(W * OWN * W, 128), potential)
    own_search = exchanged(search.reshape(PEERS, OWN * W, 128))
    extra = force_parts(depth, density, pos, kinds, ritz)
    parts, flat = own_intersections(own_search.reshape(HALF * W, 128), coeff, extra)
    arrived = exchanged(parts)
    later = lax.optimization_barrier((pos, parts))[0]
    before = passed_along(later, "img", 1)
    after = passed_along(later, "img", -1)
    arrived, before, after = lax.optimization_barrier((arrived, before, after))
    mine = totals_for_all(arrived)
    whole = exchanged(mine)
    image = jnp.stack([lax.axis_index("img"), lax.axis_size("img")]).astype(jnp.int32)
    arrived, before, after = lax.optimization_barrier((arrived, before, after, mine))[:3]
    ritz_values, tangent, spring = prepared(
        image, arrived, pos, before, after, start_pos, end_pos
    )
    correction, push, along = corrected(whole, flat, tangent, spring, coeff)
    return (
        correction.reshape(1, BLOCK, 1, 2048),
        ritz_values,
        push.transpose(1, 0, 2),
        along.reshape(1),
    )


def solution(mesh):
    in_specs = (
        P("img", None, GRID_AXES, None),
        P("img", None, None),
        P("img", None, None),
        P(),
        P(),
        P(),
        P(),
    )
    out_specs = (
        P("img", None, GRID_AXES, None),
        P("img", None),
        P("img", None, None),
        P("img"),
    )
    return jax.shard_map(body, mesh=mesh, in_specs=in_specs, out_specs=out_specs, check_vma=False)
```

```python
import math

import jax
import jax.numpy as jnp
import numpy as np
from jax import lax
from jax.experimental import pallas as pl
from jax.experimental.pallas import tpu as pltpu
from jax.sharding import PartitionSpec as P

G = 64
W = 32
BANDS = 1024
BLOCK = 256
SPECIES = 4
NPW = W * W * W
PEERS = 32
OWN = BLOCK // PEERS // 2
HALF = BLOCK // 2
PITCH = 2 * G + 1
GROUP = 32
MB = 16
SU = 1
ROWS = 136
CHUNKS = 2
FETCHES = 2
LINE = W + 1

kinetic_scale = 0.01
sigma_cells = 3.0
spring_constant = 2.0
epsilon = 1e-06

f32 = jnp.float32
bf16 = jnp.bfloat16
GRID_AXES = ("band", "pw")


def host_phases():
    turns = np.mod((np.arange(W) - W // 2)[:, None] * np.arange(G)[None, :], G)
    return turns.astype(np.float32) * np.float32(2.0 * math.pi / G)


def host_tables():
    angle = host_phases()
    cosine, sine = np.cos(angle), np.sin(angle)
    s = np.float32(1.0 / math.sqrt(W))
    fwd = np.stack([np.stack([cosine, sine], 1), np.stack([-sine, cosine], 1)], 0) * s
    t = np.float32(math.sqrt(W) / G)
    c2, s2 = cosine.T * t, sine.T * t
    inv = np.stack([np.stack([c2, -s2], 1), np.stack([s2, c2], 1)], 0)
    left = fwd.transpose(2, 3, 0, 1).reshape(2 * G, 2 * W)
    left_inv = inv.transpose(2, 3, 0, 1).reshape(2 * W, 2 * G)
    eye = np.eye(2, dtype=np.float32)
    z_fwd = np.einsum("cjdn,pq->pcjdqn", fwd, eye).reshape(4 * W, 4 * G)
    z_inv = np.einsum("dncj,pq->dpnqcj", inv, eye).reshape(4 * G, 4 * W)
    return [np.asarray(a, dtype=bf16) for a in (z_fwd, left, left_inv, z_inv)]


def split_two(value):
    high = value.astype(bf16)
    return high, (value - high.astype(f32)).astype(bf16)


def split_three(value):
    high = value.astype(bf16)
    rest = value - high.astype(f32)
    middle = rest.astype(bf16)
    return high, middle, (rest - middle.astype(f32)).astype(bf16)


def dot(a, b):
    return jnp.dot(a, b, preferred_element_type=f32)


def dot_nt(a, b):
    return lax.dot_general(a, b, (((1,), (1,)), ((), ())), preferred_element_type=f32)


def iota(shape, dim):
    return lax.broadcasted_iota(jnp.int32, shape, dim)


def orbitals_kernel(
    rot_hbm, coeff_hbm, out_hbm, coeff_ref, rot_ref, turned_ref, wide_ref, out_ref, sems
):
    lanes = 2048 // CHUNKS

    def fetch(k):
        at = pl.ds(k * lanes, lanes)
        return pltpu.make_async_copy(coeff_hbm.at[:, at], coeff_ref.at[:, at], sems.at[k])

    turned = pltpu.make_async_copy(rot_hbm, rot_ref, sems.at[CHUNKS])
    turned.start()
    for k in range(CHUNKS):
        fetch(k).start()
    source, target = iota((256, 256), 0), iota((256, 256), 1)
    same = (source & 63) == (target & 63)
    same &= (source >> 7) == ((target >> 6) & 1)
    same &= ((source >> 6) & 1) == (target >> 7)
    pack = jnp.where(same, 1.0, 0.0).astype(bf16)
    turned.wait()
    turned_ref[...] = rot_ref[...].T
    for k in range(CHUNKS):
        fetch(k).wait()
        both = dot(turned_ref[...], coeff_ref[:, k * lanes : (k + 1) * lanes]).astype(bf16)
        for j in range(lanes // 128):
            at = slice(128 * j, 128 * j + 128)
            pair = jnp.concatenate([both[:HALF, at], both[HALF:, at]], 1)
            moved = dot(pair, pack)
            y = k * (lanes // 64) + 2 * j
            wide_ref[pl.ds(y, HALF, stride=LINE), :] = moved[:, :128]
            wide_ref[pl.ds(y + 1, HALF, stride=LINE), :] = moved[:, 128:]
    parts = 4
    rows = HALF * W // parts

    def send(k):
        at = pl.ds(k * rows, rows)
        return pltpu.make_async_copy(out_ref.at[at], out_hbm.at[at], sems.at[CHUNKS + 1 + k])

    for k in range(parts):
        for t in range(k * HALF // parts, (k + 1) * HALF // parts):
            out_ref[t * W : t * W + W, :] = wide_ref[t * LINE : t * LINE + W, :].astype(bf16)
        send(k).start()
    for k in range(parts):
        send(k).wait()


def own_orbitals(rotation, coeff):
    return pl.pallas_call(
        orbitals_kernel,
        in_specs=hbm(2),
        out_specs=hbm(1)[0],
        out_shape=pltpu.HBM((HALF * W, 128), bf16),
        scratch_shapes=[
            pltpu.VMEM((BANDS, 2048), bf16),
            pltpu.VMEM((BANDS, BLOCK), bf16),
            pltpu.VMEM((BLOCK, BANDS), bf16),
            pltpu.VMEM((HALF * LINE, 128), f32),
            pltpu.VMEM((HALF * W, 128), bf16),
            pltpu.SemaphoreType.DMA((CHUNKS + 5,)),
        ],
        compiler_params=pltpu.CompilerParams(vmem_limit_bytes=20 << 20),
        name="orbitals",
    )(in_hbm(rotation), in_hbm(coeff))


def in_hbm(array):
    return pltpu.with_memory_space_constraint(array, pltpu.HBM)


def hbm(count):
    return [pl.BlockSpec(memory_space=pltpu.HBM)] * count


def vmem(count):
    return [pl.BlockSpec(memory_space=pltpu.VMEM)] * count


def gaussian(position, rows):
    cells = iota((rows, position.shape[1]), 0) & (G - 1)
    offset = (((cells - position + G // 2) & (G - 1)) - G // 2).astype(f32)
    return jnp.exp(-offset * offset / (2.0 * sigma_cells * sigma_cells)), offset


def strengths(species, depth_ref):
    strength = jnp.zeros(species.shape, f32)
    for kind in range(SPECIES):
        strength = jnp.where(species == kind, depth_ref[kind], strength)
    return strength


def potential_kernel(depth_ref, pos_ref, species_ref, out_ref, gy_ref):
    strength = strengths(species_ref[...], depth_ref)
    gauss_x, _ = gaussian(pos_ref[0:1, :], G)
    gauss_x = gauss_x * strength
    gy_ref[...], _ = gaussian(pos_ref[1:2, :], G)
    gauss_z, _ = gaussian(pos_ref[2:3, :], 2 * G)
    z_high, z_low = split_two(gauss_z)
    per = 8

    def some(i, carry):
        for k in range(per):
            m = i * per + k
            value = gauss_x * gy_ref[pl.ds(m, 1), :]
            high, low = split_two(value)
            out_ref[pl.ds(pl.multiple_of(m * G, G), G), :] = (
                dot_nt(high, z_high) + dot_nt(high, z_low) + dot_nt(low, z_high)
            )
        return carry

    lax.fori_loop(0, G // per, some, 0)


def grid_potential(depth, pos, species):
    return pl.pallas_call(
        potential_kernel,
        in_specs=[pl.BlockSpec(memory_space=pltpu.SMEM)] + vmem(2),
        out_specs=vmem(1)[0],
        out_shape=jax.ShapeDtypeStruct((G * G, 128), f32),
        scratch_shapes=[pltpu.VMEM((G, 256), f32)],
        compiler_params=pltpu.CompilerParams(vmem_limit_bytes=10 << 20),
        name="potential",
    )(depth, pos, species)


def transform_kernel(
    orb_ref, pot_ref, zf_ref, left_ref, left_inv_ref, zi_ref,
    out_hbm, dens_hbm, ritz_ref,
    mid_ref, ham_ref, num_ref, den_ref, dens_ref, out_ref, sems,
):
    group = GROUP
    rows = group * OWN * W

    def forward(i, carry):
        x = i * group
        zin = orb_ref[pl.ds(pl.multiple_of(x * OWN * W, rows), rows), :]
        along_z = dot(zin, zf_ref[...]).astype(bf16)
        parts = []
        for g in range(group * OWN):
            piece = along_z[W * g : W * g + W]
            parts.append(jnp.concatenate([piece[:, :128], piece[:, 128:]], 0))
        along_y = dot(left_ref[...], jnp.concatenate(parts, 1))
        for g in range(group * OWN):
            xx, tt = x + g // OWN, g % OWN
            at = (tt * W + xx) * PITCH
            mid_ref[pl.ds(at, 2 * G), :] = along_y[:, 128 * g : 128 * g + 128]
        return carry

    lax.fori_loop(0, W // group, forward, 0)

    def space(i, carry):
        parts = []
        for k in range(MB * OWN):
            base = (k % OWN) * W * PITCH + i * MB + k // OWN
            parts.append(
                jnp.concatenate(
                    [mid_ref[pl.ds(base + c * G, W, stride=PITCH), :] for c in range(2)], 0
                ).astype(bf16)
            )
        in_space = dot(left_ref[...], jnp.concatenate(parts, 1))
        weighted = []
        for mm in range(MB):
            at = pl.multiple_of((i * MB + mm) * G, G)
            potential = pot_ref[pl.ds(at, G), :]
            potential = jnp.concatenate([potential, potential], 0)
            density = jnp.zeros((2 * G, 128), f32)
            for tt in range(OWN):
                k = mm * OWN + tt
                one = in_space[:, 128 * k : 128 * k + 128]
                density = density + one * one
                weighted.append((one * potential).astype(bf16))
            dens_ref[pl.ds(at, G), :] = (density[:G] + density[G:]) * (1.0 / BLOCK)
        back = dot(left_inv_ref[...], jnp.concatenate(weighted, 1))
        for k in range(MB * OWN):
            base = (k % OWN) * W * PITCH + i * MB + k // OWN
            for c in range(2):
                mid_ref[pl.ds(base + c * G, W, stride=PITCH), :] = back[
                    W * c : W * c + W, 128 * k : 128 * k + 128
                ]
        return carry

    lax.fori_loop(0, G // MB, space, 0, unroll=SU)
    keep = pltpu.make_async_copy(dens_ref, dens_hbm, sems.at[4])
    keep.start()

    lane = iota((W, 128), 1)
    wave_y = iota((W, 128), 0) - W // 2
    wave_z = (lane & (W - 1)) - W // 2
    plane = wave_y * wave_y + wave_z * wave_z

    def kinetic(x):
        wave_x = x - W // 2
        return (kinetic_scale * 0.5) * (plane + wave_x * wave_x).astype(f32)

    num_ref[...] = jnp.zeros_like(num_ref)
    den_ref[...] = jnp.zeros_like(den_ref)

    def backward(i, carry):
        x = i * group
        parts = []
        for g in range(group * OWN):
            xx, tt = x + g // OWN, g % OWN
            at = (tt * W + xx) * PITCH
            parts.append(mid_ref[pl.ds(at, 2 * G), :].astype(bf16))
        back_y = dot(left_inv_ref[...], jnp.concatenate(parts, 1)).astype(bf16)
        parts = []
        for g in range(group * OWN):
            piece = back_y[:, 128 * g : 128 * g + 128]
            parts.append(jnp.concatenate([piece[:W], piece[W:]], 1))
        local = dot(jnp.concatenate(parts, 0), zi_ref[...])
        for g in range(group * OWN):
            xx, tt = x + g // OWN, g % OWN
            at = pl.multiple_of((xx * OWN + tt) * W, W)
            orbital = orb_ref[pl.ds(at, W), :].astype(f32)
            ham = kinetic(xx) * orbital + local[W * g : W * g + W]
            ham_ref[pl.ds(at, W), :] = ham
            num_ref[pl.ds(tt * W, W), :] += orbital * ham
            den_ref[pl.ds(tt * W, W), :] += orbital * orbital
        return carry

    lax.fori_loop(0, W // group, backward, 0)

    lane_row = iota((1, 128), 1)
    low = lane_row < 64
    ritz_row = jnp.zeros((1, 128), f32)
    ritz = []
    for tt in range(OWN):
        halves = []
        num = jnp.sum(num_ref[pl.ds(tt * W, W), :], 0, keepdims=True)
        den = jnp.sum(den_ref[pl.ds(tt * W, W), :], 0, keepdims=True)
        for p in range(2):
            mine = low if p == 0 else jnp.logical_not(low)
            top = jnp.sum(jnp.where(mine, num, 0.0), 1, keepdims=True)
            bottom = jnp.sum(jnp.where(mine, den, 0.0), 1, keepdims=True)
            value = (top / NPW) / (bottom / NPW + epsilon)
            halves.append(value)
            ritz_row = jnp.where(lane_row == 32 + p * OWN + tt, value, ritz_row)
        ritz.append(jnp.where(low, halves[0], halves[1]))
    ritz_ref[...] = jnp.broadcast_to(ritz_row, (8, 128))

    parts = 4
    rows = W * OWN * W // parts

    def send(k):
        at = pl.ds(k * rows, rows)
        return pltpu.make_async_copy(out_ref.at[at], out_hbm.at[at], sems.at[k])

    for x in range(W):
        kin = kinetic(x)
        scale = 1.0 / (1.0 + kin)
        for tt in range(OWN):
            at = pl.ds((x * OWN + tt) * W, W)
            orbital = orb_ref[at, :].astype(f32)
            residual = ham_ref[at, :] - ritz[tt] * orbital
            out_ref[at, :] = (residual * scale).astype(bf16)
        if (x + 1) % (W // parts) == 0:
            send(x // (W // parts)).start()
    for k in range(parts):
        send(k).wait()
    keep.wait()


def searched(orbitals, potential):
    z_fwd, left, left_inv, z_inv = host_tables()
    return pl.pallas_call(
        transform_kernel,
        in_specs=vmem(6),
        out_specs=hbm(2) + vmem(1),
        out_shape=[
            pltpu.HBM((W * OWN * W, 128), bf16),
            pltpu.HBM((G * G, 128), f32),
            jax.ShapeDtypeStruct((8, 128), f32),
        ],
        scratch_shapes=[
            pltpu.VMEM((OWN * W * PITCH, 128), f32),
            pltpu.VMEM((W * OWN * W, 128), f32),
            pltpu.VMEM((OWN * W, 128), f32),
            pltpu.VMEM((OWN * W, 128), f32),
            pltpu.VMEM((G * G, 128), f32),
            pltpu.VMEM((W * OWN * W, 128), bf16),
            pltpu.SemaphoreType.DMA((5,)),
        ],
        compiler_params=pltpu.CompilerParams(vmem_limit_bytes=30 << 20),
        name="transform",
    )(orbitals, potential, z_fwd, left, left_inv, z_inv)


def force_kernel(
    depth_ref, dens_ref, pos_ref, species_ref, ritz_ref, out_ref, gy_ref, gyo_ref, wide_ref
):
    strength = strengths(species_ref[...], depth_ref)
    gauss_x, offset_x = gaussian(pos_ref[0:1, :], G)
    gauss_y, offset_y = gaussian(pos_ref[1:2, :], G)
    gauss_z, offset_z = gaussian(pos_ref[2:3, :], 2 * G)
    gy_ref[...] = gauss_y
    gyo_ref[...] = gauss_y * offset_y
    high, low = split_two(jnp.concatenate([gauss_z, gauss_z * offset_z], 1))
    both = jnp.concatenate([high, low], 0)
    per = 4

    def some(i, carry):
        sum_x, sum_y, sum_z = carry
        at = pl.multiple_of(i * per * G, per * G)
        d_high, d_low = split_two(dens_ref[pl.ds(at, per * G), :])
        moments = dot(jnp.concatenate([d_high, d_high], 1), both) + dot(d_low, high)
        for k in range(per):
            gy = gy_ref[pl.ds(i * per + k, 1), :]
            gyo = gyo_ref[pl.ds(i * per + k, 1), :]
            plain = moments[G * k : G * k + G, :256]
            sum_x = sum_x + plain * gy
            sum_y = sum_y + plain * gyo
            sum_z = sum_z + moments[G * k : G * k + G, 256:] * gy
        return sum_x, sum_y, sum_z

    zero = jnp.zeros((G, 256), f32)
    sum_x, sum_y, sum_z = lax.fori_loop(0, G // per, some, (zero, zero, zero))
    factor = -strength / (sigma_cells * sigma_cells)
    force = [
        factor * jnp.sum(gauss_x * offset_x * sum_x, 0, keepdims=True),
        factor * jnp.sum(gauss_x * sum_y, 0, keepdims=True),
        factor * jnp.sum(gauss_x * sum_z, 0, keepdims=True),
    ]
    peer, atom = iota((PEERS, 256), 0), iota((PEERS, 256), 1)
    from_atom, lane = iota((256, 128), 0), iota((256, 128), 1)
    parts = [part.astype(f32) for part in split_three(ritz_ref[0:1, :])]
    totals = [jnp.broadcast_to(part, (PEERS, 128)) for part in parts]
    for alpha in range(3):
        own = jnp.where(atom // 8 == peer, force[alpha], 0.0)
        choose = jnp.where((from_atom & 7) + 8 * alpha == lane, 1.0, 0.0).astype(bf16)
        for k, part in enumerate(split_three(own)):
            totals[k] = totals[k] + dot(part, choose)
    wide_ref[...] = jnp.zeros_like(wide_ref)
    for k in range(3):
        wide_ref[pl.ds(k, PEERS, stride=8), :] = totals[k]
    out_ref[...] = wide_ref[...].reshape(PEERS, 8, 128).astype(bf16)


def force_parts(depth, density, pos, species, ritz):
    return pl.pallas_call(
        force_kernel,
        in_specs=[pl.BlockSpec(memory_space=pltpu.SMEM)] + vmem(4),
        out_specs=vmem(1)[0],
        out_shape=jax.ShapeDtypeStruct((PEERS, 8, 128), bf16),
        scratch_shapes=[
            pltpu.VMEM((G, 256), f32),
            pltpu.VMEM((G, 256), f32),
            pltpu.VMEM((PEERS * 8, 128), f32),
        ],
        compiler_params=pltpu.CompilerParams(vmem_limit_bytes=10 << 20),
        name="force",
    )(depth, density, pos, species, ritz)


def intersect_kernel(
    search_ref, extra_ref, coeff_hbm, out_ref, flat_ref,
    coeff_ref, wide_ref, pair_ref, sems,
):
    bands = BANDS // FETCHES

    def fetch(k):
        at = pl.ds(k * bands, bands)
        return pltpu.make_async_copy(coeff_hbm.at[at], coeff_ref.at[at], sems.at[k])

    for k in range(FETCHES):
        fetch(k).start()
    source, target = iota((256, 512), 0), iota((256, 512), 1)
    part, element = target >> 7, target & 63
    turned = part >> 1
    same = (source & 63) == (element ^ (turned * 32))
    same &= (source >> 7) == ((target >> 6) & 1)
    same &= ((source >> 6) & 1) == (part & 1)
    sign = jnp.where((turned == 1) & (element >= 32), -1.0, 1.0)
    unpack = jnp.where(same, sign, 0.0).astype(bf16)
    for t in range(HALF):
        wide_ref[t * LINE : t * LINE + W, :] = search_ref[t * W : t * W + W, :].astype(f32)
    out_ref[:, 128:, :] = extra_ref[...]
    for j in range(W // 2):
        even = wide_ref[pl.ds(2 * j, HALF, stride=LINE), :]
        odd = wide_ref[pl.ds(2 * j + 1, HALF, stride=LINE), :]
        moved = dot(jnp.concatenate([even, odd], 1).astype(bf16), unpack).astype(bf16)
        at = slice(128 * j, 128 * j + 128)
        for q in range(4):
            piece = moved[:, 128 * q : 128 * q + 128]
            pair_ref[HALF * q : HALF * q + HALF, at] = piece
            if q < 2:
                flat_ref[HALF * q : HALF * q + HALF, at] = piece
    for k in range(FETCHES):
        fetch(k).wait()
        part = dot_nt(pair_ref[...], coeff_ref[bands * k : bands * k + bands, :])
        part = (part * (1.0 / NPW)).astype(bf16)
        for j in range(bands // 128):
            at = 16 * (k * bands // 128 + j)
            out_ref[:, at : at + 16, :] = part[:, 128 * j : 128 * j + 128].reshape(PEERS, 16, 128)


def own_intersections(search, coeff, extra):
    return pl.pallas_call(
        intersect_kernel,
        in_specs=vmem(2) + hbm(1),
        out_specs=vmem(2),
        out_shape=[
            jax.ShapeDtypeStruct((PEERS, ROWS, 128), bf16),
            jax.ShapeDtypeStruct((BLOCK, 2048), bf16),
        ],
        scratch_shapes=[
            pltpu.VMEM((BANDS, 2048), bf16),
            pltpu.VMEM((HALF * LINE, 128), f32),
            pltpu.VMEM((2 * BLOCK, 2048), bf16),
            pltpu.SemaphoreType.DMA((FETCHES,)),
        ],
        compiler_params=pltpu.CompilerParams(vmem_limit_bytes=20 << 20),
        name="intersect",
    )(search, extra, in_hbm(coeff))


def total_kernel(in_ref, out_ref):
    for r in range(8):
        at = slice(16 * r, 16 * r + 16)
        total = in_ref[0, at, :].astype(f32)
        for peer in range(1, PEERS):
            total = total + in_ref[peer, at, :].astype(f32)
        total = total.astype(bf16)
        for peer in range(PEERS):
            out_ref[peer, at, :] = total
    extra = in_ref[0, 128:, :].astype(f32)
    for peer in range(1, PEERS):
        extra = extra + in_ref[peer, 128:, :].astype(f32)
    high, middle, low = split_three(extra[0:1] + extra[1:2] + extra[2:3])
    row = iota((8, 128), 0)
    parts = jnp.where(row == 0, high.astype(f32), 0.0)
    parts = jnp.where(row == 1, middle.astype(f32), parts)
    parts = jnp.where(row == 2, low.astype(f32), parts).astype(bf16)
    for peer in range(PEERS):
        out_ref[peer, 128:, :] = parts


def totals_for_all(arrived):
    return pl.pallas_call(
        total_kernel,
        in_specs=vmem(1),
        out_specs=vmem(1)[0],
        out_shape=jax.ShapeDtypeStruct((PEERS, ROWS, 128), bf16),
        compiler_params=pltpu.CompilerParams(vmem_limit_bytes=6 << 20),
        name="total",
    )(arrived)


def wrap_offset(values):
    return ((values + G // 2) & (G - 1)) - G // 2


def row_of(ref, base, lane_wanted, peer_wanted):
    lane = iota((128, 256), 0)
    choose = jnp.where(lane == lane_wanted, 1.0, 0.0).astype(bf16)
    parts = ref[:, base : base + 8, :].astype(f32).reshape(PEERS * 8, 128).astype(bf16)
    here = jnp.where((iota((PEERS * 8, 256), 0) >> 3) == peer_wanted, dot(parts, choose), 0.0)
    return jnp.sum(here, 0, keepdims=True)


def prepare_kernel(
    image_ref, first_ref, pos_ref, before_ref, after_ref, start_ref, end_ref,
    ritz_ref, tangent_ref, spring_ref,
):
    column, at = iota((128, 256), 1), iota((PEERS * 8, 256), 1)
    ritz_ref[...] = row_of(
        first_ref, 128, 32 + OWN * (column // HALF) + column % OWN, at % HALF // OWN
    )
    pos = pos_ref[...]
    image = image_ref[0]
    before = jnp.where(image == 0, start_ref[...], before_ref[...])
    after = jnp.where(image == image_ref[1] - 1, end_ref[...], after_ref[...])
    ahead = wrap_offset(after - pos).astype(f32)
    behind = wrap_offset(pos - before).astype(f32)
    raw = ahead + behind
    entries = pos.shape[0] * pos.shape[1]

    def mean_square(value):
        return jnp.sum(jnp.sum(value * value, 1, keepdims=True), 0, keepdims=True) / entries

    tangent = raw * lax.rsqrt(mean_square(raw) + epsilon) * (1.0 / math.sqrt(entries))
    length_ahead = jnp.sqrt(entries * (mean_square(ahead) + epsilon))
    length_behind = jnp.sqrt(entries * (mean_square(behind) + epsilon))
    tangent_ref[...] = tangent
    spring_ref[...] = spring_constant * (length_ahead - length_behind) * tangent


def prepared(image, arrived, pos, before, after, start_pos, end_pos):
    return pl.pallas_call(
        prepare_kernel,
        in_specs=[pl.BlockSpec(memory_space=pltpu.SMEM)] + vmem(6),
        out_specs=vmem(3),
        out_shape=[
            jax.ShapeDtypeStruct((1, 256), f32),
            jax.ShapeDtypeStruct((3, 256), f32),
            jax.ShapeDtypeStruct((3, 256), f32),
        ],
        compiler_params=pltpu.CompilerParams(vmem_limit_bytes=6 << 20),
        name="prepare",
    )(image, arrived, pos, before, after, start_pos, end_pos)


def project_kernel(
    whole_ref, flat_ref, tangent_ref, spring_ref, coeff_hbm,
    out_hbm, push_ref, along_ref, coeff_ref, inter_ref, done_ref, sems, fetch_sems,
):
    wide = 2048 // FETCHES

    def fetch(k):
        at = pl.ds(k * wide, wide)
        return pltpu.make_async_copy(coeff_hbm.at[:, at], coeff_ref.at[:, at], fetch_sems.at[k])

    for k in range(FETCHES):
        fetch(k).start()
    lanes = 256
    chunks = 2048 // lanes
    for j in range(8):
        inter_ref[:, 128 * j : 128 * j + 128] = whole_ref[:, 16 * j : 16 * j + 16, :].reshape(
            2 * BLOCK, 128
        )
    first = (iota((BLOCK, 128), 1) & 63) < 32

    def send(k):
        at = pl.ds(k * lanes, lanes)
        return pltpu.make_async_copy(done_ref.at[:, at], out_hbm.at[:, at], sems.at[k])

    column, at = iota((128, 256), 1), iota((PEERS * 8, 256), 1)
    tangent = tangent_ref[...]
    force = jnp.concatenate(
        [row_of(whole_ref, 128, 8 * alpha + (column & 7), at >> 3) for alpha in range(3)], 0
    )
    along = jnp.sum(jnp.sum(force * tangent, 1, keepdims=True), 0, keepdims=True)
    push = force - along * tangent + spring_ref[...]
    for alpha in range(3):
        push_ref[alpha] = push[alpha : alpha + 1]
    along_ref[...] = along
    for k in range(chunks):
        if k * lanes % wide == 0:
            fetch(k * lanes // wide).wait()
        projected = dot(inter_ref[...], coeff_ref[:, k * lanes : (k + 1) * lanes])
        for j in range(lanes // 128):
            here = slice(128 * j, 128 * j + 128)
            at = slice(k * lanes + 128 * j, k * lanes + 128 * j + 128)
            turned = projected[BLOCK:, here]
            turned = jnp.where(first, -pltpu.roll(turned, 96, 1), pltpu.roll(turned, 32, 1))
            done_ref[:, at] = (
                flat_ref[:, at].astype(f32) - (projected[:BLOCK, here] + turned)
            ).astype(bf16)
        send(k).start()

    for k in range(chunks):
        send(k).wait()


def corrected(whole, flat, tangent, spring, coeff):
    return pl.pallas_call(
        project_kernel,
        in_specs=vmem(4) + hbm(1),
        out_specs=hbm(1) + vmem(2),
        out_shape=[
            pltpu.HBM((BLOCK, 2048), bf16),
            jax.ShapeDtypeStruct((3, 1, 256), f32),
            jax.ShapeDtypeStruct((1, 1), f32),
        ],
        scratch_shapes=[
            pltpu.VMEM((BANDS, 2048), bf16),
            pltpu.VMEM((2 * BLOCK, BANDS), bf16),
            pltpu.VMEM((BLOCK, 2048), bf16),
            pltpu.SemaphoreType.DMA((8,)),
            pltpu.SemaphoreType.DMA((FETCHES,)),
        ],
        compiler_params=pltpu.CompilerParams(vmem_limit_bytes=16 << 20),
        name="project",
    )(whole, flat, tangent, spring, in_hbm(coeff))


def exchanged(array):
    return lax.all_to_all(array, GRID_AXES, split_axis=0, concat_axis=0, tiled=True)


def passed_along(block, axis, distance):
    devices = range(lax.axis_size(axis))
    route = [(i - distance, i) for i in devices if i - distance in devices]
    return lax.ppermute(block, axis, route)


def body(coefficients, rotation, positions, start_pos, end_pos, species, depth):
    coeff = coefficients.reshape(BANDS, 2048)
    pos = positions[0]
    kinds = species.reshape(1, -1)
    orbitals = own_orbitals(rotation[0], coeff)
    vectors = exchanged(orbitals.reshape(PEERS, OWN * W, 128))
    potential = grid_potential(depth, pos, kinds)
    search, density, ritz = searched(vectors.reshape(W * OWN * W, 128), potential)
    own_search = exchanged(search.reshape(PEERS, OWN * W, 128))
    extra = force_parts(depth, density, pos, kinds, ritz)
    parts, flat = own_intersections(own_search.reshape(HALF * W, 128), coeff, extra)
    arrived = exchanged(parts)
    mine = totals_for_all(arrived)
    later = lax.optimization_barrier((pos, mine))[0]
    before = passed_along(later, "img", 1)
    after = passed_along(later, "img", -1)
    whole = exchanged(mine)
    image = jnp.stack([lax.axis_index("img"), lax.axis_size("img")]).astype(jnp.int32)
    arrived, before, after = lax.optimization_barrier((arrived, before, after, mine))[:3]
    ritz_values, tangent, spring = prepared(
        image, arrived, pos, before, after, start_pos, end_pos
    )
    correction, push, along = corrected(whole, flat, tangent, spring, coeff)
    return (
        correction.reshape(1, BLOCK, 1, 2048),
        ritz_values,
        push.transpose(1, 0, 2),
        along.reshape(1),
    )


def solution(mesh):
    in_specs = (
        P("img", None, GRID_AXES, None),
        P("img", None, None),
        P("img", None, None),
        P(),
        P(),
        P(),
        P(),
    )
    out_specs = (
        P("img", None, GRID_AXES, None),
        P("img", None),
        P("img", None, None),
        P("img"),
    )
    return jax.shard_map(body, mesh=mesh, in_specs=in_specs, out_specs=out_specs, check_vma=False)
```

```python
import math

import jax
import jax.numpy as jnp
import numpy as np
from jax import lax
from jax.experimental import pallas as pl
from jax.experimental.pallas import tpu as pltpu
from jax.sharding import PartitionSpec as P

G = 64
W = 32
BANDS = 1024
BLOCK = 256
SPECIES = 4
NPW = W * W * W
PEERS = 32
OWN = BLOCK // PEERS // 2
HALF = BLOCK // 2
PITCH = 2 * G + 1
GROUP = 32
MB = 16
SU = 1
ROWS = 136
CHUNKS = 2
FETCHES = 2
LINE = W + 1

kinetic_scale = 0.01
sigma_cells = 3.0
spring_constant = 2.0
epsilon = 1e-06

f32 = jnp.float32
bf16 = jnp.bfloat16
GRID_AXES = ("band", "pw")


def host_phases():
    turns = np.mod((np.arange(W) - W // 2)[:, None] * np.arange(G)[None, :], G)
    return turns.astype(np.float32) * np.float32(2.0 * math.pi / G)


def host_tables():
    angle = host_phases()
    cosine, sine = np.cos(angle), np.sin(angle)
    s = np.float32(1.0 / math.sqrt(W))
    fwd = np.stack([np.stack([cosine, sine], 1), np.stack([-sine, cosine], 1)], 0) * s
    t = np.float32(math.sqrt(W) / G)
    c2, s2 = cosine.T * t, sine.T * t
    inv = np.stack([np.stack([c2, -s2], 1), np.stack([s2, c2], 1)], 0)
    left = fwd.transpose(2, 3, 0, 1).reshape(2 * G, 2 * W)
    left_inv = inv.transpose(2, 3, 0, 1).reshape(2 * W, 2 * G)
    eye = np.eye(2, dtype=np.float32)
    z_fwd = np.einsum("cjdn,pq->pcjdqn", fwd, eye).reshape(4 * W, 4 * G)
    z_inv = np.einsum("dncj,pq->dpnqcj", inv, eye).reshape(4 * G, 4 * W)
    return [np.asarray(a, dtype=bf16) for a in (z_fwd, left, left_inv, z_inv)]


def split_two(value):
    high = value.astype(bf16)
    return high, (value - high.astype(f32)).astype(bf16)


def split_three(value):
    high = value.astype(bf16)
    rest = value - high.astype(f32)
    middle = rest.astype(bf16)
    return high, middle, (rest - middle.astype(f32)).astype(bf16)


def dot(a, b):
    return jnp.dot(a, b, preferred_element_type=f32)


def dot_nt(a, b):
    return lax.dot_general(a, b, (((1,), (1,)), ((), ())), preferred_element_type=f32)


def iota(shape, dim):
    return lax.broadcasted_iota(jnp.int32, shape, dim)


def orbitals_kernel(
    rot_hbm, coeff_hbm, out_hbm, coeff_ref, rot_ref, turned_ref, wide_ref, out_ref, sems
):
    lanes = 2048 // CHUNKS

    def fetch(k):
        at = pl.ds(k * lanes, lanes)
        return pltpu.make_async_copy(coeff_hbm.at[:, at], coeff_ref.at[:, at], sems.at[k])

    turned = pltpu.make_async_copy(rot_hbm, rot_ref, sems.at[CHUNKS])
    turned.start()
    for k in range(CHUNKS):
        fetch(k).start()
    source, target = iota((256, 256), 0), iota((256, 256), 1)
    same = (source & 63) == (target & 63)
    same &= (source >> 7) == ((target >> 6) & 1)
    same &= ((source >> 6) & 1) == (target >> 7)
    pack = jnp.where(same, 1.0, 0.0).astype(bf16)
    turned.wait()
    turned_ref[...] = rot_ref[...].T
    for k in range(CHUNKS):
        fetch(k).wait()
        both = dot(turned_ref[...], coeff_ref[:, k * lanes : (k + 1) * lanes]).astype(bf16)
        for j in range(lanes // 128):
            at = slice(128 * j, 128 * j + 128)
            pair = jnp.concatenate([both[:HALF, at], both[HALF:, at]], 1)
            moved = dot(pair, pack)
            y = k * (lanes // 64) + 2 * j
            wide_ref[pl.ds(y, HALF, stride=LINE), :] = moved[:, :128]
            wide_ref[pl.ds(y + 1, HALF, stride=LINE), :] = moved[:, 128:]
    parts = 4
    rows = HALF * W // parts

    def send(k):
        at = pl.ds(k * rows, rows)
        return pltpu.make_async_copy(out_ref.at[at], out_hbm.at[at], sems.at[CHUNKS + 1 + k])

    for k in range(parts):
        for t in range(k * HALF // parts, (k + 1) * HALF // parts):
            out_ref[t * W : t * W + W, :] = wide_ref[t * LINE : t * LINE + W, :].astype(bf16)
        send(k).start()
    for k in range(parts):
        send(k).wait()


def own_orbitals(rotation, coeff):
    return pl.pallas_call(
        orbitals_kernel,
        in_specs=hbm(2),
        out_specs=hbm(1)[0],
        out_shape=pltpu.HBM((HALF * W, 128), bf16),
        scratch_shapes=[
            pltpu.VMEM((BANDS, 2048), bf16),
            pltpu.VMEM((BANDS, BLOCK), bf16),
            pltpu.VMEM((BLOCK, BANDS), bf16),
            pltpu.VMEM((HALF * LINE, 128), f32),
            pltpu.VMEM((HALF * W, 128), bf16),
            pltpu.SemaphoreType.DMA((CHUNKS + 5,)),
        ],
        compiler_params=pltpu.CompilerParams(vmem_limit_bytes=20 << 20),
        name="orbitals",
    )(in_hbm(rotation), in_hbm(coeff))


def in_hbm(array):
    return pltpu.with_memory_space_constraint(array, pltpu.HBM)


def near_kernel(coeff_hbm, order_ref, out_ref, sem):
    half = coeff_hbm.shape[1] // 2
    fetch = pltpu.make_async_copy(coeff_hbm.at[:, pl.ds(0, half)], out_ref, sem)
    fetch.start()
    fetch.wait()


def brought_near(coeff, order):
    return pl.pallas_call(
        near_kernel,
        in_specs=hbm(1) + vmem(1),
        out_specs=vmem(1)[0],
        out_shape=jax.ShapeDtypeStruct((BANDS, 1024), bf16),
        scratch_shapes=[pltpu.SemaphoreType.DMA],
        compiler_params=pltpu.CompilerParams(vmem_limit_bytes=1 << 20),
        name="near",
    )(in_hbm(coeff), order)


def hbm(count):
    return [pl.BlockSpec(memory_space=pltpu.HBM)] * count


def vmem(count):
    return [pl.BlockSpec(memory_space=pltpu.VMEM)] * count


def gaussian(position, rows):
    cells = iota((rows, position.shape[1]), 0) & (G - 1)
    offset = (((cells - position + G // 2) & (G - 1)) - G // 2).astype(f32)
    return jnp.exp(-offset * offset / (2.0 * sigma_cells * sigma_cells)), offset


def strengths(species, depth_ref):
    strength = jnp.zeros(species.shape, f32)
    for kind in range(SPECIES):
        strength = jnp.where(species == kind, depth_ref[kind], strength)
    return strength


def potential_kernel(depth_ref, pos_ref, species_ref, out_ref, gy_ref):
    strength = strengths(species_ref[...], depth_ref)
    gauss_x, _ = gaussian(pos_ref[0:1, :], G)
    gauss_x = gauss_x * strength
    gy_ref[...], _ = gaussian(pos_ref[1:2, :], G)
    gauss_z, _ = gaussian(pos_ref[2:3, :], 2 * G)
    z_high, z_low = split_two(gauss_z)
    per = 8

    def some(i, carry):
        for k in range(per):
            m = i * per + k
            value = gauss_x * gy_ref[pl.ds(m, 1), :]
            high, low = split_two(value)
            out_ref[pl.ds(pl.multiple_of(m * G, G), G), :] = (
                dot_nt(high, z_high) + dot_nt(high, z_low) + dot_nt(low, z_high)
            )
        return carry

    lax.fori_loop(0, G // per, some, 0)


def grid_potential(depth, pos, species):
    return pl.pallas_call(
        potential_kernel,
        in_specs=[pl.BlockSpec(memory_space=pltpu.SMEM)] + vmem(2),
        out_specs=vmem(1)[0],
        out_shape=jax.ShapeDtypeStruct((G * G, 128), f32),
        scratch_shapes=[pltpu.VMEM((G, 256), f32)],
        compiler_params=pltpu.CompilerParams(vmem_limit_bytes=10 << 20),
        name="potential",
    )(depth, pos, species)


def transform_kernel(
    orb_ref, pot_ref, zf_ref, left_ref, left_inv_ref, zi_ref,
    out_hbm, dens_hbm, ritz_ref,
    mid_ref, ham_ref, num_ref, den_ref, dens_ref, out_ref, sems,
):
    group = GROUP
    rows = group * OWN * W

    def forward(i, carry):
        x = i * group
        zin = orb_ref[pl.ds(pl.multiple_of(x * OWN * W, rows), rows), :]
        along_z = dot(zin, zf_ref[...]).astype(bf16)
        parts = []
        for g in range(group * OWN):
            piece = along_z[W * g : W * g + W]
            parts.append(jnp.concatenate([piece[:, :128], piece[:, 128:]], 0))
        along_y = dot(left_ref[...], jnp.concatenate(parts, 1))
        for g in range(group * OWN):
            xx, tt = x + g // OWN, g % OWN
            at = (tt * W + xx) * PITCH
            mid_ref[pl.ds(at, 2 * G), :] = along_y[:, 128 * g : 128 * g + 128]
        return carry

    lax.fori_loop(0, W // group, forward, 0)

    def space(i, carry):
        parts = []
        for k in range(MB * OWN):
            base = (k % OWN) * W * PITCH + i * MB + k // OWN
            parts.append(
                jnp.concatenate(
                    [mid_ref[pl.ds(base + c * G, W, stride=PITCH), :] for c in range(2)], 0
                ).astype(bf16)
            )
        in_space = dot(left_ref[...], jnp.concatenate(parts, 1))
        weighted = []
        for mm in range(MB):
            at = pl.multiple_of((i * MB + mm) * G, G)
            potential = pot_ref[pl.ds(at, G), :]
            potential = jnp.concatenate([potential, potential], 0)
            density = jnp.zeros((2 * G, 128), f32)
            for tt in range(OWN):
                k = mm * OWN + tt
                one = in_space[:, 128 * k : 128 * k + 128]
                density = density + one * one
                weighted.append((one * potential).astype(bf16))
            dens_ref[pl.ds(at, G), :] = (density[:G] + density[G:]) * (1.0 / BLOCK)
        back = dot(left_inv_ref[...], jnp.concatenate(weighted, 1))
        for k in range(MB * OWN):
            base = (k % OWN) * W * PITCH + i * MB + k // OWN
            for c in range(2):
                mid_ref[pl.ds(base + c * G, W, stride=PITCH), :] = back[
                    W * c : W * c + W, 128 * k : 128 * k + 128
                ]
        return carry

    lax.fori_loop(0, G // MB, space, 0, unroll=SU)
    keep = pltpu.make_async_copy(dens_ref, dens_hbm, sems.at[4])
    keep.start()

    lane = iota((W, 128), 1)
    wave_y = iota((W, 128), 0) - W // 2
    wave_z = (lane & (W - 1)) - W // 2
    plane = wave_y * wave_y + wave_z * wave_z

    def kinetic(x):
        wave_x = x - W // 2
        return (kinetic_scale * 0.5) * (plane + wave_x * wave_x).astype(f32)

    num_ref[...] = jnp.zeros_like(num_ref)
    den_ref[...] = jnp.zeros_like(den_ref)

    def backward(i, carry):
        x = i * group
        parts = []
        for g in range(group * OWN):
            xx, tt = x + g // OWN, g % OWN
            at = (tt * W + xx) * PITCH
            parts.append(mid_ref[pl.ds(at, 2 * G), :].astype(bf16))
        back_y = dot(left_inv_ref[...], jnp.concatenate(parts, 1)).astype(bf16)
        parts = []
        for g in range(group * OWN):
            piece = back_y[:, 128 * g : 128 * g + 128]
            parts.append(jnp.concatenate([piece[:W], piece[W:]], 1))
        local = dot(jnp.concatenate(parts, 0), zi_ref[...])
        for g in range(group * OWN):
            xx, tt = x + g // OWN, g % OWN
            at = pl.multiple_of((xx * OWN + tt) * W, W)
            orbital = orb_ref[pl.ds(at, W), :].astype(f32)
            ham = kinetic(xx) * orbital + local[W * g : W * g + W]
            ham_ref[pl.ds(at, W), :] = ham
            num_ref[pl.ds(tt * W, W), :] += orbital * ham
            den_ref[pl.ds(tt * W, W), :] += orbital * orbital
        return carry

    lax.fori_loop(0, W // group, backward, 0)

    lane_row = iota((1, 128), 1)
    low = lane_row < 64
    ritz_row = jnp.zeros((1, 128), f32)
    ritz = []
    for tt in range(OWN):
        halves = []
        num = jnp.sum(num_ref[pl.ds(tt * W, W), :], 0, keepdims=True)
        den = jnp.sum(den_ref[pl.ds(tt * W, W), :], 0, keepdims=True)
        for p in range(2):
            mine = low if p == 0 else jnp.logical_not(low)
            top = jnp.sum(jnp.where(mine, num, 0.0), 1, keepdims=True)
            bottom = jnp.sum(jnp.where(mine, den, 0.0), 1, keepdims=True)
            value = (top / NPW) / (bottom / NPW + epsilon)
            halves.append(value)
            ritz_row = jnp.where(lane_row == 32 + p * OWN + tt, value, ritz_row)
        ritz.append(jnp.where(low, halves[0], halves[1]))
    ritz_ref[...] = jnp.broadcast_to(ritz_row, (8, 128))

    parts = 4
    rows = W * OWN * W // parts

    def send(k):
        at = pl.ds(k * rows, rows)
        return pltpu.make_async_copy(out_ref.at[at], out_hbm.at[at], sems.at[k])

    for x in range(W):
        kin = kinetic(x)
        scale = 1.0 / (1.0 + kin)
        for tt in range(OWN):
            at = pl.ds((x * OWN + tt) * W, W)
            orbital = orb_ref[at, :].astype(f32)
            residual = ham_ref[at, :] - ritz[tt] * orbital
            out_ref[at, :] = (residual * scale).astype(bf16)
        if (x + 1) % (W // parts) == 0:
            send(x // (W // parts)).start()
    for k in range(parts):
        send(k).wait()
    keep.wait()


def searched(orbitals, potential):
    z_fwd, left, left_inv, z_inv = host_tables()
    return pl.pallas_call(
        transform_kernel,
        in_specs=vmem(6),
        out_specs=hbm(2) + vmem(1),
        out_shape=[
            pltpu.HBM((W * OWN * W, 128), bf16),
            pltpu.HBM((G * G, 128), f32),
            jax.ShapeDtypeStruct((8, 128), f32),
        ],
        scratch_shapes=[
            pltpu.VMEM((OWN * W * PITCH, 128), f32),
            pltpu.VMEM((W * OWN * W, 128), f32),
            pltpu.VMEM((OWN * W, 128), f32),
            pltpu.VMEM((OWN * W, 128), f32),
            pltpu.VMEM((G * G, 128), f32),
            pltpu.VMEM((W * OWN * W, 128), bf16),
            pltpu.SemaphoreType.DMA((5,)),
        ],
        compiler_params=pltpu.CompilerParams(vmem_limit_bytes=30 << 20),
        name="transform",
    )(orbitals, potential, z_fwd, left, left_inv, z_inv)


def force_kernel(
    depth_ref, dens_ref, pos_ref, species_ref, ritz_ref, out_ref, gy_ref, gyo_ref, wide_ref
):
    strength = strengths(species_ref[...], depth_ref)
    gauss_x, offset_x = gaussian(pos_ref[0:1, :], G)
    gauss_y, offset_y = gaussian(pos_ref[1:2, :], G)
    gauss_z, offset_z = gaussian(pos_ref[2:3, :], 2 * G)
    gy_ref[...] = gauss_y
    gyo_ref[...] = gauss_y * offset_y
    high, low = split_two(jnp.concatenate([gauss_z, gauss_z * offset_z], 1))
    both = jnp.concatenate([high, low], 0)
    per = 4

    def some(i, carry):
        sum_x, sum_y, sum_z = carry
        at = pl.multiple_of(i * per * G, per * G)
        d_high, d_low = split_two(dens_ref[pl.ds(at, per * G), :])
        moments = dot(jnp.concatenate([d_high, d_high], 1), both) + dot(d_low, high)
        for k in range(per):
            gy = gy_ref[pl.ds(i * per + k, 1), :]
            gyo = gyo_ref[pl.ds(i * per + k, 1), :]
            plain = moments[G * k : G * k + G, :256]
            sum_x = sum_x + plain * gy
            sum_y = sum_y + plain * gyo
            sum_z = sum_z + moments[G * k : G * k + G, 256:] * gy
        return sum_x, sum_y, sum_z

    zero = jnp.zeros((G, 256), f32)
    sum_x, sum_y, sum_z = lax.fori_loop(0, G // per, some, (zero, zero, zero))
    factor = -strength / (sigma_cells * sigma_cells)
    force = [
        factor * jnp.sum(gauss_x * offset_x * sum_x, 0, keepdims=True),
        factor * jnp.sum(gauss_x * sum_y, 0, keepdims=True),
        factor * jnp.sum(gauss_x * sum_z, 0, keepdims=True),
    ]
    peer, atom = iota((PEERS, 256), 0), iota((PEERS, 256), 1)
    from_atom, lane = iota((256, 128), 0), iota((256, 128), 1)
    parts = [part.astype(f32) for part in split_three(ritz_ref[0:1, :])]
    totals = [jnp.broadcast_to(part, (PEERS, 128)) for part in parts]
    for alpha in range(3):
        own = jnp.where(atom // 8 == peer, force[alpha], 0.0)
        choose = jnp.where((from_atom & 7) + 8 * alpha == lane, 1.0, 0.0).astype(bf16)
        for k, part in enumerate(split_three(own)):
            totals[k] = totals[k] + dot(part, choose)
    wide_ref[...] = jnp.zeros_like(wide_ref)
    for k in range(3):
        wide_ref[pl.ds(k, PEERS, stride=8), :] = totals[k]
    out_ref[...] = wide_ref[...].reshape(PEERS, 8, 128).astype(bf16)


def force_parts(depth, density, pos, species, ritz):
    return pl.pallas_call(
        force_kernel,
        in_specs=[pl.BlockSpec(memory_space=pltpu.SMEM)] + vmem(4),
        out_specs=vmem(1)[0],
        out_shape=jax.ShapeDtypeStruct((PEERS, 8, 128), bf16),
        scratch_shapes=[
            pltpu.VMEM((G, 256), f32),
            pltpu.VMEM((G, 256), f32),
            pltpu.VMEM((PEERS * 8, 128), f32),
        ],
        compiler_params=pltpu.CompilerParams(vmem_limit_bytes=10 << 20),
        name="force",
    )(depth, density, pos, species, ritz)


def intersect_kernel(
    search_ref, extra_ref, coeff_hbm, out_ref, flat_ref,
    coeff_ref, wide_ref, pair_ref, sems,
):
    bands = BANDS // FETCHES

    def fetch(k):
        at = pl.ds(k * bands, bands)
        return pltpu.make_async_copy(coeff_hbm.at[at], coeff_ref.at[at], sems.at[k])

    for k in range(FETCHES):
        fetch(k).start()
    source, target = iota((256, 512), 0), iota((256, 512), 1)
    part, element = target >> 7, target & 63
    turned = part >> 1
    same = (source & 63) == (element ^ (turned * 32))
    same &= (source >> 7) == ((target >> 6) & 1)
    same &= ((source >> 6) & 1) == (part & 1)
    sign = jnp.where((turned == 1) & (element >= 32), -1.0, 1.0)
    unpack = jnp.where(same, sign, 0.0).astype(bf16)
    for t in range(HALF):
        wide_ref[t * LINE : t * LINE + W, :] = search_ref[t * W : t * W + W, :].astype(f32)
    out_ref[:, 128:, :] = extra_ref[...]
    for j in range(W // 2):
        even = wide_ref[pl.ds(2 * j, HALF, stride=LINE), :]
        odd = wide_ref[pl.ds(2 * j + 1, HALF, stride=LINE), :]
        moved = dot(jnp.concatenate([even, odd], 1).astype(bf16), unpack).astype(bf16)
        at = slice(128 * j, 128 * j + 128)
        for q in range(4):
            piece = moved[:, 128 * q : 128 * q + 128]
            pair_ref[HALF * q : HALF * q + HALF, at] = piece
            if q < 2:
                flat_ref[HALF * q : HALF * q + HALF, at] = piece
    for k in range(FETCHES):
        fetch(k).wait()
        part = dot_nt(pair_ref[...], coeff_ref[bands * k : bands * k + bands, :])
        part = (part * (1.0 / NPW)).astype(bf16)
        for j in range(bands // 128):
            at = 16 * (k * bands // 128 + j)
            out_ref[:, at : at + 16, :] = part[:, 128 * j : 128 * j + 128].reshape(PEERS, 16, 128)


def own_intersections(search, coeff, extra):
    return pl.pallas_call(
        intersect_kernel,
        in_specs=vmem(2) + hbm(1),
        out_specs=vmem(2),
        out_shape=[
            jax.ShapeDtypeStruct((PEERS, ROWS, 128), bf16),
            jax.ShapeDtypeStruct((BLOCK, 2048), bf16),
        ],
        scratch_shapes=[
            pltpu.VMEM((BANDS, 2048), bf16),
            pltpu.VMEM((HALF * LINE, 128), f32),
            pltpu.VMEM((2 * BLOCK, 2048), bf16),
            pltpu.SemaphoreType.DMA((FETCHES,)),
        ],
        compiler_params=pltpu.CompilerParams(vmem_limit_bytes=20 << 20),
        name="intersect",
    )(search, extra, in_hbm(coeff))


def total_kernel(in_ref, out_ref):
    for r in range(8):
        at = slice(16 * r, 16 * r + 16)
        total = in_ref[0, at, :].astype(f32)
        for peer in range(1, PEERS):
            total = total + in_ref[peer, at, :].astype(f32)
        total = total.astype(bf16)
        for peer in range(PEERS):
            out_ref[peer, at, :] = total
    extra = in_ref[0, 128:, :].astype(f32)
    for peer in range(1, PEERS):
        extra = extra + in_ref[peer, 128:, :].astype(f32)
    high, middle, low = split_three(extra[0:1] + extra[1:2] + extra[2:3])
    row = iota((8, 128), 0)
    parts = jnp.where(row == 0, high.astype(f32), 0.0)
    parts = jnp.where(row == 1, middle.astype(f32), parts)
    parts = jnp.where(row == 2, low.astype(f32), parts).astype(bf16)
    for peer in range(PEERS):
        out_ref[peer, 128:, :] = parts


def totals_for_all(arrived):
    return pl.pallas_call(
        total_kernel,
        in_specs=vmem(1),
        out_specs=vmem(1)[0],
        out_shape=jax.ShapeDtypeStruct((PEERS, ROWS, 128), bf16),
        compiler_params=pltpu.CompilerParams(vmem_limit_bytes=6 << 20),
        name="total",
    )(arrived)


def wrap_offset(values):
    return ((values + G // 2) & (G - 1)) - G // 2


def row_of(ref, base, lane_wanted, peer_wanted):
    lane = iota((128, 256), 0)
    choose = jnp.where(lane == lane_wanted, 1.0, 0.0).astype(bf16)
    parts = ref[:, base : base + 8, :].astype(f32).reshape(PEERS * 8, 128).astype(bf16)
    here = jnp.where((iota((PEERS * 8, 256), 0) >> 3) == peer_wanted, dot(parts, choose), 0.0)
    return jnp.sum(here, 0, keepdims=True)


def prepare_kernel(
    image_ref, first_ref, pos_ref, before_ref, after_ref, start_ref, end_ref,
    ritz_ref, tangent_ref, spring_ref,
):
    column, at = iota((128, 256), 1), iota((PEERS * 8, 256), 1)
    ritz_ref[...] = row_of(
        first_ref, 128, 32 + OWN * (column // HALF) + column % OWN, at % HALF // OWN
    )
    pos = pos_ref[...]
    image = image_ref[0]
    before = jnp.where(image == 0, start_ref[...], before_ref[...])
    after = jnp.where(image == image_ref[1] - 1, end_ref[...], after_ref[...])
    ahead = wrap_offset(after - pos).astype(f32)
    behind = wrap_offset(pos - before).astype(f32)
    raw = ahead + behind
    entries = pos.shape[0] * pos.shape[1]

    def mean_square(value):
        return jnp.sum(jnp.sum(value * value, 1, keepdims=True), 0, keepdims=True) / entries

    tangent = raw * lax.rsqrt(mean_square(raw) + epsilon) * (1.0 / math.sqrt(entries))
    length_ahead = jnp.sqrt(entries * (mean_square(ahead) + epsilon))
    length_behind = jnp.sqrt(entries * (mean_square(behind) + epsilon))
    tangent_ref[...] = tangent
    spring_ref[...] = spring_constant * (length_ahead - length_behind) * tangent


def prepared(image, arrived, pos, before, after, start_pos, end_pos):
    return pl.pallas_call(
        prepare_kernel,
        in_specs=[pl.BlockSpec(memory_space=pltpu.SMEM)] + vmem(6),
        out_specs=vmem(3),
        out_shape=[
            jax.ShapeDtypeStruct((1, 256), f32),
            jax.ShapeDtypeStruct((3, 256), f32),
            jax.ShapeDtypeStruct((3, 256), f32),
        ],
        compiler_params=pltpu.CompilerParams(vmem_limit_bytes=6 << 20),
        name="prepare",
    )(image, arrived, pos, before, after, start_pos, end_pos)


def project_kernel(
    whole_ref, tangent_ref, spring_ref, near_ref, coeff_hbm, flat_hbm,
    out_hbm, push_ref, along_ref, rest_ref, flat_ref, inter_ref, done_ref, sems, rest_sem, flat_sem,
):
    search = pltpu.make_async_copy(flat_hbm, flat_ref, flat_sem)
    search.start()
    half = near_ref.shape[1]
    rest = pltpu.make_async_copy(coeff_hbm.at[:, pl.ds(half, half)], rest_ref, rest_sem)
    rest.start()
    lanes = 256
    chunks = 2048 // lanes
    for j in range(8):
        inter_ref[:, 128 * j : 128 * j + 128] = whole_ref[:, 16 * j : 16 * j + 16, :].reshape(
            2 * BLOCK, 128
        )
    first = (iota((BLOCK, 128), 1) & 63) < 32

    def send(k):
        at = pl.ds(k * lanes, lanes)
        return pltpu.make_async_copy(done_ref.at[:, at], out_hbm.at[:, at], sems.at[k])

    column, at = iota((128, 256), 1), iota((PEERS * 8, 256), 1)
    tangent = tangent_ref[...]
    force = jnp.concatenate(
        [row_of(whole_ref, 128, 8 * alpha + (column & 7), at >> 3) for alpha in range(3)], 0
    )
    along = jnp.sum(jnp.sum(force * tangent, 1, keepdims=True), 0, keepdims=True)
    push = force - along * tangent + spring_ref[...]
    for alpha in range(3):
        push_ref[alpha] = push[alpha : alpha + 1]
    along_ref[...] = along
    for k in range(chunks):
        if k == 0:
            search.wait()
        if k * lanes == half:
            rest.wait()
        side_ref = near_ref if k * lanes < half else rest_ref
        start = k * lanes % half
        projected = dot(inter_ref[...], side_ref[:, start : start + lanes])
        for j in range(lanes // 128):
            here = slice(128 * j, 128 * j + 128)
            at = slice(k * lanes + 128 * j, k * lanes + 128 * j + 128)
            turned = projected[BLOCK:, here]
            turned = jnp.where(first, -pltpu.roll(turned, 96, 1), pltpu.roll(turned, 32, 1))
            done_ref[:, at] = (
                flat_ref[:, at].astype(f32) - (projected[:BLOCK, here] + turned)
            ).astype(bf16)
        send(k).start()

    for k in range(chunks):
        send(k).wait()


def corrected(whole, flat, tangent, spring, near, coeff):
    return pl.pallas_call(
        project_kernel,
        in_specs=vmem(4) + hbm(2),
        out_specs=hbm(1) + vmem(2),
        out_shape=[
            pltpu.HBM((BLOCK, 2048), bf16),
            jax.ShapeDtypeStruct((3, 1, 256), f32),
            jax.ShapeDtypeStruct((1, 1), f32),
        ],
        scratch_shapes=[
            pltpu.VMEM((BANDS, 1024), bf16),
            pltpu.VMEM((BLOCK, 2048), bf16),
            pltpu.VMEM((2 * BLOCK, BANDS), bf16),
            pltpu.VMEM((BLOCK, 2048), bf16),
            pltpu.SemaphoreType.DMA((8,)),
            pltpu.SemaphoreType.DMA,
            pltpu.SemaphoreType.DMA,
        ],
        compiler_params=pltpu.CompilerParams(vmem_limit_bytes=16 << 20),
        name="project",
    )(whole, tangent, spring, near, in_hbm(coeff), in_hbm(flat))


def exchanged(array):
    return lax.all_to_all(array, GRID_AXES, split_axis=0, concat_axis=0, tiled=True)


def passed_along(block, axis, distance):
    devices = range(lax.axis_size(axis))
    route = [(i - distance, i) for i in devices if i - distance in devices]
    return lax.ppermute(block, axis, route)


def body(coefficients, rotation, positions, start_pos, end_pos, species, depth):
    coeff = coefficients.reshape(BANDS, 2048)
    pos = positions[0]
    kinds = species.reshape(1, -1)
    orbitals = own_orbitals(rotation[0], coeff)
    vectors = exchanged(orbitals.reshape(PEERS, OWN * W, 128))
    later = lax.optimization_barrier((pos, orbitals))[0]
    before = passed_along(later, "img", 1)
    after = passed_along(later, "img", -1)
    own, before, after = lax.optimization_barrier((pos, before, after))
    potential = grid_potential(depth, own, kinds)
    search, density, ritz = searched(vectors.reshape(W * OWN * W, 128), potential)
    own_search = exchanged(search.reshape(PEERS, OWN * W, 128))
    extra = force_parts(depth, density, pos, kinds, ritz)
    parts, flat = own_intersections(own_search.reshape(HALF * W, 128), coeff, extra)
    arrived = exchanged(parts)
    mine = totals_for_all(arrived)
    whole = exchanged(mine)
    image = jnp.stack([lax.axis_index("img"), lax.axis_size("img")]).astype(jnp.int32)
    arrived, before, after = lax.optimization_barrier((arrived, before, after, mine))[:3]
    ritz_values, tangent, spring = prepared(
        image, arrived, pos, before, after, start_pos, end_pos
    )
    near = brought_near(coeff, tangent)
    correction, push, along = corrected(whole, flat, tangent, spring, near, coeff)
    return (
        correction.reshape(1, BLOCK, 1, 2048),
        ritz_values,
        push.transpose(1, 0, 2),
        along.reshape(1),
    )


def solution(mesh):
    in_specs = (
        P("img", None, GRID_AXES, None),
        P("img", None, None),
        P("img", None, None),
        P(),
        P(),
        P(),
        P(),
    )
    out_specs = (
        P("img", None, GRID_AXES, None),
        P("img", None),
        P("img", None, None),
        P("img"),
    )
    return jax.shard_map(body, mesh=mesh, in_specs=in_specs, out_specs=out_specs, check_vma=False)
```

```python
import math

import jax
import jax.numpy as jnp
import numpy as np
from jax import lax
from jax.experimental import pallas as pl
from jax.experimental.pallas import tpu as pltpu
from jax.sharding import PartitionSpec as P

G = 64
W = 32
BANDS = 1024
BLOCK = 256
SPECIES = 4
NPW = W * W * W
PEERS = 32
OWN = BLOCK // PEERS // 2
HALF = BLOCK // 2
PITCH = 2 * G + 1
GROUP = 32
MB = 16
SU = 1
ROWS = 136
CHUNKS = 2
FETCHES = 2
LINE = W + 1

kinetic_scale = 0.01
sigma_cells = 3.0
spring_constant = 2.0
epsilon = 1e-06

f32 = jnp.float32
bf16 = jnp.bfloat16
GRID_AXES = ("band", "pw")


def host_phases():
    turns = np.mod((np.arange(W) - W // 2)[:, None] * np.arange(G)[None, :], G)
    return turns.astype(np.float32) * np.float32(2.0 * math.pi / G)


def host_tables():
    angle = host_phases()
    cosine, sine = np.cos(angle), np.sin(angle)
    s = np.float32(1.0 / math.sqrt(W))
    fwd = np.stack([np.stack([cosine, sine], 1), np.stack([-sine, cosine], 1)], 0) * s
    t = np.float32(math.sqrt(W) / G)
    c2, s2 = cosine.T * t, sine.T * t
    inv = np.stack([np.stack([c2, -s2], 1), np.stack([s2, c2], 1)], 0)
    left = fwd.transpose(2, 3, 0, 1).reshape(2 * G, 2 * W)
    left_inv = inv.transpose(2, 3, 0, 1).reshape(2 * W, 2 * G)
    eye = np.eye(2, dtype=np.float32)
    z_fwd = np.einsum("cjdn,pq->pcjdqn", fwd, eye).reshape(4 * W, 4 * G)
    z_inv = np.einsum("dncj,pq->dpnqcj", inv, eye).reshape(4 * G, 4 * W)
    return [np.asarray(a, dtype=bf16) for a in (z_fwd, left, left_inv, z_inv)]


def split_two(value):
    high = value.astype(bf16)
    return high, (value - high.astype(f32)).astype(bf16)


def split_three(value):
    high = value.astype(bf16)
    rest = value - high.astype(f32)
    middle = rest.astype(bf16)
    return high, middle, (rest - middle.astype(f32)).astype(bf16)


def dot(a, b):
    return jnp.dot(a, b, preferred_element_type=f32)


def dot_nt(a, b):
    return lax.dot_general(a, b, (((1,), (1,)), ((), ())), preferred_element_type=f32)


def iota(shape, dim):
    return lax.broadcasted_iota(jnp.int32, shape, dim)


def orbitals_kernel(
    rot_hbm, coeff_hbm, depth_hbm, pos_hbm, species_hbm, out_hbm, pot_hbm,
    coeff_ref, rot_ref, turned_ref, wide_ref, out_ref, pot_ref, gy_ref, depth_ref, pos_ref,
    species_ref, sems, small_sems,
):
    lanes = 2048 // CHUNKS

    def fetch(k):
        at = pl.ds(k * lanes, lanes)
        return pltpu.make_async_copy(coeff_hbm.at[:, at], coeff_ref.at[:, at], sems.at[k])

    turned = pltpu.make_async_copy(rot_hbm, rot_ref, sems.at[CHUNKS])
    turned.start()
    for k in range(CHUNKS):
        fetch(k).start()
    keep = pltpu.make_async_copy(pot_ref, pot_hbm, small_sems.at[3])

    @pl.when(potential_first())
    def _():
        small = [
            pltpu.make_async_copy(source, target, small_sems.at[k])
            for k, (source, target) in enumerate(
                [(depth_hbm, depth_ref), (pos_hbm, pos_ref), (species_hbm, species_ref)]
            )
        ]
        for copy in small:
            copy.start()
        for copy in small:
            copy.wait()
        places = [pos_ref[k] for k in range(3)]
        write_potential(depth_ref, places, species_ref[...], pot_ref, gy_ref)
        keep.start()

    source, target = iota((256, 256), 0), iota((256, 256), 1)
    same = (source & 63) == (target & 63)
    same &= (source >> 7) == ((target >> 6) & 1)
    same &= ((source >> 6) & 1) == (target >> 7)
    pack = jnp.where(same, 1.0, 0.0).astype(bf16)
    turned.wait()
    turned_ref[...] = rot_ref[...].T
    for k in range(CHUNKS):
        fetch(k).wait()
        both = dot(turned_ref[...], coeff_ref[:, k * lanes : (k + 1) * lanes]).astype(bf16)
        for j in range(lanes // 128):
            at = slice(128 * j, 128 * j + 128)
            pair = jnp.concatenate([both[:HALF, at], both[HALF:, at]], 1)
            moved = dot(pair, pack)
            y = k * (lanes // 64) + 2 * j
            wide_ref[pl.ds(y, HALF, stride=LINE), :] = moved[:, :128]
            wide_ref[pl.ds(y + 1, HALF, stride=LINE), :] = moved[:, 128:]
    parts = 4
    rows = HALF * W // parts

    def send(k):
        at = pl.ds(k * rows, rows)
        return pltpu.make_async_copy(out_ref.at[at], out_hbm.at[at], sems.at[CHUNKS + 1 + k])

    for k in range(parts):
        for t in range(k * HALF // parts, (k + 1) * HALF // parts):
            out_ref[t * W : t * W + W, :] = wide_ref[t * LINE : t * LINE + W, :].astype(bf16)
        send(k).start()
    for k in range(parts):
        send(k).wait()

    @pl.when(potential_first())
    def _():
        keep.wait()


def own_orbitals(rotation, coeff, depth, places, species):
    return pl.pallas_call(
        orbitals_kernel,
        in_specs=hbm(5),
        out_specs=hbm(2),
        out_shape=[pltpu.HBM((HALF * W, 128), bf16), pltpu.HBM((G * G, 128), f32)],
        scratch_shapes=[
            pltpu.VMEM((BANDS, 2048), bf16),
            pltpu.VMEM((BANDS, BLOCK), bf16),
            pltpu.VMEM((BLOCK, BANDS), bf16),
            pltpu.VMEM((HALF * LINE, 128), f32),
            pltpu.VMEM((HALF * W, 128), bf16),
            pltpu.VMEM((G * G, 128), f32),
            pltpu.VMEM((G, 256), f32),
            pltpu.SMEM((SPECIES,), f32),
            pltpu.VMEM((3, 1, 256), jnp.int32),
            pltpu.VMEM((1, 256), jnp.int32),
            pltpu.SemaphoreType.DMA((CHUNKS + 5,)),
            pltpu.SemaphoreType.DMA((4,)),
        ],
        compiler_params=pltpu.CompilerParams(vmem_limit_bytes=20 << 20),
        name="orbitals",
    )(*[in_hbm(array) for array in (rotation, coeff, depth, places, species)])


def in_hbm(array):
    return pltpu.with_memory_space_constraint(array, pltpu.HBM)


def hbm(count):
    return [pl.BlockSpec(memory_space=pltpu.HBM)] * count


def vmem(count):
    return [pl.BlockSpec(memory_space=pltpu.VMEM)] * count


def gaussian(position, rows):
    cells = iota((rows, position.shape[1]), 0) & (G - 1)
    offset = (((cells - position + G // 2) & (G - 1)) - G // 2).astype(f32)
    return jnp.exp(-offset * offset / (2.0 * sigma_cells * sigma_cells)), offset


def strengths(species, depth_ref):
    strength = jnp.zeros(species.shape, f32)
    for kind in range(SPECIES):
        strength = jnp.where(species == kind, depth_ref[kind], strength)
    return strength


def write_potential(depth_ref, places, species, out_ref, gy_ref):
    strength = strengths(species, depth_ref)
    gauss_x, _ = gaussian(places[0], G)
    gauss_x = gauss_x * strength
    gy_ref[...], _ = gaussian(places[1], G)
    gauss_z, _ = gaussian(places[2], 2 * G)
    z_high, z_low = split_two(gauss_z)
    per = 8

    def some(i, carry):
        for k in range(per):
            m = i * per + k
            value = gauss_x * gy_ref[pl.ds(m, 1), :]
            high, low = split_two(value)
            out_ref[pl.ds(pl.multiple_of(m * G, G), G), :] = (
                dot_nt(high, z_high) + dot_nt(high, z_low) + dot_nt(low, z_high)
            )
        return carry

    lax.fori_loop(0, G // per, some, 0)


def potential_first():
    return lax.axis_index("img") % 2 == 1


def potential_kernel(depth_ref, pos_ref, species_ref, given_hbm, out_hbm, pot_ref, gy_ref, sem):
    del given_hbm

    @pl.when(jnp.logical_not(potential_first()))
    def _():
        places = [pos_ref[k : k + 1, :] for k in range(3)]
        write_potential(depth_ref, places, species_ref[...], pot_ref, gy_ref)
        keep = pltpu.make_async_copy(pot_ref, out_hbm, sem)
        keep.start()
        keep.wait()


def grid_potential(depth, pos, species, given):
    return pl.pallas_call(
        potential_kernel,
        in_specs=[pl.BlockSpec(memory_space=pltpu.SMEM)] + vmem(2) + hbm(1),
        out_specs=hbm(1)[0],
        out_shape=pltpu.HBM((G * G, 128), f32),
        input_output_aliases={3: 0},
        scratch_shapes=[
            pltpu.VMEM((G * G, 128), f32),
            pltpu.VMEM((G, 256), f32),
            pltpu.SemaphoreType.DMA,
        ],
        compiler_params=pltpu.CompilerParams(vmem_limit_bytes=12 << 20),
        name="potential",
    )(depth, pos, species, in_hbm(given))


def transform_kernel(
    orb_ref, zf_ref, left_ref, left_inv_ref, zi_ref, pot_hbm,
    out_hbm, dens_hbm, ritz_ref,
    pot_ref, mid_ref, ham_ref, num_ref, den_ref, dens_ref, out_ref, sems,
):
    bring = pltpu.make_async_copy(pot_hbm, pot_ref, sems.at[5])
    bring.start()
    group = GROUP
    rows = group * OWN * W

    def forward(i, carry):
        x = i * group
        zin = orb_ref[pl.ds(pl.multiple_of(x * OWN * W, rows), rows), :]
        along_z = dot(zin, zf_ref[...]).astype(bf16)
        parts = []
        for g in range(group * OWN):
            piece = along_z[W * g : W * g + W]
            parts.append(jnp.concatenate([piece[:, :128], piece[:, 128:]], 0))
        along_y = dot(left_ref[...], jnp.concatenate(parts, 1))
        for g in range(group * OWN):
            xx, tt = x + g // OWN, g % OWN
            at = (tt * W + xx) * PITCH
            mid_ref[pl.ds(at, 2 * G), :] = along_y[:, 128 * g : 128 * g + 128]
        return carry

    lax.fori_loop(0, W // group, forward, 0)

    bring.wait()

    def space(i, carry):
        parts = []
        for k in range(MB * OWN):
            base = (k % OWN) * W * PITCH + i * MB + k // OWN
            parts.append(
                jnp.concatenate(
                    [mid_ref[pl.ds(base + c * G, W, stride=PITCH), :] for c in range(2)], 0
                ).astype(bf16)
            )
        in_space = dot(left_ref[...], jnp.concatenate(parts, 1))
        weighted = []
        for mm in range(MB):
            at = pl.multiple_of((i * MB + mm) * G, G)
            potential = pot_ref[pl.ds(at, G), :]
            potential = jnp.concatenate([potential, potential], 0)
            density = jnp.zeros((2 * G, 128), f32)
            for tt in range(OWN):
                k = mm * OWN + tt
                one = in_space[:, 128 * k : 128 * k + 128]
                density = density + one * one
                weighted.append((one * potential).astype(bf16))
            dens_ref[pl.ds(at, G), :] = (density[:G] + density[G:]) * (1.0 / BLOCK)
        back = dot(left_inv_ref[...], jnp.concatenate(weighted, 1))
        for k in range(MB * OWN):
            base = (k % OWN) * W * PITCH + i * MB + k // OWN
            for c in range(2):
                mid_ref[pl.ds(base + c * G, W, stride=PITCH), :] = back[
                    W * c : W * c + W, 128 * k : 128 * k + 128
                ]
        return carry

    lax.fori_loop(0, G // MB, space, 0, unroll=SU)
    keep = pltpu.make_async_copy(dens_ref, dens_hbm, sems.at[4])
    keep.start()

    lane = iota((W, 128), 1)
    wave_y = iota((W, 128), 0) - W // 2
    wave_z = (lane & (W - 1)) - W // 2
    plane = wave_y * wave_y + wave_z * wave_z

    def kinetic(x):
        wave_x = x - W // 2
        return (kinetic_scale * 0.5) * (plane + wave_x * wave_x).astype(f32)

    num_ref[...] = jnp.zeros_like(num_ref)
    den_ref[...] = jnp.zeros_like(den_ref)

    def backward(i, carry):
        x = i * group
        parts = []
        for g in range(group * OWN):
            xx, tt = x + g // OWN, g % OWN
            at = (tt * W + xx) * PITCH
            parts.append(mid_ref[pl.ds(at, 2 * G), :].astype(bf16))
        back_y = dot(left_inv_ref[...], jnp.concatenate(parts, 1)).astype(bf16)
        parts = []
        for g in range(group * OWN):
            piece = back_y[:, 128 * g : 128 * g + 128]
            parts.append(jnp.concatenate([piece[:W], piece[W:]], 1))
        local = dot(jnp.concatenate(parts, 0), zi_ref[...])
        for g in range(group * OWN):
            xx, tt = x + g // OWN, g % OWN
            at = pl.multiple_of((xx * OWN + tt) * W, W)
            orbital = orb_ref[pl.ds(at, W), :].astype(f32)
            ham = kinetic(xx) * orbital + local[W * g : W * g + W]
            ham_ref[pl.ds(at, W), :] = ham
            num_ref[pl.ds(tt * W, W), :] += orbital * ham
            den_ref[pl.ds(tt * W, W), :] += orbital * orbital
        return carry

    lax.fori_loop(0, W // group, backward, 0)

    lane_row = iota((1, 128), 1)
    low = lane_row < 64
    ritz_row = jnp.zeros((1, 128), f32)
    ritz = []
    for tt in range(OWN):
        halves = []
        num = jnp.sum(num_ref[pl.ds(tt * W, W), :], 0, keepdims=True)
        den = jnp.sum(den_ref[pl.ds(tt * W, W), :], 0, keepdims=True)
        for p in range(2):
            mine = low if p == 0 else jnp.logical_not(low)
            top = jnp.sum(jnp.where(mine, num, 0.0), 1, keepdims=True)
            bottom = jnp.sum(jnp.where(mine, den, 0.0), 1, keepdims=True)
            value = (top / NPW) / (bottom / NPW + epsilon)
            halves.append(value)
            ritz_row = jnp.where(lane_row == 32 + p * OWN + tt, value, ritz_row)
        ritz.append(jnp.where(low, halves[0], halves[1]))
    ritz_ref[...] = jnp.broadcast_to(ritz_row, (8, 128))

    parts = 4
    rows = W * OWN * W // parts

    def send(k):
        at = pl.ds(k * rows, rows)
        return pltpu.make_async_copy(out_ref.at[at], out_hbm.at[at], sems.at[k])

    for x in range(W):
        kin = kinetic(x)
        scale = 1.0 / (1.0 + kin)
        for tt in range(OWN):
            at = pl.ds((x * OWN + tt) * W, W)
            orbital = orb_ref[at, :].astype(f32)
            residual = ham_ref[at, :] - ritz[tt] * orbital
            out_ref[at, :] = (residual * scale).astype(bf16)
        if (x + 1) % (W // parts) == 0:
            send(x // (W // parts)).start()
    for k in range(parts):
        send(k).wait()
    keep.wait()


def searched(orbitals, potential):
    z_fwd, left, left_inv, z_inv = host_tables()
    return pl.pallas_call(
        transform_kernel,
        in_specs=vmem(5) + hbm(1),
        out_specs=hbm(2) + vmem(1),
        out_shape=[
            pltpu.HBM((W * OWN * W, 128), bf16),
            pltpu.HBM((G * G, 128), f32),
            jax.ShapeDtypeStruct((8, 128), f32),
        ],
        scratch_shapes=[
            pltpu.VMEM((G * G, 128), f32),
            pltpu.VMEM((OWN * W * PITCH, 128), f32),
            pltpu.VMEM((W * OWN * W, 128), f32),
            pltpu.VMEM((OWN * W, 128), f32),
            pltpu.VMEM((OWN * W, 128), f32),
            pltpu.VMEM((G * G, 128), f32),
            pltpu.VMEM((W * OWN * W, 128), bf16),
            pltpu.SemaphoreType.DMA((6,)),
        ],
        compiler_params=pltpu.CompilerParams(vmem_limit_bytes=30 << 20),
        name="transform",
    )(orbitals, z_fwd, left, left_inv, z_inv, in_hbm(potential))


def force_kernel(
    depth_ref, dens_ref, pos_ref, species_ref, ritz_ref, out_ref, gy_ref, gyo_ref, wide_ref
):
    strength = strengths(species_ref[...], depth_ref)
    gauss_x, offset_x = gaussian(pos_ref[0:1, :], G)
    gauss_y, offset_y = gaussian(pos_ref[1:2, :], G)
    gauss_z, offset_z = gaussian(pos_ref[2:3, :], 2 * G)
    gy_ref[...] = gauss_y
    gyo_ref[...] = gauss_y * offset_y
    high, low = split_two(jnp.concatenate([gauss_z, gauss_z * offset_z], 1))
    both = jnp.concatenate([high, low], 0)
    per = 4

    def some(i, carry):
        sum_x, sum_y, sum_z = carry
        at = pl.multiple_of(i * per * G, per * G)
        d_high, d_low = split_two(dens_ref[pl.ds(at, per * G), :])
        moments = dot(jnp.concatenate([d_high, d_high], 1), both) + dot(d_low, high)
        for k in range(per):
            gy = gy_ref[pl.ds(i * per + k, 1), :]
            gyo = gyo_ref[pl.ds(i * per + k, 1), :]
            plain = moments[G * k : G * k + G, :256]
            sum_x = sum_x + plain * gy
            sum_y = sum_y + plain * gyo
            sum_z = sum_z + moments[G * k : G * k + G, 256:] * gy
        return sum_x, sum_y, sum_z

    zero = jnp.zeros((G, 256), f32)
    sum_x, sum_y, sum_z = lax.fori_loop(0, G // per, some, (zero, zero, zero))
    factor = -strength / (sigma_cells * sigma_cells)
    force = [
        factor * jnp.sum(gauss_x * offset_x * sum_x, 0, keepdims=True),
        factor * jnp.sum(gauss_x * sum_y, 0, keepdims=True),
        factor * jnp.sum(gauss_x * sum_z, 0, keepdims=True),
    ]
    peer, atom = iota((PEERS, 256), 0), iota((PEERS, 256), 1)
    from_atom, lane = iota((256, 128), 0), iota((256, 128), 1)
    parts = [part.astype(f32) for part in split_three(ritz_ref[0:1, :])]
    totals = [jnp.broadcast_to(part, (PEERS, 128)) for part in parts]
    for alpha in range(3):
        own = jnp.where(atom // 8 == peer, force[alpha], 0.0)
        choose = jnp.where((from_atom & 7) + 8 * alpha == lane, 1.0, 0.0).astype(bf16)
        for k, part in enumerate(split_three(own)):
            totals[k] = totals[k] + dot(part, choose)
    wide_ref[...] = jnp.zeros_like(wide_ref)
    for k in range(3):
        wide_ref[pl.ds(k, PEERS, stride=8), :] = totals[k]
    out_ref[...] = wide_ref[...].reshape(PEERS, 8, 128).astype(bf16)


def force_parts(depth, density, pos, species, ritz):
    return pl.pallas_call(
        force_kernel,
        in_specs=[pl.BlockSpec(memory_space=pltpu.SMEM)] + vmem(4),
        out_specs=vmem(1)[0],
        out_shape=jax.ShapeDtypeStruct((PEERS, 8, 128), bf16),
        scratch_shapes=[
            pltpu.VMEM((G, 256), f32),
            pltpu.VMEM((G, 256), f32),
            pltpu.VMEM((PEERS * 8, 128), f32),
        ],
        compiler_params=pltpu.CompilerParams(vmem_limit_bytes=10 << 20),
        name="force",
    )(depth, density, pos, species, ritz)


def intersect_kernel(
    search_ref, extra_ref, coeff_hbm, out_ref, flat_ref,
    coeff_ref, wide_ref, pair_ref, sems,
):
    bands = BANDS // FETCHES

    def fetch(k):
        at = pl.ds(k * bands, bands)
        return pltpu.make_async_copy(coeff_hbm.at[at], coeff_ref.at[at], sems.at[k])

    for k in range(FETCHES):
        fetch(k).start()
    source, target = iota((256, 512), 0), iota((256, 512), 1)
    part, element = target >> 7, target & 63
    turned = part >> 1
    same = (source & 63) == (element ^ (turned * 32))
    same &= (source >> 7) == ((target >> 6) & 1)
    same &= ((source >> 6) & 1) == (part & 1)
    sign = jnp.where((turned == 1) & (element >= 32), -1.0, 1.0)
    unpack = jnp.where(same, sign, 0.0).astype(bf16)
    for t in range(HALF):
        wide_ref[t * LINE : t * LINE + W, :] = search_ref[t * W : t * W + W, :].astype(f32)
    out_ref[:, 128:, :] = extra_ref[...]
    for j in range(W // 2):
        even = wide_ref[pl.ds(2 * j, HALF, stride=LINE), :]
        odd = wide_ref[pl.ds(2 * j + 1, HALF, stride=LINE), :]
        moved = dot(jnp.concatenate([even, odd], 1).astype(bf16), unpack).astype(bf16)
        at = slice(128 * j, 128 * j + 128)
        for q in range(4):
            piece = moved[:, 128 * q : 128 * q + 128]
            pair_ref[HALF * q : HALF * q + HALF, at] = piece
            if q < 2:
                flat_ref[HALF * q : HALF * q + HALF, at] = piece
    for k in range(FETCHES):
        fetch(k).wait()
        part = dot_nt(pair_ref[...], coeff_ref[bands * k : bands * k + bands, :])
        part = (part * (1.0 / NPW)).astype(bf16)
        for j in range(bands // 128):
            at = 16 * (k * bands // 128 + j)
            out_ref[:, at : at + 16, :] = part[:, 128 * j : 128 * j + 128].reshape(PEERS, 16, 128)


def own_intersections(search, coeff, extra):
    return pl.pallas_call(
        intersect_kernel,
        in_specs=vmem(2) + hbm(1),
        out_specs=vmem(2),
        out_shape=[
            jax.ShapeDtypeStruct((PEERS, ROWS, 128), bf16),
            jax.ShapeDtypeStruct((BLOCK, 2048), bf16),
        ],
        scratch_shapes=[
            pltpu.VMEM((BANDS, 2048), bf16),
            pltpu.VMEM((HALF * LINE, 128), f32),
            pltpu.VMEM((2 * BLOCK, 2048), bf16),
            pltpu.SemaphoreType.DMA((FETCHES,)),
        ],
        compiler_params=pltpu.CompilerParams(vmem_limit_bytes=20 << 20),
        name="intersect",
    )(search, extra, in_hbm(coeff))


def total_kernel(in_ref, out_ref):
    for r in range(8):
        at = slice(16 * r, 16 * r + 16)
        total = in_ref[0, at, :].astype(f32)
        for peer in range(1, PEERS):
            total = total + in_ref[peer, at, :].astype(f32)
        total = total.astype(bf16)
        for peer in range(PEERS):
            out_ref[peer, at, :] = total
    extra = in_ref[0, 128:, :].astype(f32)
    for peer in range(1, PEERS):
        extra = extra + in_ref[peer, 128:, :].astype(f32)
    high, middle, low = split_three(extra[0:1] + extra[1:2] + extra[2:3])
    row = iota((8, 128), 0)
    parts = jnp.where(row == 0, high.astype(f32), 0.0)
    parts = jnp.where(row == 1, middle.astype(f32), parts)
    parts = jnp.where(row == 2, low.astype(f32), parts).astype(bf16)
    for peer in range(PEERS):
        out_ref[peer, 128:, :] = parts


def totals_for_all(arrived):
    return pl.pallas_call(
        total_kernel,
        in_specs=vmem(1),
        out_specs=vmem(1)[0],
        out_shape=jax.ShapeDtypeStruct((PEERS, ROWS, 128), bf16),
        compiler_params=pltpu.CompilerParams(vmem_limit_bytes=6 << 20),
        name="total",
    )(arrived)


def wrap_offset(values):
    return ((values + G // 2) & (G - 1)) - G // 2


def row_of(ref, base, lane_wanted, peer_wanted):
    lane = iota((128, 256), 0)
    choose = jnp.where(lane == lane_wanted, 1.0, 0.0).astype(bf16)
    parts = ref[:, base : base + 8, :].astype(f32).reshape(PEERS * 8, 128).astype(bf16)
    here = jnp.where((iota((PEERS * 8, 256), 0) >> 3) == peer_wanted, dot(parts, choose), 0.0)
    return jnp.sum(here, 0, keepdims=True)


def prepare_kernel(
    image_ref, first_ref, pos_ref, before_ref, after_ref, start_ref, end_ref,
    ritz_ref, tangent_ref, spring_ref,
):
    column, at = iota((128, 256), 1), iota((PEERS * 8, 256), 1)
    ritz_ref[...] = row_of(
        first_ref, 128, 32 + OWN * (column // HALF) + column % OWN, at % HALF // OWN
    )
    pos = pos_ref[...]
    image = image_ref[0]
    before = jnp.where(image == 0, start_ref[...], before_ref[...])
    after = jnp.where(image == image_ref[1] - 1, end_ref[...], after_ref[...])
    ahead = wrap_offset(after - pos).astype(f32)
    behind = wrap_offset(pos - before).astype(f32)
    raw = ahead + behind
    entries = pos.shape[0] * pos.shape[1]

    def mean_square(value):
        return jnp.sum(jnp.sum(value * value, 1, keepdims=True), 0, keepdims=True) / entries

    tangent = raw * lax.rsqrt(mean_square(raw) + epsilon) * (1.0 / math.sqrt(entries))
    length_ahead = jnp.sqrt(entries * (mean_square(ahead) + epsilon))
    length_behind = jnp.sqrt(entries * (mean_square(behind) + epsilon))
    tangent_ref[...] = tangent
    spring_ref[...] = spring_constant * (length_ahead - length_behind) * tangent


def prepared(image, arrived, pos, before, after, start_pos, end_pos):
    return pl.pallas_call(
        prepare_kernel,
        in_specs=[pl.BlockSpec(memory_space=pltpu.SMEM)] + vmem(6),
        out_specs=vmem(3),
        out_shape=[
            jax.ShapeDtypeStruct((1, 256), f32),
            jax.ShapeDtypeStruct((3, 256), f32),
            jax.ShapeDtypeStruct((3, 256), f32),
        ],
        compiler_params=pltpu.CompilerParams(vmem_limit_bytes=6 << 20),
        name="prepare",
    )(image, arrived, pos, before, after, start_pos, end_pos)


def project_kernel(
    whole_ref, flat_ref, tangent_ref, spring_ref, coeff_hbm,
    out_hbm, push_ref, along_ref, coeff_ref, inter_ref, done_ref, sems, fetch_sems,
):
    wide = 2048 // FETCHES

    def fetch(k):
        at = pl.ds(k * wide, wide)
        return pltpu.make_async_copy(coeff_hbm.at[:, at], coeff_ref.at[:, at], fetch_sems.at[k])

    for k in range(FETCHES):
        fetch(k).start()
    lanes = 256
    chunks = 2048 // lanes
    for j in range(8):
        inter_ref[:, 128 * j : 128 * j + 128] = whole_ref[:, 16 * j : 16 * j + 16, :].reshape(
            2 * BLOCK, 128
        )
    first = (iota((BLOCK, 128), 1) & 63) < 32

    def send(k):
        at = pl.ds(k * lanes, lanes)
        return pltpu.make_async_copy(done_ref.at[:, at], out_hbm.at[:, at], sems.at[k])

    column, at = iota((128, 256), 1), iota((PEERS * 8, 256), 1)
    tangent = tangent_ref[...]
    force = jnp.concatenate(
        [row_of(whole_ref, 128, 8 * alpha + (column & 7), at >> 3) for alpha in range(3)], 0
    )
    along = jnp.sum(jnp.sum(force * tangent, 1, keepdims=True), 0, keepdims=True)
    push = force - along * tangent + spring_ref[...]
    for alpha in range(3):
        push_ref[alpha] = push[alpha : alpha + 1]
    along_ref[...] = along
    for k in range(chunks):
        if k * lanes % wide == 0:
            fetch(k * lanes // wide).wait()
        projected = dot(inter_ref[...], coeff_ref[:, k * lanes : (k + 1) * lanes])
        for j in range(lanes // 128):
            here = slice(128 * j, 128 * j + 128)
            at = slice(k * lanes + 128 * j, k * lanes + 128 * j + 128)
            turned = projected[BLOCK:, here]
            turned = jnp.where(first, -pltpu.roll(turned, 96, 1), pltpu.roll(turned, 32, 1))
            done_ref[:, at] = (
                flat_ref[:, at].astype(f32) - (projected[:BLOCK, here] + turned)
            ).astype(bf16)
        send(k).start()

    for k in range(chunks):
        send(k).wait()


def corrected(whole, flat, tangent, spring, coeff):
    return pl.pallas_call(
        project_kernel,
        in_specs=vmem(4) + hbm(1),
        out_specs=hbm(1) + vmem(2),
        out_shape=[
            pltpu.HBM((BLOCK, 2048), bf16),
            jax.ShapeDtypeStruct((3, 1, 256), f32),
            jax.ShapeDtypeStruct((1, 1), f32),
        ],
        scratch_shapes=[
            pltpu.VMEM((BANDS, 2048), bf16),
            pltpu.VMEM((2 * BLOCK, BANDS), bf16),
            pltpu.VMEM((BLOCK, 2048), bf16),
            pltpu.SemaphoreType.DMA((8,)),
            pltpu.SemaphoreType.DMA((FETCHES,)),
        ],
        compiler_params=pltpu.CompilerParams(vmem_limit_bytes=16 << 20),
        name="project",
    )(whole, flat, tangent, spring, in_hbm(coeff))


def exchanged(array):
    return lax.all_to_all(array, GRID_AXES, split_axis=0, concat_axis=0, tiled=True)


def passed_along(block, axis, distance):
    devices = range(lax.axis_size(axis))
    route = [(i - distance, i) for i in devices if i - distance in devices]
    return lax.ppermute(block, axis, route)


def body(coefficients, rotation, positions, start_pos, end_pos, species, depth):
    coeff = coefficients.reshape(BANDS, 2048)
    pos = positions[0]
    kinds = species.reshape(1, -1)
    orbitals, given = own_orbitals(
        rotation[0], coeff, depth, positions.transpose(1, 0, 2), kinds
    )
    vectors = exchanged(orbitals.reshape(PEERS, OWN * W, 128))
    potential = grid_potential(depth, pos, kinds, given)
    search, density, ritz = searched(vectors.reshape(W * OWN * W, 128), potential)
    own_search = exchanged(search.reshape(PEERS, OWN * W, 128))
    extra = force_parts(depth, density, pos, kinds, ritz)
    parts, flat = own_intersections(own_search.reshape(HALF * W, 128), coeff, extra)
    arrived = exchanged(parts)
    mine = totals_for_all(arrived)
    later = lax.optimization_barrier((pos, mine))[0]
    before = passed_along(later, "img", 1)
    after = passed_along(later, "img", -1)
    whole = exchanged(mine)
    image = jnp.stack([lax.axis_index("img"), lax.axis_size("img")]).astype(jnp.int32)
    arrived, before, after = lax.optimization_barrier((arrived, before, after, mine))[:3]
    ritz_values, tangent, spring = prepared(
        image, arrived, pos, before, after, start_pos, end_pos
    )
    correction, push, along = corrected(whole, flat, tangent, spring, coeff)
    return (
        correction.reshape(1, BLOCK, 1, 2048),
        ritz_values,
        push.transpose(1, 0, 2),
        along.reshape(1),
    )


def solution(mesh):
    in_specs = (
        P("img", None, GRID_AXES, None),
        P("img", None, None),
        P("img", None, None),
        P(),
        P(),
        P(),
        P(),
    )
    out_specs = (
        P("img", None, GRID_AXES, None),
        P("img", None),
        P("img", None, None),
        P("img"),
    )
    return jax.shard_map(body, mesh=mesh, in_specs=in_specs, out_specs=out_specs, check_vma=False)
```

```python
import math

import jax
import jax.numpy as jnp
import numpy as np
from jax import lax
from jax.experimental import pallas as pl
from jax.experimental.pallas import tpu as pltpu
from jax.sharding import PartitionSpec as P

G = 64
W = 32
BANDS = 1024
BLOCK = 256
SPECIES = 4
NPW = W * W * W
PEERS = 32
OWN = BLOCK // PEERS // 2
HALF = BLOCK // 2
PITCH = 2 * G + 1
GROUP = 32
MB = 16
SU = 1
ROWS = 136
CHUNKS = 2
FETCHES = 2
LINE = W + 1

kinetic_scale = 0.01
sigma_cells = 3.0
spring_constant = 2.0
epsilon = 1e-06

f32 = jnp.float32
bf16 = jnp.bfloat16
GRID_AXES = ("band", "pw")


def host_phases():
    turns = np.mod((np.arange(W) - W // 2)[:, None] * np.arange(G)[None, :], G)
    return turns.astype(np.float32) * np.float32(2.0 * math.pi / G)


def host_tables():
    angle = host_phases()
    cosine, sine = np.cos(angle), np.sin(angle)
    s = np.float32(1.0 / math.sqrt(W))
    fwd = np.stack([np.stack([cosine, sine], 1), np.stack([-sine, cosine], 1)], 0) * s
    t = np.float32(math.sqrt(W) / G)
    c2, s2 = cosine.T * t, sine.T * t
    inv = np.stack([np.stack([c2, -s2], 1), np.stack([s2, c2], 1)], 0)
    left = fwd.transpose(2, 3, 0, 1).reshape(2 * G, 2 * W)
    left_inv = inv.transpose(2, 3, 0, 1).reshape(2 * W, 2 * G)
    eye = np.eye(2, dtype=np.float32)
    z_fwd = np.einsum("cjdn,pq->pcjdqn", fwd, eye).reshape(4 * W, 4 * G)
    z_inv = np.einsum("dncj,pq->dpnqcj", inv, eye).reshape(4 * G, 4 * W)
    return [np.asarray(a, dtype=bf16) for a in (z_fwd, left, left_inv, z_inv)]


def split_two(value):
    high = value.astype(bf16)
    return high, (value - high.astype(f32)).astype(bf16)


def split_three(value):
    high = value.astype(bf16)
    rest = value - high.astype(f32)
    middle = rest.astype(bf16)
    return high, middle, (rest - middle.astype(f32)).astype(bf16)


def dot(a, b):
    return jnp.dot(a, b, preferred_element_type=f32)


def dot_nt(a, b):
    return lax.dot_general(a, b, (((1,), (1,)), ((), ())), preferred_element_type=f32)


def iota(shape, dim):
    return lax.broadcasted_iota(jnp.int32, shape, dim)


def orbitals_kernel(
    rot_hbm, coeff_hbm, depth_hbm, pos_hbm, species_hbm, out_hbm, pot_hbm,
    coeff_ref, rot_ref, turned_ref, wide_ref, out_ref, pot_ref, gy_ref, depth_ref, pos_ref,
    species_ref, sems, small_sems,
):
    lanes = 2048 // CHUNKS

    def fetch(k):
        at = pl.ds(k * lanes, lanes)
        return pltpu.make_async_copy(coeff_hbm.at[:, at], coeff_ref.at[:, at], sems.at[k])

    turned = pltpu.make_async_copy(rot_hbm, rot_ref, sems.at[CHUNKS])
    turned.start()
    for k in range(CHUNKS):
        fetch(k).start()
    keep = pltpu.make_async_copy(pot_ref, pot_hbm, small_sems.at[3])

    @pl.when(potential_first())
    def _():
        small = [
            pltpu.make_async_copy(source, target, small_sems.at[k])
            for k, (source, target) in enumerate(
                [(depth_hbm, depth_ref), (pos_hbm, pos_ref), (species_hbm, species_ref)]
            )
        ]
        for copy in small:
            copy.start()
        for copy in small:
            copy.wait()
        places = [pos_ref[k] for k in range(3)]
        write_potential(depth_ref, places, species_ref[...], pot_ref, gy_ref)
        keep.start()

    source, target = iota((256, 256), 0), iota((256, 256), 1)
    same = (source & 63) == (target & 63)
    same &= (source >> 7) == ((target >> 6) & 1)
    same &= ((source >> 6) & 1) == (target >> 7)
    pack = jnp.where(same, 1.0, 0.0).astype(bf16)
    turned.wait()
    turned_ref[...] = rot_ref[...].T
    for k in range(CHUNKS):
        fetch(k).wait()
        both = dot(turned_ref[...], coeff_ref[:, k * lanes : (k + 1) * lanes]).astype(bf16)
        for j in range(lanes // 128):
            at = slice(128 * j, 128 * j + 128)
            pair = jnp.concatenate([both[:HALF, at], both[HALF:, at]], 1)
            moved = dot(pair, pack)
            y = k * (lanes // 64) + 2 * j
            wide_ref[pl.ds(y, HALF, stride=LINE), :] = moved[:, :128]
            wide_ref[pl.ds(y + 1, HALF, stride=LINE), :] = moved[:, 128:]
    parts = 4
    rows = HALF * W // parts

    def send(k):
        at = pl.ds(k * rows, rows)
        return pltpu.make_async_copy(out_ref.at[at], out_hbm.at[at], sems.at[CHUNKS + 1 + k])

    for k in range(parts):
        for t in range(k * HALF // parts, (k + 1) * HALF // parts):
            out_ref[t * W : t * W + W, :] = wide_ref[t * LINE : t * LINE + W, :].astype(bf16)
        send(k).start()
    for k in range(parts):
        send(k).wait()

    @pl.when(potential_first())
    def _():
        keep.wait()


def own_orbitals(rotation, coeff, depth, places, species):
    return pl.pallas_call(
        orbitals_kernel,
        in_specs=hbm(5),
        out_specs=hbm(2),
        out_shape=[pltpu.HBM((HALF * W, 128), bf16), pltpu.HBM((G * G, 128), f32)],
        scratch_shapes=[
            pltpu.VMEM((BANDS, 2048), bf16),
            pltpu.VMEM((BANDS, BLOCK), bf16),
            pltpu.VMEM((BLOCK, BANDS), bf16),
            pltpu.VMEM((HALF * LINE, 128), f32),
            pltpu.VMEM((HALF * W, 128), bf16),
            pltpu.VMEM((G * G, 128), f32),
            pltpu.VMEM((G, 256), f32),
            pltpu.SMEM((SPECIES,), f32),
            pltpu.VMEM((3, 1, 256), jnp.int32),
            pltpu.VMEM((1, 256), jnp.int32),
            pltpu.SemaphoreType.DMA((CHUNKS + 5,)),
            pltpu.SemaphoreType.DMA((4,)),
        ],
        compiler_params=pltpu.CompilerParams(vmem_limit_bytes=20 << 20),
        name="orbitals",
    )(*[in_hbm(array) for array in (rotation, coeff, depth, places, species)])


def in_hbm(array):
    return pltpu.with_memory_space_constraint(array, pltpu.HBM)


def hbm(count):
    return [pl.BlockSpec(memory_space=pltpu.HBM)] * count


def vmem(count):
    return [pl.BlockSpec(memory_space=pltpu.VMEM)] * count


def gaussian(position, rows):
    cells = iota((rows, position.shape[1]), 0) & (G - 1)
    offset = (((cells - position + G // 2) & (G - 1)) - G // 2).astype(f32)
    return jnp.exp(-offset * offset / (2.0 * sigma_cells * sigma_cells)), offset


def strengths(species, depth_ref):
    strength = jnp.zeros(species.shape, f32)
    for kind in range(SPECIES):
        strength = jnp.where(species == kind, depth_ref[kind], strength)
    return strength


def write_potential(depth_ref, places, species, out_ref, gy_ref):
    strength = strengths(species, depth_ref)
    gauss_x, _ = gaussian(places[0], G)
    gauss_x = gauss_x * strength
    gy_ref[...], _ = gaussian(places[1], G)
    gauss_z, _ = gaussian(places[2], 2 * G)
    z_high, z_low = split_two(gauss_z)
    per = 8

    def some(i, carry):
        for k in range(per):
            m = i * per + k
            value = gauss_x * gy_ref[pl.ds(m, 1), :]
            high, low = split_two(value)
            out_ref[pl.ds(pl.multiple_of(m * G, G), G), :] = (
                dot_nt(high, z_high) + dot_nt(high, z_low) + dot_nt(low, z_high)
            )
        return carry

    lax.fori_loop(0, G // per, some, 0)


def potential_first():
    return lax.axis_index("img") % 2 == 0


def potential_kernel(depth_ref, pos_ref, species_ref, given_hbm, out_hbm, pot_ref, gy_ref, sem):
    del given_hbm

    @pl.when(jnp.logical_not(potential_first()))
    def _():
        places = [pos_ref[k : k + 1, :] for k in range(3)]
        write_potential(depth_ref, places, species_ref[...], pot_ref, gy_ref)
        keep = pltpu.make_async_copy(pot_ref, out_hbm, sem)
        keep.start()
        keep.wait()


def grid_potential(depth, pos, species, given):
    return pl.pallas_call(
        potential_kernel,
        in_specs=[pl.BlockSpec(memory_space=pltpu.SMEM)] + vmem(2) + hbm(1),
        out_specs=hbm(1)[0],
        out_shape=pltpu.HBM((G * G, 128), f32),
        input_output_aliases={3: 0},
        scratch_shapes=[
            pltpu.VMEM((G * G, 128), f32),
            pltpu.VMEM((G, 256), f32),
            pltpu.SemaphoreType.DMA,
        ],
        compiler_params=pltpu.CompilerParams(vmem_limit_bytes=12 << 20),
        name="potential",
    )(depth, pos, species, in_hbm(given))


def transform_kernel(
    orb_ref, zf_ref, left_ref, left_inv_ref, zi_ref, pot_hbm,
    out_hbm, dens_hbm, ritz_ref,
    pot_ref, mid_ref, ham_ref, num_ref, den_ref, dens_ref, out_ref, sems,
):
    bring = pltpu.make_async_copy(pot_hbm, pot_ref, sems.at[5])
    bring.start()
    group = GROUP
    rows = group * OWN * W

    def forward(i, carry):
        x = i * group
        zin = orb_ref[pl.ds(pl.multiple_of(x * OWN * W, rows), rows), :]
        along_z = dot(zin, zf_ref[...]).astype(bf16)
        parts = []
        for g in range(group * OWN):
            piece = along_z[W * g : W * g + W]
            parts.append(jnp.concatenate([piece[:, :128], piece[:, 128:]], 0))
        along_y = dot(left_ref[...], jnp.concatenate(parts, 1))
        for g in range(group * OWN):
            xx, tt = x + g // OWN, g % OWN
            at = (tt * W + xx) * PITCH
            mid_ref[pl.ds(at, 2 * G), :] = along_y[:, 128 * g : 128 * g + 128]
        return carry

    lax.fori_loop(0, W // group, forward, 0)

    bring.wait()

    def space(i, carry):
        parts = []
        for k in range(MB * OWN):
            base = (k % OWN) * W * PITCH + i * MB + k // OWN
            parts.append(
                jnp.concatenate(
                    [mid_ref[pl.ds(base + c * G, W, stride=PITCH), :] for c in range(2)], 0
                ).astype(bf16)
            )
        in_space = dot(left_ref[...], jnp.concatenate(parts, 1))
        weighted = []
        for mm in range(MB):
            at = pl.multiple_of((i * MB + mm) * G, G)
            potential = pot_ref[pl.ds(at, G), :]
            potential = jnp.concatenate([potential, potential], 0)
            density = jnp.zeros((2 * G, 128), f32)
            for tt in range(OWN):
                k = mm * OWN + tt
                one = in_space[:, 128 * k : 128 * k + 128]
                density = density + one * one
                weighted.append((one * potential).astype(bf16))
            dens_ref[pl.ds(at, G), :] = (density[:G] + density[G:]) * (1.0 / BLOCK)
        back = dot(left_inv_ref[...], jnp.concatenate(weighted, 1))
        for k in range(MB * OWN):
            base = (k % OWN) * W * PITCH + i * MB + k // OWN
            for c in range(2):
                mid_ref[pl.ds(base + c * G, W, stride=PITCH), :] = back[
                    W * c : W * c + W, 128 * k : 128 * k + 128
                ]
        return carry

    lax.fori_loop(0, G // MB, space, 0, unroll=SU)
    keep = pltpu.make_async_copy(dens_ref, dens_hbm, sems.at[4])
    keep.start()

    lane = iota((W, 128), 1)
    wave_y = iota((W, 128), 0) - W // 2
    wave_z = (lane & (W - 1)) - W // 2
    plane = wave_y * wave_y + wave_z * wave_z

    def kinetic(x):
        wave_x = x - W // 2
        return (kinetic_scale * 0.5) * (plane + wave_x * wave_x).astype(f32)

    num_ref[...] = jnp.zeros_like(num_ref)
    den_ref[...] = jnp.zeros_like(den_ref)

    def backward(i, carry):
        x = i * group
        parts = []
        for g in range(group * OWN):
            xx, tt = x + g // OWN, g % OWN
            at = (tt * W + xx) * PITCH
            parts.append(mid_ref[pl.ds(at, 2 * G), :].astype(bf16))
        back_y = dot(left_inv_ref[...], jnp.concatenate(parts, 1)).astype(bf16)
        parts = []
        for g in range(group * OWN):
            piece = back_y[:, 128 * g : 128 * g + 128]
            parts.append(jnp.concatenate([piece[:W], piece[W:]], 1))
        local = dot(jnp.concatenate(parts, 0), zi_ref[...])
        for g in range(group * OWN):
            xx, tt = x + g // OWN, g % OWN
            at = pl.multiple_of((xx * OWN + tt) * W, W)
            orbital = orb_ref[pl.ds(at, W), :].astype(f32)
            ham = kinetic(xx) * orbital + local[W * g : W * g + W]
            ham_ref[pl.ds(at, W), :] = ham
            num_ref[pl.ds(tt * W, W), :] += orbital * ham
            den_ref[pl.ds(tt * W, W), :] += orbital * orbital
        return carry

    lax.fori_loop(0, W // group, backward, 0)

    lane_row = iota((1, 128), 1)
    low = lane_row < 64
    ritz_row = jnp.zeros((1, 128), f32)
    ritz = []
    for tt in range(OWN):
        halves = []
        num = jnp.sum(num_ref[pl.ds(tt * W, W), :], 0, keepdims=True)
        den = jnp.sum(den_ref[pl.ds(tt * W, W), :], 0, keepdims=True)
        for p in range(2):
            mine = low if p == 0 else jnp.logical_not(low)
            top = jnp.sum(jnp.where(mine, num, 0.0), 1, keepdims=True)
            bottom = jnp.sum(jnp.where(mine, den, 0.0), 1, keepdims=True)
            value = (top / NPW) / (bottom / NPW + epsilon)
            halves.append(value)
            ritz_row = jnp.where(lane_row == 32 + p * OWN + tt, value, ritz_row)
        ritz.append(jnp.where(low, halves[0], halves[1]))
    ritz_ref[...] = jnp.broadcast_to(ritz_row, (8, 128))

    parts = 4
    rows = W * OWN * W // parts

    def send(k):
        at = pl.ds(k * rows, rows)
        return pltpu.make_async_copy(out_ref.at[at], out_hbm.at[at], sems.at[k])

    for x in range(W):
        kin = kinetic(x)
        scale = 1.0 / (1.0 + kin)
        for tt in range(OWN):
            at = pl.ds((x * OWN + tt) * W, W)
            orbital = orb_ref[at, :].astype(f32)
            residual = ham_ref[at, :] - ritz[tt] * orbital
            out_ref[at, :] = (residual * scale).astype(bf16)
        if (x + 1) % (W // parts) == 0:
            send(x // (W // parts)).start()
    for k in range(parts):
        send(k).wait()
    keep.wait()


def searched(orbitals, potential):
    z_fwd, left, left_inv, z_inv = host_tables()
    return pl.pallas_call(
        transform_kernel,
        in_specs=vmem(5) + hbm(1),
        out_specs=hbm(2) + vmem(1),
        out_shape=[
            pltpu.HBM((W * OWN * W, 128), bf16),
            pltpu.HBM((G * G, 128), f32),
            jax.ShapeDtypeStruct((8, 128), f32),
        ],
        scratch_shapes=[
            pltpu.VMEM((G * G, 128), f32),
            pltpu.VMEM((OWN * W * PITCH, 128), f32),
            pltpu.VMEM((W * OWN * W, 128), f32),
            pltpu.VMEM((OWN * W, 128), f32),
            pltpu.VMEM((OWN * W, 128), f32),
            pltpu.VMEM((G * G, 128), f32),
            pltpu.VMEM((W * OWN * W, 128), bf16),
            pltpu.SemaphoreType.DMA((6,)),
        ],
        compiler_params=pltpu.CompilerParams(vmem_limit_bytes=30 << 20),
        name="transform",
    )(orbitals, z_fwd, left, left_inv, z_inv, in_hbm(potential))


def force_kernel(
    depth_ref, dens_ref, pos_ref, species_ref, ritz_ref, out_ref, gy_ref, gyo_ref, wide_ref
):
    strength = strengths(species_ref[...], depth_ref)
    gauss_x, offset_x = gaussian(pos_ref[0:1, :], G)
    gauss_y, offset_y = gaussian(pos_ref[1:2, :], G)
    gauss_z, offset_z = gaussian(pos_ref[2:3, :], 2 * G)
    gy_ref[...] = gauss_y
    gyo_ref[...] = gauss_y * offset_y
    high, low = split_two(jnp.concatenate([gauss_z, gauss_z * offset_z], 1))
    both = jnp.concatenate([high, low], 0)
    per = 4

    def some(i, carry):
        sum_x, sum_y, sum_z = carry
        at = pl.multiple_of(i * per * G, per * G)
        d_high, d_low = split_two(dens_ref[pl.ds(at, per * G), :])
        moments = dot(jnp.concatenate([d_high, d_high], 1), both) + dot(d_low, high)
        for k in range(per):
            gy = gy_ref[pl.ds(i * per + k, 1), :]
            gyo = gyo_ref[pl.ds(i * per + k, 1), :]
            plain = moments[G * k : G * k + G, :256]
            sum_x = sum_x + plain * gy
            sum_y = sum_y + plain * gyo
            sum_z = sum_z + moments[G * k : G * k + G, 256:] * gy
        return sum_x, sum_y, sum_z

    zero = jnp.zeros((G, 256), f32)
    sum_x, sum_y, sum_z = lax.fori_loop(0, G // per, some, (zero, zero, zero))
    factor = -strength / (sigma_cells * sigma_cells)
    force = [
        factor * jnp.sum(gauss_x * offset_x * sum_x, 0, keepdims=True),
        factor * jnp.sum(gauss_x * sum_y, 0, keepdims=True),
        factor * jnp.sum(gauss_x * sum_z, 0, keepdims=True),
    ]
    peer, atom = iota((PEERS, 256), 0), iota((PEERS, 256), 1)
    from_atom, lane = iota((256, 128), 0), iota((256, 128), 1)
    parts = [part.astype(f32) for part in split_three(ritz_ref[0:1, :])]
    totals = [jnp.broadcast_to(part, (PEERS, 128)) for part in parts]
    for alpha in range(3):
        own = jnp.where(atom // 8 == peer, force[alpha], 0.0)
        choose = jnp.where((from_atom & 7) + 8 * alpha == lane, 1.0, 0.0).astype(bf16)
        for k, part in enumerate(split_three(own)):
            totals[k] = totals[k] + dot(part, choose)
    wide_ref[...] = jnp.zeros_like(wide_ref)
    for k in range(3):
        wide_ref[pl.ds(k, PEERS, stride=8), :] = totals[k]
    out_ref[...] = wide_ref[...].reshape(PEERS, 8, 128).astype(bf16)


def force_parts(depth, density, pos, species, ritz):
    return pl.pallas_call(
        force_kernel,
        in_specs=[pl.BlockSpec(memory_space=pltpu.SMEM)] + vmem(4),
        out_specs=vmem(1)[0],
        out_shape=jax.ShapeDtypeStruct((PEERS, 8, 128), bf16),
        scratch_shapes=[
            pltpu.VMEM((G, 256), f32),
            pltpu.VMEM((G, 256), f32),
            pltpu.VMEM((PEERS * 8, 128), f32),
        ],
        compiler_params=pltpu.CompilerParams(vmem_limit_bytes=10 << 20),
        name="force",
    )(depth, density, pos, species, ritz)


def intersect_kernel(
    search_ref, extra_ref, coeff_hbm, out_ref, flat_ref,
    coeff_ref, wide_ref, pair_ref, sems,
):
    bands = BANDS // FETCHES

    def fetch(k):
        at = pl.ds(k * bands, bands)
        return pltpu.make_async_copy(coeff_hbm.at[at], coeff_ref.at[at], sems.at[k])

    for k in range(FETCHES):
        fetch(k).start()
    source, target = iota((256, 512), 0), iota((256, 512), 1)
    part, element = target >> 7, target & 63
    turned = part >> 1
    same = (source & 63) == (element ^ (turned * 32))
    same &= (source >> 7) == ((target >> 6) & 1)
    same &= ((source >> 6) & 1) == (part & 1)
    sign = jnp.where((turned == 1) & (element >= 32), -1.0, 1.0)
    unpack = jnp.where(same, sign, 0.0).astype(bf16)
    for t in range(HALF):
        wide_ref[t * LINE : t * LINE + W, :] = search_ref[t * W : t * W + W, :].astype(f32)
    out_ref[:, 128:, :] = extra_ref[...]
    for j in range(W // 2):
        even = wide_ref[pl.ds(2 * j, HALF, stride=LINE), :]
        odd = wide_ref[pl.ds(2 * j + 1, HALF, stride=LINE), :]
        moved = dot(jnp.concatenate([even, odd], 1).astype(bf16), unpack).astype(bf16)
        at = slice(128 * j, 128 * j + 128)
        for q in range(4):
            piece = moved[:, 128 * q : 128 * q + 128]
            pair_ref[HALF * q : HALF * q + HALF, at] = piece
            if q < 2:
                flat_ref[HALF * q : HALF * q + HALF, at] = piece
    for k in range(FETCHES):
        fetch(k).wait()
        part = dot_nt(pair_ref[...], coeff_ref[bands * k : bands * k + bands, :])
        part = (part * (1.0 / NPW)).astype(bf16)
        for j in range(bands // 128):
            at = 16 * (k * bands // 128 + j)
            out_ref[:, at : at + 16, :] = part[:, 128 * j : 128 * j + 128].reshape(PEERS, 16, 128)


def own_intersections(search, coeff, extra):
    return pl.pallas_call(
        intersect_kernel,
        in_specs=vmem(2) + hbm(1),
        out_specs=vmem(2),
        out_shape=[
            jax.ShapeDtypeStruct((PEERS, ROWS, 128), bf16),
            jax.ShapeDtypeStruct((BLOCK, 2048), bf16),
        ],
        scratch_shapes=[
            pltpu.VMEM((BANDS, 2048), bf16),
            pltpu.VMEM((HALF * LINE, 128), f32),
            pltpu.VMEM((2 * BLOCK, 2048), bf16),
            pltpu.SemaphoreType.DMA((FETCHES,)),
        ],
        compiler_params=pltpu.CompilerParams(vmem_limit_bytes=20 << 20),
        name="intersect",
    )(search, extra, in_hbm(coeff))


def total_kernel(in_ref, out_ref):
    for r in range(8):
        at = slice(16 * r, 16 * r + 16)
        total = in_ref[0, at, :].astype(f32)
        for peer in range(1, PEERS):
            total = total + in_ref[peer, at, :].astype(f32)
        total = total.astype(bf16)
        for peer in range(PEERS):
            out_ref[peer, at, :] = total
    extra = in_ref[0, 128:, :].astype(f32)
    for peer in range(1, PEERS):
        extra = extra + in_ref[peer, 128:, :].astype(f32)
    high, middle, low = split_three(extra[0:1] + extra[1:2] + extra[2:3])
    row = iota((8, 128), 0)
    parts = jnp.where(row == 0, high.astype(f32), 0.0)
    parts = jnp.where(row == 1, middle.astype(f32), parts)
    parts = jnp.where(row == 2, low.astype(f32), parts).astype(bf16)
    for peer in range(PEERS):
        out_ref[peer, 128:, :] = parts


def totals_for_all(arrived):
    return pl.pallas_call(
        total_kernel,
        in_specs=vmem(1),
        out_specs=vmem(1)[0],
        out_shape=jax.ShapeDtypeStruct((PEERS, ROWS, 128), bf16),
        compiler_params=pltpu.CompilerParams(vmem_limit_bytes=6 << 20),
        name="total",
    )(arrived)


def wrap_offset(values):
    return ((values + G // 2) & (G - 1)) - G // 2


def row_of(ref, base, lane_wanted, peer_wanted):
    lane = iota((128, 256), 0)
    choose = jnp.where(lane == lane_wanted, 1.0, 0.0).astype(bf16)
    parts = ref[:, base : base + 8, :].astype(f32).reshape(PEERS * 8, 128).astype(bf16)
    here = jnp.where((iota((PEERS * 8, 256), 0) >> 3) == peer_wanted, dot(parts, choose), 0.0)
    return jnp.sum(here, 0, keepdims=True)


def prepare_kernel(
    image_ref, first_ref, pos_ref, before_ref, after_ref, start_ref, end_ref,
    ritz_ref, tangent_ref, spring_ref,
):
    column, at = iota((128, 256), 1), iota((PEERS * 8, 256), 1)
    ritz_ref[...] = row_of(
        first_ref, 128, 32 + OWN * (column // HALF) + column % OWN, at % HALF // OWN
    )
    pos = pos_ref[...]
    image = image_ref[0]
    before = jnp.where(image == 0, start_ref[...], before_ref[...])
    after = jnp.where(image == image_ref[1] - 1, end_ref[...], after_ref[...])
    ahead = wrap_offset(after - pos).astype(f32)
    behind = wrap_offset(pos - before).astype(f32)
    raw = ahead + behind
    entries = pos.shape[0] * pos.shape[1]

    def mean_square(value):
        return jnp.sum(jnp.sum(value * value, 1, keepdims=True), 0, keepdims=True) / entries

    tangent = raw * lax.rsqrt(mean_square(raw) + epsilon) * (1.0 / math.sqrt(entries))
    length_ahead = jnp.sqrt(entries * (mean_square(ahead) + epsilon))
    length_behind = jnp.sqrt(entries * (mean_square(behind) + epsilon))
    tangent_ref[...] = tangent
    spring_ref[...] = spring_constant * (length_ahead - length_behind) * tangent


def prepared(image, arrived, pos, before, after, start_pos, end_pos):
    return pl.pallas_call(
        prepare_kernel,
        in_specs=[pl.BlockSpec(memory_space=pltpu.SMEM)] + vmem(6),
        out_specs=vmem(3),
        out_shape=[
            jax.ShapeDtypeStruct((1, 256), f32),
            jax.ShapeDtypeStruct((3, 256), f32),
            jax.ShapeDtypeStruct((3, 256), f32),
        ],
        compiler_params=pltpu.CompilerParams(vmem_limit_bytes=6 << 20),
        name="prepare",
    )(image, arrived, pos, before, after, start_pos, end_pos)


def project_kernel(
    whole_ref, flat_ref, tangent_ref, spring_ref, coeff_hbm,
    out_hbm, push_ref, along_ref, coeff_ref, inter_ref, done_ref, sems, fetch_sems,
):
    wide = 2048 // FETCHES

    def fetch(k):
        at = pl.ds(k * wide, wide)
        return pltpu.make_async_copy(coeff_hbm.at[:, at], coeff_ref.at[:, at], fetch_sems.at[k])

    for k in range(FETCHES):
        fetch(k).start()
    lanes = 256
    chunks = 2048 // lanes
    for j in range(8):
        inter_ref[:, 128 * j : 128 * j + 128] = whole_ref[:, 16 * j : 16 * j + 16, :].reshape(
            2 * BLOCK, 128
        )
    first = (iota((BLOCK, 128), 1) & 63) < 32

    def send(k):
        at = pl.ds(k * lanes, lanes)
        return pltpu.make_async_copy(done_ref.at[:, at], out_hbm.at[:, at], sems.at[k])

    column, at = iota((128, 256), 1), iota((PEERS * 8, 256), 1)
    tangent = tangent_ref[...]
    force = jnp.concatenate(
        [row_of(whole_ref, 128, 8 * alpha + (column & 7), at >> 3) for alpha in range(3)], 0
    )
    along = jnp.sum(jnp.sum(force * tangent, 1, keepdims=True), 0, keepdims=True)
    push = force - along * tangent + spring_ref[...]
    for alpha in range(3):
        push_ref[alpha] = push[alpha : alpha + 1]
    along_ref[...] = along
    for k in range(chunks):
        if k * lanes % wide == 0:
            fetch(k * lanes // wide).wait()
        projected = dot(inter_ref[...], coeff_ref[:, k * lanes : (k + 1) * lanes])
        for j in range(lanes // 128):
            here = slice(128 * j, 128 * j + 128)
            at = slice(k * lanes + 128 * j, k * lanes + 128 * j + 128)
            turned = projected[BLOCK:, here]
            turned = jnp.where(first, -pltpu.roll(turned, 96, 1), pltpu.roll(turned, 32, 1))
            done_ref[:, at] = (
                flat_ref[:, at].astype(f32) - (projected[:BLOCK, here] + turned)
            ).astype(bf16)
        send(k).start()

    for k in range(chunks):
        send(k).wait()


def corrected(whole, flat, tangent, spring, coeff):
    return pl.pallas_call(
        project_kernel,
        in_specs=vmem(4) + hbm(1),
        out_specs=hbm(1) + vmem(2),
        out_shape=[
            pltpu.HBM((BLOCK, 2048), bf16),
            jax.ShapeDtypeStruct((3, 1, 256), f32),
            jax.ShapeDtypeStruct((1, 1), f32),
        ],
        scratch_shapes=[
            pltpu.VMEM((BANDS, 2048), bf16),
            pltpu.VMEM((2 * BLOCK, BANDS), bf16),
            pltpu.VMEM((BLOCK, 2048), bf16),
            pltpu.SemaphoreType.DMA((8,)),
            pltpu.SemaphoreType.DMA((FETCHES,)),
        ],
        compiler_params=pltpu.CompilerParams(vmem_limit_bytes=16 << 20),
        name="project",
    )(whole, flat, tangent, spring, in_hbm(coeff))


def exchanged(array):
    return lax.all_to_all(array, GRID_AXES, split_axis=0, concat_axis=0, tiled=True)


def passed_along(block, axis, distance):
    devices = range(lax.axis_size(axis))
    route = [(i - distance, i) for i in devices if i - distance in devices]
    return lax.ppermute(block, axis, route)


def body(coefficients, rotation, positions, start_pos, end_pos, species, depth):
    coeff = coefficients.reshape(BANDS, 2048)
    pos = positions[0]
    kinds = species.reshape(1, -1)
    orbitals, given = own_orbitals(
        rotation[0], coeff, depth, positions.transpose(1, 0, 2), kinds
    )
    vectors = exchanged(orbitals.reshape(PEERS, OWN * W, 128))
    potential = grid_potential(depth, pos, kinds, given)
    search, density, ritz = searched(vectors.reshape(W * OWN * W, 128), potential)
    own_search = exchanged(search.reshape(PEERS, OWN * W, 128))
    extra = force_parts(depth, density, pos, kinds, ritz)
    parts, flat = own_intersections(own_search.reshape(HALF * W, 128), coeff, extra)
    arrived = exchanged(parts)
    mine = totals_for_all(arrived)
    later = lax.optimization_barrier((pos, mine))[0]
    before = passed_along(later, "img", 1)
    after = passed_along(later, "img", -1)
    whole = exchanged(mine)
    image = jnp.stack([lax.axis_index("img"), lax.axis_size("img")]).astype(jnp.int32)
    arrived, before, after = lax.optimization_barrier((arrived, before, after, mine))[:3]
    ritz_values, tangent, spring = prepared(
        image, arrived, pos, before, after, start_pos, end_pos
    )
    correction, push, along = corrected(whole, flat, tangent, spring, coeff)
    return (
        correction.reshape(1, BLOCK, 1, 2048),
        ritz_values,
        push.transpose(1, 0, 2),
        along.reshape(1),
    )


def solution(mesh):
    in_specs = (
        P("img", None, GRID_AXES, None),
        P("img", None, None),
        P("img", None, None),
        P(),
        P(),
        P(),
        P(),
    )
    out_specs = (
        P("img", None, GRID_AXES, None),
        P("img", None),
        P("img", None, None),
        P("img"),
    )
    return jax.shard_map(body, mesh=mesh, in_specs=in_specs, out_specs=out_specs, check_vma=False)
```

```python
import math

import jax
import jax.numpy as jnp
import numpy as np
from jax import lax
from jax.experimental import pallas as pl
from jax.experimental.pallas import tpu as pltpu
from jax.sharding import PartitionSpec as P

G = 64
W = 32
BANDS = 1024
BLOCK = 256
SPECIES = 4
NPW = W * W * W
PEERS = 32
OWN = BLOCK // PEERS // 2
HALF = BLOCK // 2
PITCH = 2 * G + 1
GROUP = 32
MB = 16
SU = 1
ROWS = 136
CHUNKS = 2
FETCHES = 2
LINE = W + 1
SHARES = 8
EARLY = 4
EARLY_ROWS = G * G * EARLY // SHARES

kinetic_scale = 0.01
sigma_cells = 3.0
spring_constant = 2.0
epsilon = 1e-06

f32 = jnp.float32
bf16 = jnp.bfloat16
GRID_AXES = ("band", "pw")


def host_phases():
    turns = np.mod((np.arange(W) - W // 2)[:, None] * np.arange(G)[None, :], G)
    return turns.astype(np.float32) * np.float32(2.0 * math.pi / G)


def host_tables():
    angle = host_phases()
    cosine, sine = np.cos(angle), np.sin(angle)
    s = np.float32(1.0 / math.sqrt(W))
    fwd = np.stack([np.stack([cosine, sine], 1), np.stack([-sine, cosine], 1)], 0) * s
    t = np.float32(math.sqrt(W) / G)
    c2, s2 = cosine.T * t, sine.T * t
    inv = np.stack([np.stack([c2, -s2], 1), np.stack([s2, c2], 1)], 0)
    left = fwd.transpose(2, 3, 0, 1).reshape(2 * G, 2 * W)
    left_inv = inv.transpose(2, 3, 0, 1).reshape(2 * W, 2 * G)
    eye = np.eye(2, dtype=np.float32)
    z_fwd = np.einsum("cjdn,pq->pcjdqn", fwd, eye).reshape(4 * W, 4 * G)
    z_inv = np.einsum("dncj,pq->dpnqcj", inv, eye).reshape(4 * G, 4 * W)
    return [np.asarray(a, dtype=bf16) for a in (z_fwd, left, left_inv, z_inv)]


def split_two(value):
    high = value.astype(bf16)
    return high, (value - high.astype(f32)).astype(bf16)


def split_three(value):
    high = value.astype(bf16)
    rest = value - high.astype(f32)
    middle = rest.astype(bf16)
    return high, middle, (rest - middle.astype(f32)).astype(bf16)


def dot(a, b):
    return jnp.dot(a, b, preferred_element_type=f32)


def dot_nt(a, b):
    return lax.dot_general(a, b, (((1,), (1,)), ((), ())), preferred_element_type=f32)


def iota(shape, dim):
    return lax.broadcasted_iota(jnp.int32, shape, dim)


def orbitals_kernel(
    rot_hbm, coeff_hbm, depth_hbm, pos_hbm, species_hbm, out_hbm, pot_hbm,
    coeff_ref, rot_ref, turned_ref, wide_ref, out_ref, pot_ref, gy_ref, depth_ref, pos_ref,
    species_ref, sems, small_sems,
):
    lanes = 2048 // CHUNKS

    def fetch(k):
        at = pl.ds(k * lanes, lanes)
        return pltpu.make_async_copy(coeff_hbm.at[:, at], coeff_ref.at[:, at], sems.at[k])

    turned = pltpu.make_async_copy(rot_hbm, rot_ref, sems.at[CHUNKS])
    turned.start()
    for k in range(CHUNKS):
        fetch(k).start()
    ahead = pl.ds(0, EARLY_ROWS)
    keep = pltpu.make_async_copy(pot_ref.at[ahead], pot_hbm.at[ahead], small_sems.at[3])

    @pl.when(potential_first())
    def _():
        small = [
            pltpu.make_async_copy(source, target, small_sems.at[k])
            for k, (source, target) in enumerate(
                [(depth_hbm, depth_ref), (pos_hbm, pos_ref), (species_hbm, species_ref)]
            )
        ]
        for copy in small:
            copy.start()
        for copy in small:
            copy.wait()
        places = [pos_ref[k] for k in range(3)]
        write_potential(depth_ref, places, species_ref[...], pot_ref, gy_ref, 0, EARLY)
        keep.start()

    source, target = iota((256, 256), 0), iota((256, 256), 1)
    same = (source & 63) == (target & 63)
    same &= (source >> 7) == ((target >> 6) & 1)
    same &= ((source >> 6) & 1) == (target >> 7)
    pack = jnp.where(same, 1.0, 0.0).astype(bf16)
    turned.wait()
    turned_ref[...] = rot_ref[...].T
    for k in range(CHUNKS):
        fetch(k).wait()
        both = dot(turned_ref[...], coeff_ref[:, k * lanes : (k + 1) * lanes]).astype(bf16)
        for j in range(lanes // 128):
            at = slice(128 * j, 128 * j + 128)
            pair = jnp.concatenate([both[:HALF, at], both[HALF:, at]], 1)
            moved = dot(pair, pack)
            y = k * (lanes // 64) + 2 * j
            wide_ref[pl.ds(y, HALF, stride=LINE), :] = moved[:, :128]
            wide_ref[pl.ds(y + 1, HALF, stride=LINE), :] = moved[:, 128:]
    parts = 4
    rows = HALF * W // parts

    def send(k):
        at = pl.ds(k * rows, rows)
        return pltpu.make_async_copy(out_ref.at[at], out_hbm.at[at], sems.at[CHUNKS + 1 + k])

    for k in range(parts):
        for t in range(k * HALF // parts, (k + 1) * HALF // parts):
            out_ref[t * W : t * W + W, :] = wide_ref[t * LINE : t * LINE + W, :].astype(bf16)
        send(k).start()
    for k in range(parts):
        send(k).wait()

    @pl.when(potential_first())
    def _():
        keep.wait()


def own_orbitals(rotation, coeff, depth, places, species):
    return pl.pallas_call(
        orbitals_kernel,
        in_specs=hbm(5),
        out_specs=hbm(2),
        out_shape=[pltpu.HBM((HALF * W, 128), bf16), pltpu.HBM((G * G, 128), f32)],
        scratch_shapes=[
            pltpu.VMEM((BANDS, 2048), bf16),
            pltpu.VMEM((BANDS, BLOCK), bf16),
            pltpu.VMEM((BLOCK, BANDS), bf16),
            pltpu.VMEM((HALF * LINE, 128), f32),
            pltpu.VMEM((HALF * W, 128), bf16),
            pltpu.VMEM((G * G, 128), f32),
            pltpu.VMEM((G, 256), f32),
            pltpu.SMEM((SPECIES,), f32),
            pltpu.VMEM((3, 1, 256), jnp.int32),
            pltpu.VMEM((1, 256), jnp.int32),
            pltpu.SemaphoreType.DMA((CHUNKS + 5,)),
            pltpu.SemaphoreType.DMA((4,)),
        ],
        compiler_params=pltpu.CompilerParams(vmem_limit_bytes=20 << 20),
        name="orbitals",
    )(*[in_hbm(array) for array in (rotation, coeff, depth, places, species)])


def in_hbm(array):
    return pltpu.with_memory_space_constraint(array, pltpu.HBM)


def hbm(count):
    return [pl.BlockSpec(memory_space=pltpu.HBM)] * count


def vmem(count):
    return [pl.BlockSpec(memory_space=pltpu.VMEM)] * count


def gaussian(position, rows):
    cells = iota((rows, position.shape[1]), 0) & (G - 1)
    offset = (((cells - position + G // 2) & (G - 1)) - G // 2).astype(f32)
    return jnp.exp(-offset * offset / (2.0 * sigma_cells * sigma_cells)), offset


def strengths(species, depth_ref):
    strength = jnp.zeros(species.shape, f32)
    for kind in range(SPECIES):
        strength = jnp.where(species == kind, depth_ref[kind], strength)
    return strength


def write_potential(depth_ref, places, species, out_ref, gy_ref, begin, end):
    strength = strengths(species, depth_ref)
    gauss_x, _ = gaussian(places[0], G)
    gauss_x = gauss_x * strength
    gy_ref[...], _ = gaussian(places[1], G)
    gauss_z, _ = gaussian(places[2], 2 * G)
    z_high, z_low = split_two(gauss_z)
    per = G // SHARES

    def some(i, carry):
        for k in range(per):
            m = i * per + k
            value = gauss_x * gy_ref[pl.ds(m, 1), :]
            high, low = split_two(value)
            out_ref[pl.ds(pl.multiple_of(m * G, G), G), :] = (
                dot_nt(high, z_high) + dot_nt(high, z_low) + dot_nt(low, z_high)
            )
        return carry

    lax.fori_loop(begin, end, some, 0)


def potential_first():
    return lax.axis_index("img") % 2 == 0


def potential_kernel(depth_ref, pos_ref, species_ref, given_hbm, out_hbm, pot_ref, gy_ref, sem):
    del given_hbm
    first = potential_first()
    places = [pos_ref[k : k + 1, :] for k in range(3)]
    begin = jnp.where(first, EARLY, 0)
    write_potential(depth_ref, places, species_ref[...], pot_ref, gy_ref, begin, SHARES)
    ahead, late = pl.ds(0, EARLY_ROWS), pl.ds(EARLY_ROWS, G * G - EARLY_ROWS)
    keep_late = pltpu.make_async_copy(pot_ref.at[late], out_hbm.at[late], sem.at[0])
    keep_late.start()

    @pl.when(jnp.logical_not(first))
    def _():
        keep = pltpu.make_async_copy(pot_ref.at[ahead], out_hbm.at[ahead], sem.at[1])
        keep.start()
        keep.wait()

    keep_late.wait()


def grid_potential(depth, pos, species, given):
    return pl.pallas_call(
        potential_kernel,
        in_specs=[pl.BlockSpec(memory_space=pltpu.SMEM)] + vmem(2) + hbm(1),
        out_specs=hbm(1)[0],
        out_shape=pltpu.HBM((G * G, 128), f32),
        input_output_aliases={3: 0},
        scratch_shapes=[
            pltpu.VMEM((G * G, 128), f32),
            pltpu.VMEM((G, 256), f32),
            pltpu.SemaphoreType.DMA((2,)),
        ],
        compiler_params=pltpu.CompilerParams(vmem_limit_bytes=12 << 20),
        name="potential",
    )(depth, pos, species, in_hbm(given))


def transform_kernel(
    orb_ref, zf_ref, left_ref, left_inv_ref, zi_ref, pot_hbm,
    out_hbm, dens_hbm, ritz_ref,
    pot_ref, mid_ref, ham_ref, num_ref, den_ref, dens_ref, out_ref, sems,
):
    bring = pltpu.make_async_copy(pot_hbm, pot_ref, sems.at[5])
    bring.start()
    group = GROUP
    rows = group * OWN * W

    def forward(i, carry):
        x = i * group
        zin = orb_ref[pl.ds(pl.multiple_of(x * OWN * W, rows), rows), :]
        along_z = dot(zin, zf_ref[...]).astype(bf16)
        parts = []
        for g in range(group * OWN):
            piece = along_z[W * g : W * g + W]
            parts.append(jnp.concatenate([piece[:, :128], piece[:, 128:]], 0))
        along_y = dot(left_ref[...], jnp.concatenate(parts, 1))
        for g in range(group * OWN):
            xx, tt = x + g // OWN, g % OWN
            at = (tt * W + xx) * PITCH
            mid_ref[pl.ds(at, 2 * G), :] = along_y[:, 128 * g : 128 * g + 128]
        return carry

    lax.fori_loop(0, W // group, forward, 0)

    bring.wait()

    def space(i, carry):
        parts = []
        for k in range(MB * OWN):
            base = (k % OWN) * W * PITCH + i * MB + k // OWN
            parts.append(
                jnp.concatenate(
                    [mid_ref[pl.ds(base + c * G, W, stride=PITCH), :] for c in range(2)], 0
                ).astype(bf16)
            )
        in_space = dot(left_ref[...], jnp.concatenate(parts, 1))
        weighted = []
        for mm in range(MB):
            at = pl.multiple_of((i * MB + mm) * G, G)
            potential = pot_ref[pl.ds(at, G), :]
            potential = jnp.concatenate([potential, potential], 0)
            density = jnp.zeros((2 * G, 128), f32)
            for tt in range(OWN):
                k = mm * OWN + tt
                one = in_space[:, 128 * k : 128 * k + 128]
                density = density + one * one
                weighted.append((one * potential).astype(bf16))
            dens_ref[pl.ds(at, G), :] = (density[:G] + density[G:]) * (1.0 / BLOCK)
        back = dot(left_inv_ref[...], jnp.concatenate(weighted, 1))
        for k in range(MB * OWN):
            base = (k % OWN) * W * PITCH + i * MB + k // OWN
            for c in range(2):
                mid_ref[pl.ds(base + c * G, W, stride=PITCH), :] = back[
                    W * c : W * c + W, 128 * k : 128 * k + 128
                ]
        return carry

    lax.fori_loop(0, G // MB, space, 0, unroll=SU)
    keep = pltpu.make_async_copy(dens_ref, dens_hbm, sems.at[4])
    keep.start()

    lane = iota((W, 128), 1)
    wave_y = iota((W, 128), 0) - W // 2
    wave_z = (lane & (W - 1)) - W // 2
    plane = wave_y * wave_y + wave_z * wave_z

    def kinetic(x):
        wave_x = x - W // 2
        return (kinetic_scale * 0.5) * (plane + wave_x * wave_x).astype(f32)

    num_ref[...] = jnp.zeros_like(num_ref)
    den_ref[...] = jnp.zeros_like(den_ref)

    def backward(i, carry):
        x = i * group
        parts = []
        for g in range(group * OWN):
            xx, tt = x + g // OWN, g % OWN
            at = (tt * W + xx) * PITCH
            parts.append(mid_ref[pl.ds(at, 2 * G), :].astype(bf16))
        back_y = dot(left_inv_ref[...], jnp.concatenate(parts, 1)).astype(bf16)
        parts = []
        for g in range(group * OWN):
            piece = back_y[:, 128 * g : 128 * g + 128]
            parts.append(jnp.concatenate([piece[:W], piece[W:]], 1))
        local = dot(jnp.concatenate(parts, 0), zi_ref[...])
        for g in range(group * OWN):
            xx, tt = x + g // OWN, g % OWN
            at = pl.multiple_of((xx * OWN + tt) * W, W)
            orbital = orb_ref[pl.ds(at, W), :].astype(f32)
            ham = kinetic(xx) * orbital + local[W * g : W * g + W]
            ham_ref[pl.ds(at, W), :] = ham
            num_ref[pl.ds(tt * W, W), :] += orbital * ham
            den_ref[pl.ds(tt * W, W), :] += orbital * orbital
        return carry

    lax.fori_loop(0, W // group, backward, 0)

    lane_row = iota((1, 128), 1)
    low = lane_row < 64
    ritz_row = jnp.zeros((1, 128), f32)
    ritz = []
    for tt in range(OWN):
        halves = []
        num = jnp.sum(num_ref[pl.ds(tt * W, W), :], 0, keepdims=True)
        den = jnp.sum(den_ref[pl.ds(tt * W, W), :], 0, keepdims=True)
        for p in range(2):
            mine = low if p == 0 else jnp.logical_not(low)
            top = jnp.sum(jnp.where(mine, num, 0.0), 1, keepdims=True)
            bottom = jnp.sum(jnp.where(mine, den, 0.0), 1, keepdims=True)
            value = (top / NPW) / (bottom / NPW + epsilon)
            halves.append(value)
            ritz_row = jnp.where(lane_row == 32 + p * OWN + tt, value, ritz_row)
        ritz.append(jnp.where(low, halves[0], halves[1]))
    ritz_ref[...] = jnp.broadcast_to(ritz_row, (8, 128))

    parts = 4
    rows = W * OWN * W // parts

    def send(k):
        at = pl.ds(k * rows, rows)
        return pltpu.make_async_copy(out_ref.at[at], out_hbm.at[at], sems.at[k])

    for x in range(W):
        kin = kinetic(x)
        scale = 1.0 / (1.0 + kin)
        for tt in range(OWN):
            at = pl.ds((x * OWN + tt) * W, W)
            orbital = orb_ref[at, :].astype(f32)
            residual = ham_ref[at, :] - ritz[tt] * orbital
            out_ref[at, :] = (residual * scale).astype(bf16)
        if (x + 1) % (W // parts) == 0:
            send(x // (W // parts)).start()
    for k in range(parts):
        send(k).wait()
    keep.wait()


def searched(orbitals, potential):
    z_fwd, left, left_inv, z_inv = host_tables()
    return pl.pallas_call(
        transform_kernel,
        in_specs=vmem(5) + hbm(1),
        out_specs=hbm(2) + vmem(1),
        out_shape=[
            pltpu.HBM((W * OWN * W, 128), bf16),
            pltpu.HBM((G * G, 128), f32),
            jax.ShapeDtypeStruct((8, 128), f32),
        ],
        scratch_shapes=[
            pltpu.VMEM((G * G, 128), f32),
            pltpu.VMEM((OWN * W * PITCH, 128), f32),
            pltpu.VMEM((W * OWN * W, 128), f32),
            pltpu.VMEM((OWN * W, 128), f32),
            pltpu.VMEM((OWN * W, 128), f32),
            pltpu.VMEM((G * G, 128), f32),
            pltpu.VMEM((W * OWN * W, 128), bf16),
            pltpu.SemaphoreType.DMA((6,)),
        ],
        compiler_params=pltpu.CompilerParams(vmem_limit_bytes=30 << 20),
        name="transform",
    )(orbitals, z_fwd, left, left_inv, z_inv, in_hbm(potential))


def force_kernel(
    depth_ref, dens_ref, pos_ref, species_ref, ritz_ref, out_ref, gy_ref, gyo_ref, wide_ref
):
    strength = strengths(species_ref[...], depth_ref)
    gauss_x, offset_x = gaussian(pos_ref[0:1, :], G)
    gauss_y, offset_y = gaussian(pos_ref[1:2, :], G)
    gauss_z, offset_z = gaussian(pos_ref[2:3, :], 2 * G)
    gy_ref[...] = gauss_y
    gyo_ref[...] = gauss_y * offset_y
    high, low = split_two(jnp.concatenate([gauss_z, gauss_z * offset_z], 1))
    both = jnp.concatenate([high, low], 0)
    per = 4

    def some(i, carry):
        sum_x, sum_y, sum_z = carry
        at = pl.multiple_of(i * per * G, per * G)
        d_high, d_low = split_two(dens_ref[pl.ds(at, per * G), :])
        moments = dot(jnp.concatenate([d_high, d_high], 1), both) + dot(d_low, high)
        for k in range(per):
            gy = gy_ref[pl.ds(i * per + k, 1), :]
            gyo = gyo_ref[pl.ds(i * per + k, 1), :]
            plain = moments[G * k : G * k + G, :256]
            sum_x = sum_x + plain * gy
            sum_y = sum_y + plain * gyo
            sum_z = sum_z + moments[G * k : G * k + G, 256:] * gy
        return sum_x, sum_y, sum_z

    zero = jnp.zeros((G, 256), f32)
    sum_x, sum_y, sum_z = lax.fori_loop(0, G // per, some, (zero, zero, zero))
    factor = -strength / (sigma_cells * sigma_cells)
    force = [
        factor * jnp.sum(gauss_x * offset_x * sum_x, 0, keepdims=True),
        factor * jnp.sum(gauss_x * sum_y, 0, keepdims=True),
        factor * jnp.sum(gauss_x * sum_z, 0, keepdims=True),
    ]
    peer, atom = iota((PEERS, 256), 0), iota((PEERS, 256), 1)
    from_atom, lane = iota((256, 128), 0), iota((256, 128), 1)
    parts = [part.astype(f32) for part in split_three(ritz_ref[0:1, :])]
    totals = [jnp.broadcast_to(part, (PEERS, 128)) for part in parts]
    for alpha in range(3):
        own = jnp.where(atom // 8 == peer, force[alpha], 0.0)
        choose = jnp.where((from_atom & 7) + 8 * alpha == lane, 1.0, 0.0).astype(bf16)
        for k, part in enumerate(split_three(own)):
            totals[k] = totals[k] + dot(part, choose)
    wide_ref[...] = jnp.zeros_like(wide_ref)
    for k in range(3):
        wide_ref[pl.ds(k, PEERS, stride=8), :] = totals[k]
    out_ref[...] = wide_ref[...].reshape(PEERS, 8, 128).astype(bf16)


def force_parts(depth, density, pos, species, ritz):
    return pl.pallas_call(
        force_kernel,
        in_specs=[pl.BlockSpec(memory_space=pltpu.SMEM)] + vmem(4),
        out_specs=vmem(1)[0],
        out_shape=jax.ShapeDtypeStruct((PEERS, 8, 128), bf16),
        scratch_shapes=[
            pltpu.VMEM((G, 256), f32),
            pltpu.VMEM((G, 256), f32),
            pltpu.VMEM((PEERS * 8, 128), f32),
        ],
        compiler_params=pltpu.CompilerParams(vmem_limit_bytes=10 << 20),
        name="force",
    )(depth, density, pos, species, ritz)


def intersect_kernel(
    search_ref, extra_ref, coeff_hbm, out_ref, flat_ref,
    coeff_ref, wide_ref, pair_ref, sems,
):
    bands = BANDS // FETCHES

    def fetch(k):
        at = pl.ds(k * bands, bands)
        return pltpu.make_async_copy(coeff_hbm.at[at], coeff_ref.at[at], sems.at[k])

    for k in range(FETCHES):
        fetch(k).start()
    source, target = iota((256, 512), 0), iota((256, 512), 1)
    part, element = target >> 7, target & 63
    turned = part >> 1
    same = (source & 63) == (element ^ (turned * 32))
    same &= (source >> 7) == ((target >> 6) & 1)
    same &= ((source >> 6) & 1) == (part & 1)
    sign = jnp.where((turned == 1) & (element >= 32), -1.0, 1.0)
    unpack = jnp.where(same, sign, 0.0).astype(bf16)
    for t in range(HALF):
        wide_ref[t * LINE : t * LINE + W, :] = search_ref[t * W : t * W + W, :].astype(f32)
    out_ref[:, 128:, :] = extra_ref[...]
    for j in range(W // 2):
        even = wide_ref[pl.ds(2 * j, HALF, stride=LINE), :]
        odd = wide_ref[pl.ds(2 * j + 1, HALF, stride=LINE), :]
        moved = dot(jnp.concatenate([even, odd], 1).astype(bf16), unpack).astype(bf16)
        at = slice(128 * j, 128 * j + 128)
        for q in range(4):
            piece = moved[:, 128 * q : 128 * q + 128]
            pair_ref[HALF * q : HALF * q + HALF, at] = piece
            if q < 2:
                flat_ref[HALF * q : HALF * q + HALF, at] = piece
    for k in range(FETCHES):
        fetch(k).wait()
        part = dot_nt(pair_ref[...], coeff_ref[bands * k : bands * k + bands, :])
        part = (part * (1.0 / NPW)).astype(bf16)
        for j in range(bands // 128):
            at = 16 * (k * bands // 128 + j)
            out_ref[:, at : at + 16, :] = part[:, 128 * j : 128 * j + 128].reshape(PEERS, 16, 128)


def own_intersections(search, coeff, extra):
    return pl.pallas_call(
        intersect_kernel,
        in_specs=vmem(2) + hbm(1),
        out_specs=vmem(2),
        out_shape=[
            jax.ShapeDtypeStruct((PEERS, ROWS, 128), bf16),
            jax.ShapeDtypeStruct((BLOCK, 2048), bf16),
        ],
        scratch_shapes=[
            pltpu.VMEM((BANDS, 2048), bf16),
            pltpu.VMEM((HALF * LINE, 128), f32),
            pltpu.VMEM((2 * BLOCK, 2048), bf16),
            pltpu.SemaphoreType.DMA((FETCHES,)),
        ],
        compiler_params=pltpu.CompilerParams(vmem_limit_bytes=20 << 20),
        name="intersect",
    )(search, extra, in_hbm(coeff))


def total_kernel(in_ref, out_ref):
    for r in range(8):
        at = slice(16 * r, 16 * r + 16)
        total = in_ref[0, at, :].astype(f32)
        for peer in range(1, PEERS):
            total = total + in_ref[peer, at, :].astype(f32)
        total = total.astype(bf16)
        for peer in range(PEERS):
            out_ref[peer, at, :] = total
    extra = in_ref[0, 128:, :].astype(f32)
    for peer in range(1, PEERS):
        extra = extra + in_ref[peer, 128:, :].astype(f32)
    high, middle, low = split_three(extra[0:1] + extra[1:2] + extra[2:3])
    row = iota((8, 128), 0)
    parts = jnp.where(row == 0, high.astype(f32), 0.0)
    parts = jnp.where(row == 1, middle.astype(f32), parts)
    parts = jnp.where(row == 2, low.astype(f32), parts).astype(bf16)
    for peer in range(PEERS):
        out_ref[peer, 128:, :] = parts


def totals_for_all(arrived):
    return pl.pallas_call(
        total_kernel,
        in_specs=vmem(1),
        out_specs=vmem(1)[0],
        out_shape=jax.ShapeDtypeStruct((PEERS, ROWS, 128), bf16),
        compiler_params=pltpu.CompilerParams(vmem_limit_bytes=6 << 20),
        name="total",
    )(arrived)


def wrap_offset(values):
    return ((values + G // 2) & (G - 1)) - G // 2


def row_of(ref, base, lane_wanted, peer_wanted):
    lane = iota((128, 256), 0)
    choose = jnp.where(lane == lane_wanted, 1.0, 0.0).astype(bf16)
    parts = ref[:, base : base + 8, :].astype(f32).reshape(PEERS * 8, 128).astype(bf16)
    here = jnp.where((iota((PEERS * 8, 256), 0) >> 3) == peer_wanted, dot(parts, choose), 0.0)
    return jnp.sum(here, 0, keepdims=True)


def prepare_kernel(first_ref, order_ref, ritz_ref):
    del order_ref
    column, at = iota((128, 256), 1), iota((PEERS * 8, 256), 1)
    ritz_ref[...] = row_of(
        first_ref, 128, 32 + OWN * (column // HALF) + column % OWN, at % HALF // OWN
    )


def prepared(arrived, order):
    return pl.pallas_call(
        prepare_kernel,
        in_specs=vmem(1) + hbm(1),
        out_specs=vmem(1)[0],
        out_shape=jax.ShapeDtypeStruct((1, 256), f32),
        compiler_params=pltpu.CompilerParams(vmem_limit_bytes=6 << 20),
        name="prepare",
    )(arrived, in_hbm(order))


def project_kernel(
    image_ref, whole_ref, flat_ref, pos_ref, before_ref, after_ref, start_ref, end_ref, coeff_hbm,
    out_hbm, push_ref, along_ref, coeff_ref, inter_ref, done_ref, sems, fetch_sems,
):
    wide = 2048 // FETCHES

    def fetch(k):
        at = pl.ds(k * wide, wide)
        return pltpu.make_async_copy(coeff_hbm.at[:, at], coeff_ref.at[:, at], fetch_sems.at[k])

    for k in range(FETCHES):
        fetch(k).start()
    lanes = 256
    chunks = 2048 // lanes
    for j in range(8):
        inter_ref[:, 128 * j : 128 * j + 128] = whole_ref[:, 16 * j : 16 * j + 16, :].reshape(
            2 * BLOCK, 128
        )
    first = (iota((BLOCK, 128), 1) & 63) < 32

    def send(k):
        at = pl.ds(k * lanes, lanes)
        return pltpu.make_async_copy(done_ref.at[:, at], out_hbm.at[:, at], sems.at[k])

    column, at = iota((128, 256), 1), iota((PEERS * 8, 256), 1)
    pos = pos_ref[...]
    image = image_ref[0]
    before = jnp.where(image == 0, start_ref[...], before_ref[...])
    after = jnp.where(image == image_ref[1] - 1, end_ref[...], after_ref[...])
    ahead = wrap_offset(after - pos).astype(f32)
    behind = wrap_offset(pos - before).astype(f32)
    raw = ahead + behind
    entries = pos.shape[0] * pos.shape[1]

    def mean_square(value):
        return jnp.sum(jnp.sum(value * value, 1, keepdims=True), 0, keepdims=True) / entries

    tangent = raw * lax.rsqrt(mean_square(raw) + epsilon) * (1.0 / math.sqrt(entries))
    length_ahead = jnp.sqrt(entries * (mean_square(ahead) + epsilon))
    length_behind = jnp.sqrt(entries * (mean_square(behind) + epsilon))
    spring = spring_constant * (length_ahead - length_behind) * tangent
    force = jnp.concatenate(
        [row_of(whole_ref, 128, 8 * alpha + (column & 7), at >> 3) for alpha in range(3)], 0
    )
    along = jnp.sum(jnp.sum(force * tangent, 1, keepdims=True), 0, keepdims=True)
    push = force - along * tangent + spring
    for alpha in range(3):
        push_ref[alpha] = push[alpha : alpha + 1]
    along_ref[...] = along
    for k in range(chunks):
        if k * lanes % wide == 0:
            fetch(k * lanes // wide).wait()
        projected = dot(inter_ref[...], coeff_ref[:, k * lanes : (k + 1) * lanes])
        for j in range(lanes // 128):
            here = slice(128 * j, 128 * j + 128)
            at = slice(k * lanes + 128 * j, k * lanes + 128 * j + 128)
            turned = projected[BLOCK:, here]
            turned = jnp.where(first, -pltpu.roll(turned, 96, 1), pltpu.roll(turned, 32, 1))
            done_ref[:, at] = (
                flat_ref[:, at].astype(f32) - (projected[:BLOCK, here] + turned)
            ).astype(bf16)
        send(k).start()

    for k in range(chunks):
        send(k).wait()


def corrected(image, whole, flat, pos, before, after, start_pos, end_pos, coeff):
    return pl.pallas_call(
        project_kernel,
        in_specs=[pl.BlockSpec(memory_space=pltpu.SMEM)] + vmem(7) + hbm(1),
        out_specs=hbm(1) + vmem(2),
        out_shape=[
            pltpu.HBM((BLOCK, 2048), bf16),
            jax.ShapeDtypeStruct((3, 1, 256), f32),
            jax.ShapeDtypeStruct((1, 1), f32),
        ],
        scratch_shapes=[
            pltpu.VMEM((BANDS, 2048), bf16),
            pltpu.VMEM((2 * BLOCK, BANDS), bf16),
            pltpu.VMEM((BLOCK, 2048), bf16),
            pltpu.SemaphoreType.DMA((8,)),
            pltpu.SemaphoreType.DMA((FETCHES,)),
        ],
        compiler_params=pltpu.CompilerParams(vmem_limit_bytes=16 << 20),
        name="project",
    )(image, whole, flat, pos, before, after, start_pos, end_pos, in_hbm(coeff))


def exchanged(array):
    return lax.all_to_all(array, GRID_AXES, split_axis=0, concat_axis=0, tiled=True)


def passed_along(block, axis, distance):
    devices = range(lax.axis_size(axis))
    route = [(i - distance, i) for i in devices if i - distance in devices]
    return lax.ppermute(block, axis, route)


def body(coefficients, rotation, positions, start_pos, end_pos, species, depth):
    coeff = coefficients.reshape(BANDS, 2048)
    pos = positions[0]
    kinds = species.reshape(1, -1)
    orbitals, given = own_orbitals(
        rotation[0], coeff, depth, positions.transpose(1, 0, 2), kinds
    )
    vectors = exchanged(orbitals.reshape(PEERS, OWN * W, 128))
    potential = grid_potential(depth, pos, kinds, given)
    search, density, ritz = searched(vectors.reshape(W * OWN * W, 128), potential)
    own_search = exchanged(search.reshape(PEERS, OWN * W, 128))
    extra = force_parts(depth, density, pos, kinds, ritz)
    parts, flat = own_intersections(own_search.reshape(HALF * W, 128), coeff, extra)
    arrived = exchanged(parts)
    mine = totals_for_all(arrived)
    later = lax.optimization_barrier((pos, mine))[0]
    before = passed_along(later, "img", 1)
    after = passed_along(later, "img", -1)
    whole = exchanged(mine)
    image = jnp.stack([lax.axis_index("img"), lax.axis_size("img")]).astype(jnp.int32)
    ritz_values = prepared(arrived, mine)
    correction, push, along = corrected(
        image, whole, flat, pos, before, after, start_pos, end_pos, coeff
    )
    return (
        correction.reshape(1, BLOCK, 1, 2048),
        ritz_values,
        push.transpose(1, 0, 2),
        along.reshape(1),
    )


def solution(mesh):
    in_specs = (
        P("img", None, GRID_AXES, None),
        P("img", None, None),
        P("img", None, None),
        P(),
        P(),
        P(),
        P(),
    )
    out_specs = (
        P("img", None, GRID_AXES, None),
        P("img", None),
        P("img", None, None),
        P("img"),
    )
    return jax.shard_map(body, mesh=mesh, in_specs=in_specs, out_specs=out_specs, check_vma=False)
```

```python
import math

import jax
import jax.numpy as jnp
import numpy as np
from jax import lax
from jax.experimental import pallas as pl
from jax.experimental.pallas import tpu as pltpu
from jax.sharding import PartitionSpec as P

G = 64
W = 32
BANDS = 1024
BLOCK = 256
SPECIES = 4
NPW = W * W * W
PEERS = 32
OWN = BLOCK // PEERS // 2
HALF = BLOCK // 2
PITCH = 2 * G + 1
GROUP = 32
MB = 16
SU = 1
ROWS = 136
CHUNKS = 2
FETCHES = 2
LINE = W + 1
NEAR = 512
SHARES = 8
EARLY = 4
EARLY_ROWS = G * G * EARLY // SHARES

kinetic_scale = 0.01
sigma_cells = 3.0
spring_constant = 2.0
epsilon = 1e-06

f32 = jnp.float32
bf16 = jnp.bfloat16
GRID_AXES = ("band", "pw")


def host_phases():
    turns = np.mod((np.arange(W) - W // 2)[:, None] * np.arange(G)[None, :], G)
    return turns.astype(np.float32) * np.float32(2.0 * math.pi / G)


def host_tables():
    angle = host_phases()
    cosine, sine = np.cos(angle), np.sin(angle)
    s = np.float32(1.0 / math.sqrt(W))
    fwd = np.stack([np.stack([cosine, sine], 1), np.stack([-sine, cosine], 1)], 0) * s
    t = np.float32(math.sqrt(W) / G)
    c2, s2 = cosine.T * t, sine.T * t
    inv = np.stack([np.stack([c2, -s2], 1), np.stack([s2, c2], 1)], 0)
    left = fwd.transpose(2, 3, 0, 1).reshape(2 * G, 2 * W)
    left_inv = inv.transpose(2, 3, 0, 1).reshape(2 * W, 2 * G)
    eye = np.eye(2, dtype=np.float32)
    z_fwd = np.einsum("cjdn,pq->pcjdqn", fwd, eye).reshape(4 * W, 4 * G)
    z_inv = np.einsum("dncj,pq->dpnqcj", inv, eye).reshape(4 * G, 4 * W)
    return [np.asarray(a, dtype=bf16) for a in (z_fwd, left, left_inv, z_inv)]


def split_two(value):
    high = value.astype(bf16)
    return high, (value - high.astype(f32)).astype(bf16)


def split_three(value):
    high = value.astype(bf16)
    rest = value - high.astype(f32)
    middle = rest.astype(bf16)
    return high, middle, (rest - middle.astype(f32)).astype(bf16)


def dot(a, b):
    return jnp.dot(a, b, preferred_element_type=f32)


def dot_nt(a, b):
    return lax.dot_general(a, b, (((1,), (1,)), ((), ())), preferred_element_type=f32)


def iota(shape, dim):
    return lax.broadcasted_iota(jnp.int32, shape, dim)


def orbitals_kernel(
    rot_hbm, coeff_hbm, depth_hbm, pos_hbm, species_hbm, out_hbm, pot_hbm,
    coeff_ref, rot_ref, turned_ref, wide_ref, out_ref, pot_ref, gy_ref, depth_ref, pos_ref,
    species_ref, sems, small_sems,
):
    lanes = 2048 // CHUNKS

    def fetch(k):
        at = pl.ds(k * lanes, lanes)
        return pltpu.make_async_copy(coeff_hbm.at[:, at], coeff_ref.at[:, at], sems.at[k])

    turned = pltpu.make_async_copy(rot_hbm, rot_ref, sems.at[CHUNKS])
    turned.start()
    for k in range(CHUNKS):
        fetch(k).start()
    ahead = pl.ds(0, EARLY_ROWS)
    keep = pltpu.make_async_copy(pot_ref.at[ahead], pot_hbm.at[ahead], small_sems.at[3])

    @pl.when(potential_first())
    def _():
        small = [
            pltpu.make_async_copy(source, target, small_sems.at[k])
            for k, (source, target) in enumerate(
                [(depth_hbm, depth_ref), (pos_hbm, pos_ref), (species_hbm, species_ref)]
            )
        ]
        for copy in small:
            copy.start()
        for copy in small:
            copy.wait()
        places = [pos_ref[k] for k in range(3)]
        write_potential(depth_ref, places, species_ref[...], pot_ref, gy_ref, 0, EARLY)
        keep.start()

    source, target = iota((256, 256), 0), iota((256, 256), 1)
    same = (source & 63) == (target & 63)
    same &= (source >> 7) == ((target >> 6) & 1)
    same &= ((source >> 6) & 1) == (target >> 7)
    pack = jnp.where(same, 1.0, 0.0).astype(bf16)
    turned.wait()
    turned_ref[...] = rot_ref[...].T
    for k in range(CHUNKS):
        fetch(k).wait()
        both = dot(turned_ref[...], coeff_ref[:, k * lanes : (k + 1) * lanes]).astype(bf16)
        for j in range(lanes // 128):
            at = slice(128 * j, 128 * j + 128)
            pair = jnp.concatenate([both[:HALF, at], both[HALF:, at]], 1)
            moved = dot(pair, pack)
            y = k * (lanes // 64) + 2 * j
            wide_ref[pl.ds(y, HALF, stride=LINE), :] = moved[:, :128]
            wide_ref[pl.ds(y + 1, HALF, stride=LINE), :] = moved[:, 128:]
    parts = 4
    rows = HALF * W // parts

    def send(k):
        at = pl.ds(k * rows, rows)
        return pltpu.make_async_copy(out_ref.at[at], out_hbm.at[at], sems.at[CHUNKS + 1 + k])

    for k in range(parts):
        for t in range(k * HALF // parts, (k + 1) * HALF // parts):
            out_ref[t * W : t * W + W, :] = wide_ref[t * LINE : t * LINE + W, :].astype(bf16)
        send(k).start()
    for k in range(parts):
        send(k).wait()

    @pl.when(potential_first())
    def _():
        keep.wait()


def own_orbitals(rotation, coeff, depth, places, species):
    return pl.pallas_call(
        orbitals_kernel,
        in_specs=hbm(5),
        out_specs=hbm(2),
        out_shape=[pltpu.HBM((HALF * W, 128), bf16), pltpu.HBM((G * G, 128), f32)],
        scratch_shapes=[
            pltpu.VMEM((BANDS, 2048), bf16),
            pltpu.VMEM((BANDS, BLOCK), bf16),
            pltpu.VMEM((BLOCK, BANDS), bf16),
            pltpu.VMEM((HALF * LINE, 128), f32),
            pltpu.VMEM((HALF * W, 128), bf16),
            pltpu.VMEM((G * G, 128), f32),
            pltpu.VMEM((G, 256), f32),
            pltpu.SMEM((SPECIES,), f32),
            pltpu.VMEM((3, 1, 256), jnp.int32),
            pltpu.VMEM((1, 256), jnp.int32),
            pltpu.SemaphoreType.DMA((CHUNKS + 5,)),
            pltpu.SemaphoreType.DMA((4,)),
        ],
        compiler_params=pltpu.CompilerParams(vmem_limit_bytes=20 << 20),
        name="orbitals",
    )(*[in_hbm(array) for array in (rotation, coeff, depth, places, species)])


def in_hbm(array):
    return pltpu.with_memory_space_constraint(array, pltpu.HBM)


def near_kernel(coeff_hbm, order_hbm, out_ref, sem):
    del order_hbm
    fetch = pltpu.make_async_copy(coeff_hbm.at[:, pl.ds(0, NEAR)], out_ref, sem)
    fetch.start()
    fetch.wait()


def brought_near(coeff, order):
    return pl.pallas_call(
        near_kernel,
        in_specs=hbm(2),
        out_specs=vmem(1)[0],
        out_shape=jax.ShapeDtypeStruct((BANDS, NEAR), bf16),
        scratch_shapes=[pltpu.SemaphoreType.DMA],
        compiler_params=pltpu.CompilerParams(vmem_limit_bytes=1 << 20),
        name="near",
    )(in_hbm(coeff), in_hbm(order))


def hbm(count):
    return [pl.BlockSpec(memory_space=pltpu.HBM)] * count


def vmem(count):
    return [pl.BlockSpec(memory_space=pltpu.VMEM)] * count


def gaussian(position, rows):
    cells = iota((rows, position.shape[1]), 0) & (G - 1)
    offset = (((cells - position + G // 2) & (G - 1)) - G // 2).astype(f32)
    return jnp.exp(-offset * offset / (2.0 * sigma_cells * sigma_cells)), offset


def strengths(species, depth_ref):
    strength = jnp.zeros(species.shape, f32)
    for kind in range(SPECIES):
        strength = jnp.where(species == kind, depth_ref[kind], strength)
    return strength


def write_potential(depth_ref, places, species, out_ref, gy_ref, begin, end):
    strength = strengths(species, depth_ref)
    gauss_x, _ = gaussian(places[0], G)
    gauss_x = gauss_x * strength
    gy_ref[...], _ = gaussian(places[1], G)
    gauss_z, _ = gaussian(places[2], 2 * G)
    z_high, z_low = split_two(gauss_z)
    per = G // SHARES

    def some(i, carry):
        for k in range(per):
            m = i * per + k
            value = gauss_x * gy_ref[pl.ds(m, 1), :]
            high, low = split_two(value)
            out_ref[pl.ds(pl.multiple_of(m * G, G), G), :] = (
                dot_nt(high, z_high) + dot_nt(high, z_low) + dot_nt(low, z_high)
            )
        return carry

    lax.fori_loop(begin, end, some, 0)


def potential_first():
    return lax.axis_index("img") % 2 == 0


def potential_kernel(depth_ref, pos_ref, species_ref, given_hbm, out_hbm, pot_ref, gy_ref, sem):
    del given_hbm
    first = potential_first()
    places = [pos_ref[k : k + 1, :] for k in range(3)]
    begin = jnp.where(first, EARLY, 0)
    write_potential(depth_ref, places, species_ref[...], pot_ref, gy_ref, begin, SHARES)
    ahead, late = pl.ds(0, EARLY_ROWS), pl.ds(EARLY_ROWS, G * G - EARLY_ROWS)
    keep_late = pltpu.make_async_copy(pot_ref.at[late], out_hbm.at[late], sem.at[0])
    keep_late.start()

    @pl.when(jnp.logical_not(first))
    def _():
        keep = pltpu.make_async_copy(pot_ref.at[ahead], out_hbm.at[ahead], sem.at[1])
        keep.start()
        keep.wait()

    keep_late.wait()


def grid_potential(depth, pos, species, given):
    return pl.pallas_call(
        potential_kernel,
        in_specs=[pl.BlockSpec(memory_space=pltpu.SMEM)] + vmem(2) + hbm(1),
        out_specs=hbm(1)[0],
        out_shape=pltpu.HBM((G * G, 128), f32),
        input_output_aliases={3: 0},
        scratch_shapes=[
            pltpu.VMEM((G * G, 128), f32),
            pltpu.VMEM((G, 256), f32),
            pltpu.SemaphoreType.DMA((2,)),
        ],
        compiler_params=pltpu.CompilerParams(vmem_limit_bytes=12 << 20),
        name="potential",
    )(depth, pos, species, in_hbm(given))


def transform_kernel(
    orb_ref, zf_ref, left_ref, left_inv_ref, zi_ref, pot_hbm,
    out_hbm, dens_hbm, ritz_ref,
    pot_ref, mid_ref, ham_ref, num_ref, den_ref, dens_ref, out_ref, sems,
):
    bring = pltpu.make_async_copy(pot_hbm, pot_ref, sems.at[5])
    bring.start()
    group = GROUP
    rows = group * OWN * W

    def forward(i, carry):
        x = i * group
        zin = orb_ref[pl.ds(pl.multiple_of(x * OWN * W, rows), rows), :]
        along_z = dot(zin, zf_ref[...]).astype(bf16)
        parts = []
        for g in range(group * OWN):
            piece = along_z[W * g : W * g + W]
            parts.append(jnp.concatenate([piece[:, :128], piece[:, 128:]], 0))
        along_y = dot(left_ref[...], jnp.concatenate(parts, 1))
        for g in range(group * OWN):
            xx, tt = x + g // OWN, g % OWN
            at = (tt * W + xx) * PITCH
            mid_ref[pl.ds(at, 2 * G), :] = along_y[:, 128 * g : 128 * g + 128]
        return carry

    lax.fori_loop(0, W // group, forward, 0)

    bring.wait()

    def space(i, carry):
        parts = []
        for k in range(MB * OWN):
            base = (k % OWN) * W * PITCH + i * MB + k // OWN
            parts.append(
                jnp.concatenate(
                    [mid_ref[pl.ds(base + c * G, W, stride=PITCH), :] for c in range(2)], 0
                ).astype(bf16)
            )
        in_space = dot(left_ref[...], jnp.concatenate(parts, 1))
        weighted = []
        for mm in range(MB):
            at = pl.multiple_of((i * MB + mm) * G, G)
            potential = pot_ref[pl.ds(at, G), :]
            potential = jnp.concatenate([potential, potential], 0)
            density = jnp.zeros((2 * G, 128), f32)
            for tt in range(OWN):
                k = mm * OWN + tt
                one = in_space[:, 128 * k : 128 * k + 128]
                density = density + one * one
                weighted.append((one * potential).astype(bf16))
            dens_ref[pl.ds(at, G), :] = (density[:G] + density[G:]) * (1.0 / BLOCK)
        back = dot(left_inv_ref[...], jnp.concatenate(weighted, 1))
        for k in range(MB * OWN):
            base = (k % OWN) * W * PITCH + i * MB + k // OWN
            for c in range(2):
                mid_ref[pl.ds(base + c * G, W, stride=PITCH), :] = back[
                    W * c : W * c + W, 128 * k : 128 * k + 128
                ]
        return carry

    lax.fori_loop(0, G // MB, space, 0, unroll=SU)
    keep = pltpu.make_async_copy(dens_ref, dens_hbm, sems.at[4])
    keep.start()

    lane = iota((W, 128), 1)
    wave_y = iota((W, 128), 0) - W // 2
    wave_z = (lane & (W - 1)) - W // 2
    plane = wave_y * wave_y + wave_z * wave_z

    def kinetic(x):
        wave_x = x - W // 2
        return (kinetic_scale * 0.5) * (plane + wave_x * wave_x).astype(f32)

    num_ref[...] = jnp.zeros_like(num_ref)
    den_ref[...] = jnp.zeros_like(den_ref)

    def backward(i, carry):
        x = i * group
        parts = []
        for g in range(group * OWN):
            xx, tt = x + g // OWN, g % OWN
            at = (tt * W + xx) * PITCH
            parts.append(mid_ref[pl.ds(at, 2 * G), :].astype(bf16))
        back_y = dot(left_inv_ref[...], jnp.concatenate(parts, 1)).astype(bf16)
        parts = []
        for g in range(group * OWN):
            piece = back_y[:, 128 * g : 128 * g + 128]
            parts.append(jnp.concatenate([piece[:W], piece[W:]], 1))
        local = dot(jnp.concatenate(parts, 0), zi_ref[...])
        for g in range(group * OWN):
            xx, tt = x + g // OWN, g % OWN
            at = pl.multiple_of((xx * OWN + tt) * W, W)
            orbital = orb_ref[pl.ds(at, W), :].astype(f32)
            ham = kinetic(xx) * orbital + local[W * g : W * g + W]
            ham_ref[pl.ds(at, W), :] = ham
            num_ref[pl.ds(tt * W, W), :] += orbital * ham
            den_ref[pl.ds(tt * W, W), :] += orbital * orbital
        return carry

    lax.fori_loop(0, W // group, backward, 0)

    lane_row = iota((1, 128), 1)
    low = lane_row < 64
    ritz_row = jnp.zeros((1, 128), f32)
    ritz = []
    for tt in range(OWN):
        halves = []
        num = jnp.sum(num_ref[pl.ds(tt * W, W), :], 0, keepdims=True)
        den = jnp.sum(den_ref[pl.ds(tt * W, W), :], 0, keepdims=True)
        for p in range(2):
            mine = low if p == 0 else jnp.logical_not(low)
            top = jnp.sum(jnp.where(mine, num, 0.0), 1, keepdims=True)
            bottom = jnp.sum(jnp.where(mine, den, 0.0), 1, keepdims=True)
            value = (top / NPW) / (bottom / NPW + epsilon)
            halves.append(value)
            ritz_row = jnp.where(lane_row == 32 + p * OWN + tt, value, ritz_row)
        ritz.append(jnp.where(low, halves[0], halves[1]))
    ritz_ref[...] = jnp.broadcast_to(ritz_row, (8, 128))

    parts = 4
    rows = W * OWN * W // parts

    def send(k):
        at = pl.ds(k * rows, rows)
        return pltpu.make_async_copy(out_ref.at[at], out_hbm.at[at], sems.at[k])

    for x in range(W):
        kin = kinetic(x)
        scale = 1.0 / (1.0 + kin)
        for tt in range(OWN):
            at = pl.ds((x * OWN + tt) * W, W)
            orbital = orb_ref[at, :].astype(f32)
            residual = ham_ref[at, :] - ritz[tt] * orbital
            out_ref[at, :] = (residual * scale).astype(bf16)
        if (x + 1) % (W // parts) == 0:
            send(x // (W // parts)).start()
    for k in range(parts):
        send(k).wait()
    keep.wait()


def searched(orbitals, potential):
    z_fwd, left, left_inv, z_inv = host_tables()
    return pl.pallas_call(
        transform_kernel,
        in_specs=vmem(5) + hbm(1),
        out_specs=hbm(2) + vmem(1),
        out_shape=[
            pltpu.HBM((W * OWN * W, 128), bf16),
            pltpu.HBM((G * G, 128), f32),
            jax.ShapeDtypeStruct((8, 128), f32),
        ],
        scratch_shapes=[
            pltpu.VMEM((G * G, 128), f32),
            pltpu.VMEM((OWN * W * PITCH, 128), f32),
            pltpu.VMEM((W * OWN * W, 128), f32),
            pltpu.VMEM((OWN * W, 128), f32),
            pltpu.VMEM((OWN * W, 128), f32),
            pltpu.VMEM((G * G, 128), f32),
            pltpu.VMEM((W * OWN * W, 128), bf16),
            pltpu.SemaphoreType.DMA((6,)),
        ],
        compiler_params=pltpu.CompilerParams(vmem_limit_bytes=30 << 20),
        name="transform",
    )(orbitals, z_fwd, left, left_inv, z_inv, in_hbm(potential))


def force_kernel(
    depth_ref, dens_ref, pos_ref, species_ref, ritz_ref, out_ref, gy_ref, gyo_ref, wide_ref
):
    strength = strengths(species_ref[...], depth_ref)
    gauss_x, offset_x = gaussian(pos_ref[0:1, :], G)
    gauss_y, offset_y = gaussian(pos_ref[1:2, :], G)
    gauss_z, offset_z = gaussian(pos_ref[2:3, :], 2 * G)
    gy_ref[...] = gauss_y
    gyo_ref[...] = gauss_y * offset_y
    high, low = split_two(jnp.concatenate([gauss_z, gauss_z * offset_z], 1))
    both = jnp.concatenate([high, low], 0)
    per = 4

    def some(i, carry):
        sum_x, sum_y, sum_z = carry
        at = pl.multiple_of(i * per * G, per * G)
        d_high, d_low = split_two(dens_ref[pl.ds(at, per * G), :])
        moments = dot(jnp.concatenate([d_high, d_high], 1), both) + dot(d_low, high)
        for k in range(per):
            gy = gy_ref[pl.ds(i * per + k, 1), :]
            gyo = gyo_ref[pl.ds(i * per + k, 1), :]
            plain = moments[G * k : G * k + G, :256]
            sum_x = sum_x + plain * gy
            sum_y = sum_y + plain * gyo
            sum_z = sum_z + moments[G * k : G * k + G, 256:] * gy
        return sum_x, sum_y, sum_z

    zero = jnp.zeros((G, 256), f32)
    sum_x, sum_y, sum_z = lax.fori_loop(0, G // per, some, (zero, zero, zero))
    factor = -strength / (sigma_cells * sigma_cells)
    force = [
        factor * jnp.sum(gauss_x * offset_x * sum_x, 0, keepdims=True),
        factor * jnp.sum(gauss_x * sum_y, 0, keepdims=True),
        factor * jnp.sum(gauss_x * sum_z, 0, keepdims=True),
    ]
    peer, atom = iota((PEERS, 256), 0), iota((PEERS, 256), 1)
    from_atom, lane = iota((256, 128), 0), iota((256, 128), 1)
    parts = [part.astype(f32) for part in split_three(ritz_ref[0:1, :])]
    totals = [jnp.broadcast_to(part, (PEERS, 128)) for part in parts]
    for alpha in range(3):
        own = jnp.where(atom // 8 == peer, force[alpha], 0.0)
        choose = jnp.where((from_atom & 7) + 8 * alpha == lane, 1.0, 0.0).astype(bf16)
        for k, part in enumerate(split_three(own)):
            totals[k] = totals[k] + dot(part, choose)
    wide_ref[...] = jnp.zeros_like(wide_ref)
    for k in range(3):
        wide_ref[pl.ds(k, PEERS, stride=8), :] = totals[k]
    out_ref[...] = wide_ref[...].reshape(PEERS, 8, 128).astype(bf16)


def force_parts(depth, density, pos, species, ritz):
    return pl.pallas_call(
        force_kernel,
        in_specs=[pl.BlockSpec(memory_space=pltpu.SMEM)] + vmem(4),
        out_specs=vmem(1)[0],
        out_shape=jax.ShapeDtypeStruct((PEERS, 8, 128), bf16),
        scratch_shapes=[
            pltpu.VMEM((G, 256), f32),
            pltpu.VMEM((G, 256), f32),
            pltpu.VMEM((PEERS * 8, 128), f32),
        ],
        compiler_params=pltpu.CompilerParams(vmem_limit_bytes=10 << 20),
        name="force",
    )(depth, density, pos, species, ritz)


def intersect_kernel(
    search_ref, extra_ref, coeff_hbm, out_ref, flat_ref,
    coeff_ref, wide_ref, pair_ref, sems,
):
    bands = BANDS // FETCHES

    def fetch(k):
        at = pl.ds(k * bands, bands)
        return pltpu.make_async_copy(coeff_hbm.at[at], coeff_ref.at[at], sems.at[k])

    for k in range(FETCHES):
        fetch(k).start()
    source, target = iota((256, 512), 0), iota((256, 512), 1)
    part, element = target >> 7, target & 63
    turned = part >> 1
    same = (source & 63) == (element ^ (turned * 32))
    same &= (source >> 7) == ((target >> 6) & 1)
    same &= ((source >> 6) & 1) == (part & 1)
    sign = jnp.where((turned == 1) & (element >= 32), -1.0, 1.0)
    unpack = jnp.where(same, sign, 0.0).astype(bf16)
    for t in range(HALF):
        wide_ref[t * LINE : t * LINE + W, :] = search_ref[t * W : t * W + W, :].astype(f32)
    out_ref[:, 128:, :] = extra_ref[...]
    for j in range(W // 2):
        even = wide_ref[pl.ds(2 * j, HALF, stride=LINE), :]
        odd = wide_ref[pl.ds(2 * j + 1, HALF, stride=LINE), :]
        moved = dot(jnp.concatenate([even, odd], 1).astype(bf16), unpack).astype(bf16)
        at = slice(128 * j, 128 * j + 128)
        for q in range(4):
            piece = moved[:, 128 * q : 128 * q + 128]
            pair_ref[HALF * q : HALF * q + HALF, at] = piece
            if q < 2:
                flat_ref[HALF * q : HALF * q + HALF, at] = piece
    for k in range(FETCHES):
        fetch(k).wait()
        part = dot_nt(pair_ref[...], coeff_ref[bands * k : bands * k + bands, :])
        part = (part * (1.0 / NPW)).astype(bf16)
        for j in range(bands // 128):
            at = 16 * (k * bands // 128 + j)
            out_ref[:, at : at + 16, :] = part[:, 128 * j : 128 * j + 128].reshape(PEERS, 16, 128)


def own_intersections(search, coeff, extra):
    return pl.pallas_call(
        intersect_kernel,
        in_specs=vmem(2) + hbm(1),
        out_specs=vmem(2),
        out_shape=[
            jax.ShapeDtypeStruct((PEERS, ROWS, 128), bf16),
            jax.ShapeDtypeStruct((BLOCK, 2048), bf16),
        ],
        scratch_shapes=[
            pltpu.VMEM((BANDS, 2048), bf16),
            pltpu.VMEM((HALF * LINE, 128), f32),
            pltpu.VMEM((2 * BLOCK, 2048), bf16),
            pltpu.SemaphoreType.DMA((FETCHES,)),
        ],
        compiler_params=pltpu.CompilerParams(vmem_limit_bytes=20 << 20),
        name="intersect",
    )(search, extra, in_hbm(coeff))


def total_kernel(in_ref, out_ref):
    for r in range(8):
        at = slice(16 * r, 16 * r + 16)
        total = in_ref[0, at, :].astype(f32)
        for peer in range(1, PEERS):
            total = total + in_ref[peer, at, :].astype(f32)
        total = total.astype(bf16)
        for peer in range(PEERS):
            out_ref[peer, at, :] = total
    extra = in_ref[0, 128:, :].astype(f32)
    for peer in range(1, PEERS):
        extra = extra + in_ref[peer, 128:, :].astype(f32)
    high, middle, low = split_three(extra[0:1] + extra[1:2] + extra[2:3])
    row = iota((8, 128), 0)
    parts = jnp.where(row == 0, high.astype(f32), 0.0)
    parts = jnp.where(row == 1, middle.astype(f32), parts)
    parts = jnp.where(row == 2, low.astype(f32), parts).astype(bf16)
    for peer in range(PEERS):
        out_ref[peer, 128:, :] = parts


def totals_for_all(arrived):
    return pl.pallas_call(
        total_kernel,
        in_specs=vmem(1),
        out_specs=vmem(1)[0],
        out_shape=jax.ShapeDtypeStruct((PEERS, ROWS, 128), bf16),
        compiler_params=pltpu.CompilerParams(vmem_limit_bytes=6 << 20),
        name="total",
    )(arrived)


def wrap_offset(values):
    return ((values + G // 2) & (G - 1)) - G // 2


def row_of(ref, base, lane_wanted, peer_wanted):
    lane = iota((128, 256), 0)
    choose = jnp.where(lane == lane_wanted, 1.0, 0.0).astype(bf16)
    parts = ref[:, base : base + 8, :].astype(f32).reshape(PEERS * 8, 128).astype(bf16)
    here = jnp.where((iota((PEERS * 8, 256), 0) >> 3) == peer_wanted, dot(parts, choose), 0.0)
    return jnp.sum(here, 0, keepdims=True)


def prepare_kernel(first_ref, order_ref, ritz_ref):
    del order_ref
    column, at = iota((128, 256), 1), iota((PEERS * 8, 256), 1)
    ritz_ref[...] = row_of(
        first_ref, 128, 32 + OWN * (column // HALF) + column % OWN, at % HALF // OWN
    )


def prepared(arrived, order):
    return pl.pallas_call(
        prepare_kernel,
        in_specs=vmem(1) + hbm(1),
        out_specs=vmem(1)[0],
        out_shape=jax.ShapeDtypeStruct((1, 256), f32),
        compiler_params=pltpu.CompilerParams(vmem_limit_bytes=6 << 20),
        name="prepare",
    )(arrived, in_hbm(order))


def project_kernel(
    image_ref, whole_ref, near_ref, pos_ref, before_ref, after_ref, start_ref, end_ref, coeff_hbm,
    flat_hbm, out_hbm, push_ref, along_ref,
    rest_ref, flat_ref, inter_ref, part_ref, done_ref, sems, fetch_sems,
):
    search = pltpu.make_async_copy(flat_hbm, flat_ref, fetch_sems.at[0])
    search.start()
    rest = pltpu.make_async_copy(coeff_hbm.at[:, pl.ds(NEAR, 2048 - NEAR)], rest_ref, fetch_sems.at[1])
    rest.start()
    lanes = 256
    chunks = 2048 // lanes
    for j in range(8):
        inter_ref[:, 128 * j : 128 * j + 128] = whole_ref[:, 16 * j : 16 * j + 16, :].reshape(
            2 * BLOCK, 128
        )
    first = (iota((BLOCK, 128), 1) & 63) < 32

    def send(k):
        at = pl.ds(k * lanes, lanes)
        return pltpu.make_async_copy(done_ref.at[:, at], out_hbm.at[:, at], sems.at[k])

    column, at = iota((128, 256), 1), iota((PEERS * 8, 256), 1)
    pos = pos_ref[...]
    image = image_ref[0]
    before = jnp.where(image == 0, start_ref[...], before_ref[...])
    after = jnp.where(image == image_ref[1] - 1, end_ref[...], after_ref[...])
    ahead = wrap_offset(after - pos).astype(f32)
    behind = wrap_offset(pos - before).astype(f32)
    raw = ahead + behind
    entries = pos.shape[0] * pos.shape[1]

    def mean_square(value):
        return jnp.sum(jnp.sum(value * value, 1, keepdims=True), 0, keepdims=True) / entries

    tangent = raw * lax.rsqrt(mean_square(raw) + epsilon) * (1.0 / math.sqrt(entries))
    length_ahead = jnp.sqrt(entries * (mean_square(ahead) + epsilon))
    length_behind = jnp.sqrt(entries * (mean_square(behind) + epsilon))
    spring = spring_constant * (length_ahead - length_behind) * tangent
    force = jnp.concatenate(
        [row_of(whole_ref, 128, 8 * alpha + (column & 7), at >> 3) for alpha in range(3)], 0
    )
    along = jnp.sum(jnp.sum(force * tangent, 1, keepdims=True), 0, keepdims=True)
    push = force - along * tangent + spring
    for alpha in range(3):
        push_ref[alpha] = push[alpha : alpha + 1]
    along_ref[...] = along

    def part_of(source_ref, start):
        projected = dot(inter_ref[...], source_ref[:, start : start + lanes])
        parts = []
        for j in range(lanes // 128):
            here = slice(128 * j, 128 * j + 128)
            turned = projected[BLOCK:, here]
            turned = jnp.where(first, -pltpu.roll(turned, 96, 1), pltpu.roll(turned, 32, 1))
            parts.append(projected[:BLOCK, here] + turned)
        return jnp.concatenate(parts, 1)

    for k in range(NEAR // lanes):
        here = slice(k * lanes, (k + 1) * lanes)
        part_ref[:, here] = part_of(near_ref, k * lanes)
    search.wait()
    rest.wait()
    for k in range(NEAR // lanes):
        here = slice(k * lanes, (k + 1) * lanes)
        done_ref[:, here] = (flat_ref[:, here].astype(f32) - part_ref[:, here]).astype(bf16)
        send(k).start()
    for k in range(NEAR // lanes, chunks):
        here = slice(k * lanes, (k + 1) * lanes)
        part = part_of(rest_ref, k * lanes - NEAR)
        done_ref[:, here] = (flat_ref[:, here].astype(f32) - part).astype(bf16)
        send(k).start()

    for k in range(chunks):
        send(k).wait()


def corrected(image, whole, near, pos, before, after, start_pos, end_pos, coeff, flat):
    return pl.pallas_call(
        project_kernel,
        in_specs=[pl.BlockSpec(memory_space=pltpu.SMEM)] + vmem(7) + hbm(2),
        out_specs=hbm(1) + vmem(2),
        out_shape=[
            pltpu.HBM((BLOCK, 2048), bf16),
            jax.ShapeDtypeStruct((3, 1, 256), f32),
            jax.ShapeDtypeStruct((1, 1), f32),
        ],
        scratch_shapes=[
            pltpu.VMEM((BANDS, 2048 - NEAR), bf16),
            pltpu.VMEM((BLOCK, 2048), bf16),
            pltpu.VMEM((2 * BLOCK, BANDS), bf16),
            pltpu.VMEM((BLOCK, NEAR), f32),
            pltpu.VMEM((BLOCK, 2048), bf16),
            pltpu.SemaphoreType.DMA((8,)),
            pltpu.SemaphoreType.DMA((2,)),
        ],
        compiler_params=pltpu.CompilerParams(vmem_limit_bytes=16 << 20),
        name="project",
    )(image, whole, near, pos, before, after, start_pos, end_pos, in_hbm(coeff), in_hbm(flat))


def exchanged(array):
    return lax.all_to_all(array, GRID_AXES, split_axis=0, concat_axis=0, tiled=True)


def passed_along(block, axis, distance):
    devices = range(lax.axis_size(axis))
    route = [(i - distance, i) for i in devices if i - distance in devices]
    return lax.ppermute(block, axis, route)


def body(coefficients, rotation, positions, start_pos, end_pos, species, depth):
    coeff = coefficients.reshape(BANDS, 2048)
    pos = positions[0]
    kinds = species.reshape(1, -1)
    orbitals, given = own_orbitals(
        rotation[0], coeff, depth, positions.transpose(1, 0, 2), kinds
    )
    vectors = exchanged(orbitals.reshape(PEERS, OWN * W, 128))
    potential = grid_potential(depth, pos, kinds, given)
    search, density, ritz = searched(vectors.reshape(W * OWN * W, 128), potential)
    own_search = exchanged(search.reshape(PEERS, OWN * W, 128))
    extra = force_parts(depth, density, pos, kinds, ritz)
    parts, flat = own_intersections(own_search.reshape(HALF * W, 128), coeff, extra)
    arrived = exchanged(parts)
    mine = totals_for_all(arrived)
    later = lax.optimization_barrier((pos, mine))[0]
    before = passed_along(later, "img", 1)
    after = passed_along(later, "img", -1)
    whole = exchanged(mine)
    image = jnp.stack([lax.axis_index("img"), lax.axis_size("img")]).astype(jnp.int32)
    ritz_values = prepared(arrived, mine)
    near = brought_near(coeff, mine)
    correction, push, along = corrected(
        image, whole, near, pos, before, after, start_pos, end_pos, coeff, flat
    )
    return (
        correction.reshape(1, BLOCK, 1, 2048),
        ritz_values,
        push.transpose(1, 0, 2),
        along.reshape(1),
    )


def solution(mesh):
    in_specs = (
        P("img", None, GRID_AXES, None),
        P("img", None, None),
        P("img", None, None),
        P(),
        P(),
        P(),
        P(),
    )
    out_specs = (
        P("img", None, GRID_AXES, None),
        P("img", None),
        P("img", None, None),
        P("img"),
    )
    return jax.shard_map(body, mesh=mesh, in_specs=in_specs, out_specs=out_specs, check_vma=False)
```

```python
import math

import jax
import jax.numpy as jnp
import numpy as np
from jax import lax
from jax.experimental import pallas as pl
from jax.experimental.pallas import tpu as pltpu
from jax.sharding import PartitionSpec as P

G = 64
W = 32
BANDS = 1024
BLOCK = 256
SPECIES = 4
NPW = W * W * W
PEERS = 32
OWN = BLOCK // PEERS // 2
HALF = BLOCK // 2
PITCH = 2 * G + 1
GROUP = 32
MB = 16
SU = 1
ROWS = 136
CHUNKS = 2
FETCHES = 2
LINE = W + 1
NEAR = 512
SHARES = 8
EARLY = 6
EARLY_ROWS = G * G * EARLY // SHARES

kinetic_scale = 0.01
sigma_cells = 3.0
spring_constant = 2.0
epsilon = 1e-06

f32 = jnp.float32
bf16 = jnp.bfloat16
GRID_AXES = ("band", "pw")


def host_phases():
    turns = np.mod((np.arange(W) - W // 2)[:, None] * np.arange(G)[None, :], G)
    return turns.astype(np.float32) * np.float32(2.0 * math.pi / G)


def host_tables():
    angle = host_phases()
    cosine, sine = np.cos(angle), np.sin(angle)
    s = np.float32(1.0 / math.sqrt(W))
    fwd = np.stack([np.stack([cosine, sine], 1), np.stack([-sine, cosine], 1)], 0) * s
    t = np.float32(math.sqrt(W) / G)
    c2, s2 = cosine.T * t, sine.T * t
    inv = np.stack([np.stack([c2, -s2], 1), np.stack([s2, c2], 1)], 0)
    left = fwd.transpose(2, 3, 0, 1).reshape(2 * G, 2 * W)
    left_inv = inv.transpose(2, 3, 0, 1).reshape(2 * W, 2 * G)
    eye = np.eye(2, dtype=np.float32)
    z_fwd = np.einsum("cjdn,pq->pcjdqn", fwd, eye).reshape(4 * W, 4 * G)
    z_inv = np.einsum("dncj,pq->dpnqcj", inv, eye).reshape(4 * G, 4 * W)
    return [np.asarray(a, dtype=bf16) for a in (z_fwd, left, left_inv, z_inv)]


def split_two(value):
    high = value.astype(bf16)
    return high, (value - high.astype(f32)).astype(bf16)


def split_three(value):
    high = value.astype(bf16)
    rest = value - high.astype(f32)
    middle = rest.astype(bf16)
    return high, middle, (rest - middle.astype(f32)).astype(bf16)


def dot(a, b):
    return jnp.dot(a, b, preferred_element_type=f32)


def dot_nt(a, b):
    return lax.dot_general(a, b, (((1,), (1,)), ((), ())), preferred_element_type=f32)


def iota(shape, dim):
    return lax.broadcasted_iota(jnp.int32, shape, dim)


def orbitals_kernel(
    rot_hbm, coeff_hbm, depth_hbm, pos_hbm, species_hbm, out_hbm, pot_hbm,
    coeff_ref, rot_ref, turned_ref, wide_ref, out_ref, pot_ref, gy_ref, depth_ref, pos_ref,
    species_ref, sems, small_sems,
):
    lanes = 2048 // CHUNKS

    def fetch(k):
        at = pl.ds(k * lanes, lanes)
        return pltpu.make_async_copy(coeff_hbm.at[:, at], coeff_ref.at[:, at], sems.at[k])

    turned = pltpu.make_async_copy(rot_hbm, rot_ref, sems.at[CHUNKS])
    turned.start()
    for k in range(CHUNKS):
        fetch(k).start()
    ahead = pl.ds(0, EARLY_ROWS)
    keep = pltpu.make_async_copy(pot_ref.at[ahead], pot_hbm.at[ahead], small_sems.at[3])

    @pl.when(potential_first())
    def _():
        small = [
            pltpu.make_async_copy(source, target, small_sems.at[k])
            for k, (source, target) in enumerate(
                [(depth_hbm, depth_ref), (pos_hbm, pos_ref), (species_hbm, species_ref)]
            )
        ]
        for copy in small:
            copy.start()
        for copy in small:
            copy.wait()
        places = [pos_ref[k] for k in range(3)]
        write_potential(depth_ref, places, species_ref[...], pot_ref, gy_ref, 0, EARLY)
        keep.start()

    source, target = iota((256, 256), 0), iota((256, 256), 1)
    same = (source & 63) == (target & 63)
    same &= (source >> 7) == ((target >> 6) & 1)
    same &= ((source >> 6) & 1) == (target >> 7)
    pack = jnp.where(same, 1.0, 0.0).astype(bf16)
    turned.wait()
    turned_ref[...] = rot_ref[...].T
    for k in range(CHUNKS):
        fetch(k).wait()
        both = dot(turned_ref[...], coeff_ref[:, k * lanes : (k + 1) * lanes]).astype(bf16)
        for j in range(lanes // 128):
            at = slice(128 * j, 128 * j + 128)
            pair = jnp.concatenate([both[:HALF, at], both[HALF:, at]], 1)
            moved = dot(pair, pack)
            y = k * (lanes // 64) + 2 * j
            wide_ref[pl.ds(y, HALF, stride=LINE), :] = moved[:, :128]
            wide_ref[pl.ds(y + 1, HALF, stride=LINE), :] = moved[:, 128:]
    parts = 4
    rows = HALF * W // parts

    def send(k):
        at = pl.ds(k * rows, rows)
        return pltpu.make_async_copy(out_ref.at[at], out_hbm.at[at], sems.at[CHUNKS + 1 + k])

    for k in range(parts):
        for t in range(k * HALF // parts, (k + 1) * HALF // parts):
            out_ref[t * W : t * W + W, :] = wide_ref[t * LINE : t * LINE + W, :].astype(bf16)
        send(k).start()
    for k in range(parts):
        send(k).wait()

    @pl.when(potential_first())
    def _():
        keep.wait()


def own_orbitals(rotation, coeff, depth, places, species):
    return pl.pallas_call(
        orbitals_kernel,
        in_specs=hbm(5),
        out_specs=hbm(2),
        out_shape=[pltpu.HBM((HALF * W, 128), bf16), pltpu.HBM((G * G, 128), f32)],
        scratch_shapes=[
            pltpu.VMEM((BANDS, 2048), bf16),
            pltpu.VMEM((BANDS, BLOCK), bf16),
            pltpu.VMEM((BLOCK, BANDS), bf16),
            pltpu.VMEM((HALF * LINE, 128), f32),
            pltpu.VMEM((HALF * W, 128), bf16),
            pltpu.VMEM((G * G, 128), f32),
            pltpu.VMEM((G, 256), f32),
            pltpu.SMEM((SPECIES,), f32),
            pltpu.VMEM((3, 1, 256), jnp.int32),
            pltpu.VMEM((1, 256), jnp.int32),
            pltpu.SemaphoreType.DMA((CHUNKS + 5,)),
            pltpu.SemaphoreType.DMA((4,)),
        ],
        compiler_params=pltpu.CompilerParams(vmem_limit_bytes=20 << 20),
        name="orbitals",
    )(*[in_hbm(array) for array in (rotation, coeff, depth, places, species)])


def in_hbm(array):
    return pltpu.with_memory_space_constraint(array, pltpu.HBM)


def near_kernel(coeff_hbm, order_hbm, out_ref, sem):
    del order_hbm
    fetch = pltpu.make_async_copy(coeff_hbm.at[:, pl.ds(0, NEAR)], out_ref, sem)
    fetch.start()
    fetch.wait()


def brought_near(coeff, order):
    return pl.pallas_call(
        near_kernel,
        in_specs=hbm(2),
        out_specs=vmem(1)[0],
        out_shape=jax.ShapeDtypeStruct((BANDS, NEAR), bf16),
        scratch_shapes=[pltpu.SemaphoreType.DMA],
        compiler_params=pltpu.CompilerParams(vmem_limit_bytes=1 << 20),
        name="near",
    )(in_hbm(coeff), in_hbm(order))


def hbm(count):
    return [pl.BlockSpec(memory_space=pltpu.HBM)] * count


def vmem(count):
    return [pl.BlockSpec(memory_space=pltpu.VMEM)] * count


def gaussian(position, rows):
    cells = iota((rows, position.shape[1]), 0) & (G - 1)
    offset = (((cells - position + G // 2) & (G - 1)) - G // 2).astype(f32)
    return jnp.exp(-offset * offset / (2.0 * sigma_cells * sigma_cells)), offset


def strengths(species, depth_ref):
    strength = jnp.zeros(species.shape, f32)
    for kind in range(SPECIES):
        strength = jnp.where(species == kind, depth_ref[kind], strength)
    return strength


def write_potential(depth_ref, places, species, out_ref, gy_ref, begin, end):
    strength = strengths(species, depth_ref)
    gauss_x, _ = gaussian(places[0], G)
    gauss_x = gauss_x * strength
    gy_ref[...], _ = gaussian(places[1], G)
    gauss_z, _ = gaussian(places[2], 2 * G)
    z_high, z_low = split_two(gauss_z)
    per = G // SHARES

    def some(i, carry):
        for k in range(per):
            m = i * per + k
            value = gauss_x * gy_ref[pl.ds(m, 1), :]
            high, low = split_two(value)
            out_ref[pl.ds(pl.multiple_of(m * G, G), G), :] = (
                dot_nt(high, z_high) + dot_nt(high, z_low) + dot_nt(low, z_high)
            )
        return carry

    lax.fori_loop(begin, end, some, 0)


def potential_first():
    return lax.axis_index("img") % 2 == 0


def potential_kernel(depth_ref, pos_ref, species_ref, given_hbm, out_hbm, pot_ref, gy_ref, sem):
    del given_hbm
    first = potential_first()
    places = [pos_ref[k : k + 1, :] for k in range(3)]
    begin = jnp.where(first, EARLY, 0)
    write_potential(depth_ref, places, species_ref[...], pot_ref, gy_ref, begin, SHARES)
    ahead, late = pl.ds(0, EARLY_ROWS), pl.ds(EARLY_ROWS, G * G - EARLY_ROWS)
    keep_late = pltpu.make_async_copy(pot_ref.at[late], out_hbm.at[late], sem.at[0])
    keep_late.start()

    @pl.when(jnp.logical_not(first))
    def _():
        keep = pltpu.make_async_copy(pot_ref.at[ahead], out_hbm.at[ahead], sem.at[1])
        keep.start()
        keep.wait()

    keep_late.wait()


def grid_potential(depth, pos, species, given):
    return pl.pallas_call(
        potential_kernel,
        in_specs=[pl.BlockSpec(memory_space=pltpu.SMEM)] + vmem(2) + hbm(1),
        out_specs=hbm(1)[0],
        out_shape=pltpu.HBM((G * G, 128), f32),
        input_output_aliases={3: 0},
        scratch_shapes=[
            pltpu.VMEM((G * G, 128), f32),
            pltpu.VMEM((G, 256), f32),
            pltpu.SemaphoreType.DMA((2,)),
        ],
        compiler_params=pltpu.CompilerParams(vmem_limit_bytes=12 << 20),
        name="potential",
    )(depth, pos, species, in_hbm(given))


def transform_kernel(
    orb_ref, zf_ref, left_ref, left_inv_ref, zi_ref, pot_hbm,
    out_hbm, dens_hbm, ritz_ref,
    pot_ref, mid_ref, ham_ref, num_ref, den_ref, dens_ref, out_ref, sems,
):
    bring = pltpu.make_async_copy(pot_hbm, pot_ref, sems.at[5])
    bring.start()
    group = GROUP
    rows = group * OWN * W

    def forward(i, carry):
        x = i * group
        zin = orb_ref[pl.ds(pl.multiple_of(x * OWN * W, rows), rows), :]
        along_z = dot(zin, zf_ref[...]).astype(bf16)
        parts = []
        for g in range(group * OWN):
            piece = along_z[W * g : W * g + W]
            parts.append(jnp.concatenate([piece[:, :128], piece[:, 128:]], 0))
        along_y = dot(left_ref[...], jnp.concatenate(parts, 1))
        for g in range(group * OWN):
            xx, tt = x + g // OWN, g % OWN
            at = (tt * W + xx) * PITCH
            mid_ref[pl.ds(at, 2 * G), :] = along_y[:, 128 * g : 128 * g + 128]
        return carry

    lax.fori_loop(0, W // group, forward, 0)

    bring.wait()

    def space(i, carry):
        parts = []
        for k in range(MB * OWN):
            base = (k % OWN) * W * PITCH + i * MB + k // OWN
            parts.append(
                jnp.concatenate(
                    [mid_ref[pl.ds(base + c * G, W, stride=PITCH), :] for c in range(2)], 0
                ).astype(bf16)
            )
        in_space = dot(left_ref[...], jnp.concatenate(parts, 1))
        weighted = []
        for mm in range(MB):
            at = pl.multiple_of((i * MB + mm) * G, G)
            potential = pot_ref[pl.ds(at, G), :]
            potential = jnp.concatenate([potential, potential], 0)
            density = jnp.zeros((2 * G, 128), f32)
            for tt in range(OWN):
                k = mm * OWN + tt
                one = in_space[:, 128 * k : 128 * k + 128]
                density = density + one * one
                weighted.append((one * potential).astype(bf16))
            dens_ref[pl.ds(at, G), :] = (density[:G] + density[G:]) * (1.0 / BLOCK)
        back = dot(left_inv_ref[...], jnp.concatenate(weighted, 1))
        for k in range(MB * OWN):
            base = (k % OWN) * W * PITCH + i * MB + k // OWN
            for c in range(2):
                mid_ref[pl.ds(base + c * G, W, stride=PITCH), :] = back[
                    W * c : W * c + W, 128 * k : 128 * k + 128
                ]
        return carry

    lax.fori_loop(0, G // MB, space, 0, unroll=SU)
    keep = pltpu.make_async_copy(dens_ref, dens_hbm, sems.at[4])
    keep.start()

    lane = iota((W, 128), 1)
    wave_y = iota((W, 128), 0) - W // 2
    wave_z = (lane & (W - 1)) - W // 2
    plane = wave_y * wave_y + wave_z * wave_z

    def kinetic(x):
        wave_x = x - W // 2
        return (kinetic_scale * 0.5) * (plane + wave_x * wave_x).astype(f32)

    num_ref[...] = jnp.zeros_like(num_ref)
    den_ref[...] = jnp.zeros_like(den_ref)

    def backward(i, carry):
        x = i * group
        parts = []
        for g in range(group * OWN):
            xx, tt = x + g // OWN, g % OWN
            at = (tt * W + xx) * PITCH
            parts.append(mid_ref[pl.ds(at, 2 * G), :].astype(bf16))
        back_y = dot(left_inv_ref[...], jnp.concatenate(parts, 1)).astype(bf16)
        parts = []
        for g in range(group * OWN):
            piece = back_y[:, 128 * g : 128 * g + 128]
            parts.append(jnp.concatenate([piece[:W], piece[W:]], 1))
        local = dot(jnp.concatenate(parts, 0), zi_ref[...])
        for g in range(group * OWN):
            xx, tt = x + g // OWN, g % OWN
            at = pl.multiple_of((xx * OWN + tt) * W, W)
            orbital = orb_ref[pl.ds(at, W), :].astype(f32)
            ham = kinetic(xx) * orbital + local[W * g : W * g + W]
            ham_ref[pl.ds(at, W), :] = ham
            num_ref[pl.ds(tt * W, W), :] += orbital * ham
            den_ref[pl.ds(tt * W, W), :] += orbital * orbital
        return carry

    lax.fori_loop(0, W // group, backward, 0)

    lane_row = iota((1, 128), 1)
    low = lane_row < 64
    ritz_row = jnp.zeros((1, 128), f32)
    ritz = []
    for tt in range(OWN):
        halves = []
        num = jnp.sum(num_ref[pl.ds(tt * W, W), :], 0, keepdims=True)
        den = jnp.sum(den_ref[pl.ds(tt * W, W), :], 0, keepdims=True)
        for p in range(2):
            mine = low if p == 0 else jnp.logical_not(low)
            top = jnp.sum(jnp.where(mine, num, 0.0), 1, keepdims=True)
            bottom = jnp.sum(jnp.where(mine, den, 0.0), 1, keepdims=True)
            value = (top / NPW) / (bottom / NPW + epsilon)
            halves.append(value)
            ritz_row = jnp.where(lane_row == 32 + p * OWN + tt, value, ritz_row)
        ritz.append(jnp.where(low, halves[0], halves[1]))
    ritz_ref[...] = jnp.broadcast_to(ritz_row, (8, 128))

    parts = 4
    rows = W * OWN * W // parts

    def send(k):
        at = pl.ds(k * rows, rows)
        return pltpu.make_async_copy(out_ref.at[at], out_hbm.at[at], sems.at[k])

    for x in range(W):
        kin = kinetic(x)
        scale = 1.0 / (1.0 + kin)
        for tt in range(OWN):
            at = pl.ds((x * OWN + tt) * W, W)
            orbital = orb_ref[at, :].astype(f32)
            residual = ham_ref[at, :] - ritz[tt] * orbital
            out_ref[at, :] = (residual * scale).astype(bf16)
        if (x + 1) % (W // parts) == 0:
            send(x // (W // parts)).start()
    for k in range(parts):
        send(k).wait()
    keep.wait()


def searched(orbitals, potential):
    z_fwd, left, left_inv, z_inv = host_tables()
    return pl.pallas_call(
        transform_kernel,
        in_specs=vmem(5) + hbm(1),
        out_specs=hbm(2) + vmem(1),
        out_shape=[
            pltpu.HBM((W * OWN * W, 128), bf16),
            pltpu.HBM((G * G, 128), f32),
            jax.ShapeDtypeStruct((8, 128), f32),
        ],
        scratch_shapes=[
            pltpu.VMEM((G * G, 128), f32),
            pltpu.VMEM((OWN * W * PITCH, 128), f32),
            pltpu.VMEM((W * OWN * W, 128), f32),
            pltpu.VMEM((OWN * W, 128), f32),
            pltpu.VMEM((OWN * W, 128), f32),
            pltpu.VMEM((G * G, 128), f32),
            pltpu.VMEM((W * OWN * W, 128), bf16),
            pltpu.SemaphoreType.DMA((6,)),
        ],
        compiler_params=pltpu.CompilerParams(vmem_limit_bytes=30 << 20),
        name="transform",
    )(orbitals, z_fwd, left, left_inv, z_inv, in_hbm(potential))


def force_kernel(
    depth_ref, dens_ref, pos_ref, species_ref, ritz_ref, out_ref, gy_ref, gyo_ref, wide_ref
):
    strength = strengths(species_ref[...], depth_ref)
    gauss_x, offset_x = gaussian(pos_ref[0:1, :], G)
    gauss_y, offset_y = gaussian(pos_ref[1:2, :], G)
    gauss_z, offset_z = gaussian(pos_ref[2:3, :], 2 * G)
    gy_ref[...] = gauss_y
    gyo_ref[...] = gauss_y * offset_y
    high, low = split_two(jnp.concatenate([gauss_z, gauss_z * offset_z], 1))
    both = jnp.concatenate([high, low], 0)
    per = 4

    def some(i, carry):
        sum_x, sum_y, sum_z = carry
        at = pl.multiple_of(i * per * G, per * G)
        d_high, d_low = split_two(dens_ref[pl.ds(at, per * G), :])
        moments = dot(jnp.concatenate([d_high, d_high], 1), both) + dot(d_low, high)
        for k in range(per):
            gy = gy_ref[pl.ds(i * per + k, 1), :]
            gyo = gyo_ref[pl.ds(i * per + k, 1), :]
            plain = moments[G * k : G * k + G, :256]
            sum_x = sum_x + plain * gy
            sum_y = sum_y + plain * gyo
            sum_z = sum_z + moments[G * k : G * k + G, 256:] * gy
        return sum_x, sum_y, sum_z

    zero = jnp.zeros((G, 256), f32)
    sum_x, sum_y, sum_z = lax.fori_loop(0, G // per, some, (zero, zero, zero))
    factor = -strength / (sigma_cells * sigma_cells)
    force = [
        factor * jnp.sum(gauss_x * offset_x * sum_x, 0, keepdims=True),
        factor * jnp.sum(gauss_x * sum_y, 0, keepdims=True),
        factor * jnp.sum(gauss_x * sum_z, 0, keepdims=True),
    ]
    peer, atom = iota((PEERS, 256), 0), iota((PEERS, 256), 1)
    from_atom, lane = iota((256, 128), 0), iota((256, 128), 1)
    parts = [part.astype(f32) for part in split_three(ritz_ref[0:1, :])]
    totals = [jnp.broadcast_to(part, (PEERS, 128)) for part in parts]
    for alpha in range(3):
        own = jnp.where(atom // 8 == peer, force[alpha], 0.0)
        choose = jnp.where((from_atom & 7) + 8 * alpha == lane, 1.0, 0.0).astype(bf16)
        for k, part in enumerate(split_three(own)):
            totals[k] = totals[k] + dot(part, choose)
    wide_ref[...] = jnp.zeros_like(wide_ref)
    for k in range(3):
        wide_ref[pl.ds(k, PEERS, stride=8), :] = totals[k]
    out_ref[...] = wide_ref[...].reshape(PEERS, 8, 128).astype(bf16)


def force_parts(depth, density, pos, species, ritz):
    return pl.pallas_call(
        force_kernel,
        in_specs=[pl.BlockSpec(memory_space=pltpu.SMEM)] + vmem(4),
        out_specs=vmem(1)[0],
        out_shape=jax.ShapeDtypeStruct((PEERS, 8, 128), bf16),
        scratch_shapes=[
            pltpu.VMEM((G, 256), f32),
            pltpu.VMEM((G, 256), f32),
            pltpu.VMEM((PEERS * 8, 128), f32),
        ],
        compiler_params=pltpu.CompilerParams(vmem_limit_bytes=10 << 20),
        name="force",
    )(depth, density, pos, species, ritz)


def intersect_kernel(
    search_ref, extra_ref, coeff_hbm, out_ref, flat_ref,
    coeff_ref, wide_ref, pair_ref, sems,
):
    bands = BANDS // FETCHES

    def fetch(k):
        at = pl.ds(k * bands, bands)
        return pltpu.make_async_copy(coeff_hbm.at[at], coeff_ref.at[at], sems.at[k])

    for k in range(FETCHES):
        fetch(k).start()
    source, target = iota((256, 512), 0), iota((256, 512), 1)
    part, element = target >> 7, target & 63
    turned = part >> 1
    same = (source & 63) == (element ^ (turned * 32))
    same &= (source >> 7) == ((target >> 6) & 1)
    same &= ((source >> 6) & 1) == (part & 1)
    sign = jnp.where((turned == 1) & (element >= 32), -1.0, 1.0)
    unpack = jnp.where(same, sign, 0.0).astype(bf16)
    for t in range(HALF):
        wide_ref[t * LINE : t * LINE + W, :] = search_ref[t * W : t * W + W, :].astype(f32)
    out_ref[:, 128:, :] = extra_ref[...]
    for j in range(W // 2):
        even = wide_ref[pl.ds(2 * j, HALF, stride=LINE), :]
        odd = wide_ref[pl.ds(2 * j + 1, HALF, stride=LINE), :]
        moved = dot(jnp.concatenate([even, odd], 1).astype(bf16), unpack).astype(bf16)
        at = slice(128 * j, 128 * j + 128)
        for q in range(4):
            piece = moved[:, 128 * q : 128 * q + 128]
            pair_ref[HALF * q : HALF * q + HALF, at] = piece
            if q < 2:
                flat_ref[HALF * q : HALF * q + HALF, at] = piece
    for k in range(FETCHES):
        fetch(k).wait()
        part = dot_nt(pair_ref[...], coeff_ref[bands * k : bands * k + bands, :])
        part = (part * (1.0 / NPW)).astype(bf16)
        for j in range(bands // 128):
            at = 16 * (k * bands // 128 + j)
            out_ref[:, at : at + 16, :] = part[:, 128 * j : 128 * j + 128].reshape(PEERS, 16, 128)


def own_intersections(search, coeff, extra):
    return pl.pallas_call(
        intersect_kernel,
        in_specs=vmem(2) + hbm(1),
        out_specs=vmem(2),
        out_shape=[
            jax.ShapeDtypeStruct((PEERS, ROWS, 128), bf16),
            jax.ShapeDtypeStruct((BLOCK, 2048), bf16),
        ],
        scratch_shapes=[
            pltpu.VMEM((BANDS, 2048), bf16),
            pltpu.VMEM((HALF * LINE, 128), f32),
            pltpu.VMEM((2 * BLOCK, 2048), bf16),
            pltpu.SemaphoreType.DMA((FETCHES,)),
        ],
        compiler_params=pltpu.CompilerParams(vmem_limit_bytes=20 << 20),
        name="intersect",
    )(search, extra, in_hbm(coeff))


def total_kernel(in_ref, out_ref):
    for r in range(8):
        at = slice(16 * r, 16 * r + 16)
        total = in_ref[0, at, :].astype(f32)
        for peer in range(1, PEERS):
            total = total + in_ref[peer, at, :].astype(f32)
        total = total.astype(bf16)
        for peer in range(PEERS):
            out_ref[peer, at, :] = total
    extra = in_ref[0, 128:, :].astype(f32)
    for peer in range(1, PEERS):
        extra = extra + in_ref[peer, 128:, :].astype(f32)
    high, middle, low = split_three(extra[0:1] + extra[1:2] + extra[2:3])
    row = iota((8, 128), 0)
    parts = jnp.where(row == 0, high.astype(f32), 0.0)
    parts = jnp.where(row == 1, middle.astype(f32), parts)
    parts = jnp.where(row == 2, low.astype(f32), parts).astype(bf16)
    for peer in range(PEERS):
        out_ref[peer, 128:, :] = parts


def totals_for_all(arrived):
    return pl.pallas_call(
        total_kernel,
        in_specs=vmem(1),
        out_specs=vmem(1)[0],
        out_shape=jax.ShapeDtypeStruct((PEERS, ROWS, 128), bf16),
        compiler_params=pltpu.CompilerParams(vmem_limit_bytes=6 << 20),
        name="total",
    )(arrived)


def wrap_offset(values):
    return ((values + G // 2) & (G - 1)) - G // 2


def row_of(ref, base, lane_wanted, peer_wanted):
    lane = iota((128, 256), 0)
    choose = jnp.where(lane == lane_wanted, 1.0, 0.0).astype(bf16)
    parts = ref[:, base : base + 8, :].astype(f32).reshape(PEERS * 8, 128).astype(bf16)
    here = jnp.where((iota((PEERS * 8, 256), 0) >> 3) == peer_wanted, dot(parts, choose), 0.0)
    return jnp.sum(here, 0, keepdims=True)


def prepare_kernel(first_ref, order_ref, ritz_ref):
    del order_ref
    column, at = iota((128, 256), 1), iota((PEERS * 8, 256), 1)
    ritz_ref[...] = row_of(
        first_ref, 128, 32 + OWN * (column // HALF) + column % OWN, at % HALF // OWN
    )


def prepared(arrived, order):
    return pl.pallas_call(
        prepare_kernel,
        in_specs=vmem(1) + hbm(1),
        out_specs=vmem(1)[0],
        out_shape=jax.ShapeDtypeStruct((1, 256), f32),
        compiler_params=pltpu.CompilerParams(vmem_limit_bytes=6 << 20),
        name="prepare",
    )(arrived, in_hbm(order))


def project_kernel(
    image_ref, whole_ref, near_ref, pos_ref, before_ref, after_ref, start_ref, end_ref, coeff_hbm,
    flat_hbm, out_hbm, push_ref, along_ref,
    rest_ref, flat_ref, inter_ref, part_ref, done_ref, sems, fetch_sems,
):
    search = pltpu.make_async_copy(flat_hbm, flat_ref, fetch_sems.at[0])
    search.start()
    rest = pltpu.make_async_copy(coeff_hbm.at[:, pl.ds(NEAR, 2048 - NEAR)], rest_ref, fetch_sems.at[1])
    rest.start()
    lanes = 256
    chunks = 2048 // lanes
    for j in range(8):
        inter_ref[:, 128 * j : 128 * j + 128] = whole_ref[:, 16 * j : 16 * j + 16, :].reshape(
            2 * BLOCK, 128
        )
    first = (iota((BLOCK, 128), 1) & 63) < 32

    def send(k):
        at = pl.ds(k * lanes, lanes)
        return pltpu.make_async_copy(done_ref.at[:, at], out_hbm.at[:, at], sems.at[k])

    column, at = iota((128, 256), 1), iota((PEERS * 8, 256), 1)
    pos = pos_ref[...]
    image = image_ref[0]
    before = jnp.where(image == 0, start_ref[...], before_ref[...])
    after = jnp.where(image == image_ref[1] - 1, end_ref[...], after_ref[...])
    ahead = wrap_offset(after - pos).astype(f32)
    behind = wrap_offset(pos - before).astype(f32)
    raw = ahead + behind
    entries = pos.shape[0] * pos.shape[1]

    def mean_square(value):
        return jnp.sum(jnp.sum(value * value, 1, keepdims=True), 0, keepdims=True) / entries

    tangent = raw * lax.rsqrt(mean_square(raw) + epsilon) * (1.0 / math.sqrt(entries))
    length_ahead = jnp.sqrt(entries * (mean_square(ahead) + epsilon))
    length_behind = jnp.sqrt(entries * (mean_square(behind) + epsilon))
    spring = spring_constant * (length_ahead - length_behind) * tangent
    force = jnp.concatenate(
        [row_of(whole_ref, 128, 8 * alpha + (column & 7), at >> 3) for alpha in range(3)], 0
    )
    along = jnp.sum(jnp.sum(force * tangent, 1, keepdims=True), 0, keepdims=True)
    push = force - along * tangent + spring
    for alpha in range(3):
        push_ref[alpha] = push[alpha : alpha + 1]
    along_ref[...] = along

    def part_of(source_ref, start):
        projected = dot(inter_ref[...], source_ref[:, start : start + lanes])
        parts = []
        for j in range(lanes // 128):
            here = slice(128 * j, 128 * j + 128)
            turned = projected[BLOCK:, here]
            turned = jnp.where(first, -pltpu.roll(turned, 96, 1), pltpu.roll(turned, 32, 1))
            parts.append(projected[:BLOCK, here] + turned)
        return jnp.concatenate(parts, 1)

    for k in range(NEAR // lanes):
        here = slice(k * lanes, (k + 1) * lanes)
        part_ref[:, here] = part_of(near_ref, k * lanes)
    search.wait()
    rest.wait()
    for k in range(NEAR // lanes):
        here = slice(k * lanes, (k + 1) * lanes)
        done_ref[:, here] = (flat_ref[:, here].astype(f32) - part_ref[:, here]).astype(bf16)
        send(k).start()
    for k in range(NEAR // lanes, chunks):
        here = slice(k * lanes, (k + 1) * lanes)
        part = part_of(rest_ref, k * lanes - NEAR)
        done_ref[:, here] = (flat_ref[:, here].astype(f32) - part).astype(bf16)
        send(k).start()

    for k in range(chunks):
        send(k).wait()


def corrected(image, whole, near, pos, before, after, start_pos, end_pos, coeff, flat):
    return pl.pallas_call(
        project_kernel,
        in_specs=[pl.BlockSpec(memory_space=pltpu.SMEM)] + vmem(7) + hbm(2),
        out_specs=hbm(1) + vmem(2),
        out_shape=[
            pltpu.HBM((BLOCK, 2048), bf16),
            jax.ShapeDtypeStruct((3, 1, 256), f32),
            jax.ShapeDtypeStruct((1, 1), f32),
        ],
        scratch_shapes=[
            pltpu.VMEM((BANDS, 2048 - NEAR), bf16),
            pltpu.VMEM((BLOCK, 2048), bf16),
            pltpu.VMEM((2 * BLOCK, BANDS), bf16),
            pltpu.VMEM((BLOCK, NEAR), f32),
            pltpu.VMEM((BLOCK, 2048), bf16),
            pltpu.SemaphoreType.DMA((8,)),
            pltpu.SemaphoreType.DMA((2,)),
        ],
        compiler_params=pltpu.CompilerParams(vmem_limit_bytes=16 << 20),
        name="project",
    )(image, whole, near, pos, before, after, start_pos, end_pos, in_hbm(coeff), in_hbm(flat))


def exchanged(array):
    return lax.all_to_all(array, GRID_AXES, split_axis=0, concat_axis=0, tiled=True)


def passed_along(block, axis, distance):
    devices = range(lax.axis_size(axis))
    route = [(i - distance, i) for i in devices if i - distance in devices]
    return lax.ppermute(block, axis, route)


def body(coefficients, rotation, positions, start_pos, end_pos, species, depth):
    coeff = coefficients.reshape(BANDS, 2048)
    pos = positions[0]
    kinds = species.reshape(1, -1)
    orbitals, given = own_orbitals(
        rotation[0], coeff, depth, positions.transpose(1, 0, 2), kinds
    )
    vectors = exchanged(orbitals.reshape(PEERS, OWN * W, 128))
    potential = grid_potential(depth, pos, kinds, given)
    search, density, ritz = searched(vectors.reshape(W * OWN * W, 128), potential)
    own_search = exchanged(search.reshape(PEERS, OWN * W, 128))
    extra = force_parts(depth, density, pos, kinds, ritz)
    parts, flat = own_intersections(own_search.reshape(HALF * W, 128), coeff, extra)
    arrived = exchanged(parts)
    mine = totals_for_all(arrived)
    later = lax.optimization_barrier((pos, mine))[0]
    before = passed_along(later, "img", 1)
    after = passed_along(later, "img", -1)
    whole = exchanged(mine)
    image = jnp.stack([lax.axis_index("img"), lax.axis_size("img")]).astype(jnp.int32)
    ritz_values = prepared(arrived, mine)
    near = brought_near(coeff, mine)
    correction, push, along = corrected(
        image, whole, near, pos, before, after, start_pos, end_pos, coeff, flat
    )
    return (
        correction.reshape(1, BLOCK, 1, 2048),
        ritz_values,
        push.transpose(1, 0, 2),
        along.reshape(1),
    )


def solution(mesh):
    in_specs = (
        P("img", None, GRID_AXES, None),
        P("img", None, None),
        P("img", None, None),
        P(),
        P(),
        P(),
        P(),
    )
    out_specs = (
        P("img", None, GRID_AXES, None),
        P("img", None),
        P("img", None, None),
        P("img"),
    )
    return jax.shard_map(body, mesh=mesh, in_specs=in_specs, out_specs=out_specs, check_vma=False)
```
